128 devices in a mesh: dp: 8 (over x, core), space: 16 (over y, z).
Axes of the slice: x: 4, y: 4, z: 4, core: 2. Of those that a mesh axis runs over, the one named last changes fastest.
Arguments:
- layer_input: bfloat16 [8, 64, 32, 1024], P('dp', None, 'space'), may hold values from -6 to 6
- hidden_pre: bfloat16 [8, 128, 32, 1024], P('dp', None, 'space'), may hold values from -6 to 6
- output_pre: bfloat16 [8, 256, 16, 256], P('dp', None, 'space'), may hold values from -6 to 6
- output_grad: bfloat16 [8, 256, 16, 256], P('dp', None, 'space'), may hold values from -48 to 48
- weight_a: bfloat16 [27, 64, 128], replicated, may hold values from -0.15625 to 0.15625
- weight_b: bfloat16 [27, 128, 256], replicated, may hold values from -0.109375 to 0.109375
Outputs:
- input_grad: bfloat16 [8, 64, 32, 1024], P('dp', None, 'space')
- weight_grad_a: float32 [27, 64, 128], replicated
- weight_grad_b: float32 [27, 128, 256], replicated
The draws below stay inside these ranges and needn't reach their ends.
All inputs are finite; a program needn't handle non-finite values.
Results may differ from the reference program's by a relative error of at most 0.013.
Values may be sent and summed in bfloat16 or wider, within the bound.
A program may use at most 64 MiB of HBM per device.

```python
import jax
import jax.numpy as jnp
from jax import lax

CA = 64
KA = 128
KB = 256
GRID = 32
SAMPLES = 8
NZA = 32
NZB = 16


def steps_of(rng, dims, split, low, high):
    level, own = 1.0, jax.random.fold_in(rng, 6)
    for dim, shards_of in split:
        heights = jnp.exp(jax.random.uniform(jax.random.fold_in(own, dim), (shards_of,), jnp.float32, low / len(split), high / len(split)))
        level = level * jnp.repeat(heights, dims[dim] // shards_of).reshape([-1 if axis == dim else 1 for axis in range(len(dims))])
    return level


def noise(key, shape, scale, reach, shards=(), held_as=jnp.bfloat16):
    drawn = jax.random.normal(key, shape, jnp.float32) * scale
    if len(shards) > 0:
        drawn = steps_of(key, shape, shards, -0.22, 0.18) * drawn
    return jnp.clip(drawn, min=-reach, max=reach).astype(held_as)


def setup_inputs(seed: int = 0) -> dict:
    seeds = jax.random.split(jax.random.key(seed), 7)
    return {
        "layer_input": noise(seeds[0], (SAMPLES, CA, NZA, GRID * GRID), 1.0, 6.0, ((0, 8), (2, 16))),
        "hidden_pre": noise(seeds[1], (SAMPLES, KA, NZA, GRID * GRID), 1.0, 6.0, ((0, 8), (2, 16))),
        "output_pre": noise(seeds[2], (SAMPLES, KB, NZB, GRID * GRID // 4), 1.0, 6.0, ((0, 8), (2, 16))),
        "output_grad": noise(seeds[3], (SAMPLES, KB, NZB, GRID * GRID // 4), 8.0, 48.0, ((0, 8), (2, 16))),
        "weight_a": noise(seeds[4], (27, CA, KA), (27 * CA) ** -0.5, 0.15625),
        "weight_b": noise(seeds[5], (27, KA, KB), (27 * KA) ** -0.5, 0.109375),
    }


negative_slope = 0.3

def conv_layer(field, kernel):
    shaped = kernel.reshape(3, 3, 3, kernel.shape[1], kernel.shape[2])
    result = lax.conv_general_dilated(field[None], shaped, (1, 1, 1), ((1, 1), (1, 1), (1, 1)), dimension_numbers=('NCDHW', 'DHWIO', 'NCDHW'), precision=lax.Precision.HIGHEST)
    return result[0]

def slopes(values):
    return jnp.where(values > 0, jnp.ones_like(values), negative_slope * jnp.ones_like(values))

def reference(layer_input, hidden_pre, output_pre, output_grad, weight_a, weight_b):
    half = GRID // 2
    kernel_a = weight_a.astype(jnp.float32)
    kernel_b = weight_b.astype(jnp.float32)

    def one_sample(carry, items):
        source, hidden, outer, upstream = items
        outer_f = outer.astype(jnp.float32)
        grad_outer = (upstream.astype(jnp.float32) * slopes(outer_f)).astype(jnp.bfloat16)
        hidden_f = hidden.astype(jnp.float32)
        active = jnp.where(hidden_f > 0, hidden_f, negative_slope * hidden_f)
        pooled = active.reshape(KA, NZB, 2, half, 2, half, 2).mean(axis=(2, 4, 6)).astype(jnp.bfloat16)
        unused_b, pull_b = jax.vjp(conv_layer, pooled.astype(jnp.float32), kernel_b)
        back_b, term_b = pull_b(grad_outer.astype(jnp.float32).reshape(KB, NZB, half, half))
        spread = jnp.repeat(jnp.repeat(jnp.repeat(back_b, 2, 1), 2, 2), 2, 3) * 0.125
        grad_hidden = (spread * slopes(hidden_f.reshape(KA, NZA, GRID, GRID))).astype(jnp.bfloat16)
        field = source.astype(jnp.float32).reshape(CA, NZA, GRID, GRID)
        unused_a, pull_a = jax.vjp(conv_layer, field, kernel_a)
        back_a, term_a = pull_a(grad_hidden.astype(jnp.float32))
        carry = (carry[0] + term_a.reshape(27, CA, KA), carry[1] + term_b.reshape(27, KA, KB))
        return (carry, back_a.astype(jnp.bfloat16).reshape(CA, NZA, GRID * GRID))
    start = (jnp.zeros((27, CA, KA), jnp.float32), jnp.zeros((27, KA, KB), jnp.float32))
    totals, input_grad = lax.scan(one_sample, start, (layer_input, hidden_pre, output_pre, output_grad))
    scale_a = 1.0 / jnp.sqrt(jnp.float32(SAMPLES * NZA * GRID * GRID))
    scale_b = 1.0 / jnp.sqrt(jnp.float32(SAMPLES * NZB * half * half))
    return (input_grad, totals[0] * scale_a, totals[1] * scale_b)
```

```python
import math

import jax
import jax.numpy as jnp
from jax import lax
from jax.sharding import PartitionSpec as P
from jax.experimental import pallas as pl
from jax.experimental.pallas import tpu as pltpu

negative_slope = 0.3


def padded_2(cells, sides, width):
    for axis, dim in sides:
        count = lax.axis_size(axis)
        ends = count - 1
        head = lax.slice_in_dim(cells, 0, width, axis=dim)
        tail = lax.slice_in_dim(cells, cells.shape[dim] - width, cells.shape[dim], axis=dim)
        cells = jnp.concatenate(
            [
                lax.ppermute(tail, axis, [(i, (i + 1) % count) for i in range(ends)]),
                cells,
                lax.ppermute(head, axis, [((i + 1) % count, i) for i in range(ends)]),
            ],
            axis=dim,
        )
    return cells


def slopes(values):
    return jnp.where(values > 0, jnp.ones_like(values), negative_slope * jnp.ones_like(values))


def window(padded, tap_z, tap_y, tap_x, depth, side):
    planes = padded[:, tap_z : tap_z + depth, :]
    margin = side + 1
    wider = jnp.pad(planes, ((0, 0), (0, 0), (margin, margin)))
    offset = (tap_y - 1) * side + (tap_x - 1)
    piece = wider[:, :, margin + offset : margin + offset + side * side]
    column = jnp.arange(side * side, dtype=jnp.int32) % side + (tap_x - 1)
    inside = (column >= 0) & (column < side)
    piece = jnp.where(inside, piece, jnp.zeros_like(piece))
    return piece.reshape(padded.shape[0], depth * side * side)


def outer_product(left, right):
    return lax.dot_general(
        left, right, (((1,), (1,)), ((), ())), preferred_element_type=jnp.float32
    )


def _all_reduce_kernel(x_ref, o_ref, full, recv_a, acc_a, recv_b, acc_b, recv_c, acc_c, recv_d, sends, recvs):
    rows = x_ref.shape[0]
    half, eighth, piece = rows // 2, rows // 8, rows // 32
    mesh_id = pl.DeviceIdType.MESH
    dp = lax.axis_index("dp")
    sp = lax.axis_index("space")
    core, xi, yi, zi = dp % 2, dp // 2, sp // 4, sp % 4
    partner = (xi * 2 + (1 - core), sp)

    def x_peer(k):
        return (((xi + k) % 4) * 2 + core, sp)

    def y_peer(k):
        return (dp, ((yi + k) % 4) * 4 + zi)

    def z_peer(k):
        return (dp, yi * 4 + (zi + k) % 4)

    peers = [partner] + [f(k) for f in (x_peer, y_peer, z_peer) for k in (1, 2, 3)]
    barrier = pltpu.get_barrier_semaphore()
    for peer in peers:
        pl.semaphore_signal(barrier, inc=1, device_id=peer, device_id_type=mesh_id)
    pl.semaphore_wait(barrier, len(peers))

    def rows_at(start, size):
        return pl.ds(pl.multiple_of(start, 8), size)

    def exchange(pairs, first):
        copies = []
        for n, (src, dst, peer) in enumerate(pairs):
            copy = pltpu.make_async_remote_copy(
                src_ref=src,
                dst_ref=dst,
                send_sem=sends.at[first + n],
                recv_sem=recvs.at[first + n],
                device_id=peer,
                device_id_type=mesh_id,
            )
            copy.start()
            copies.append(copy)
        for copy in copies:
            copy.wait()

    exchange([(x_ref.at[rows_at((1 - core) * half, half)], recv_a, partner)], 0)
    acc_a[...] = x_ref[rows_at(core * half, half), :] + recv_a[...]
    exchange(
        [(acc_a.at[rows_at(((xi + k) % 4) * eighth, eighth)], recv_b.at[k - 1], x_peer(k)) for k in (1, 2, 3)], 1
    )
    acc_b[...] = acc_a[rows_at(xi * eighth, eighth), :] + recv_b[0] + recv_b[1] + recv_b[2]
    exchange(
        [(acc_b.at[rows_at(((yi + k) % 4) * piece, piece)], recv_c.at[k - 1], y_peer(k)) for k in (1, 2, 3)], 4
    )
    acc_c[...] = acc_b[rows_at(yi * piece, piece), :] + recv_c[0] + recv_c[1] + recv_c[2]
    recv_d[0] = acc_c[...]
    exchange([(acc_c, recv_d.at[k], z_peer(k)) for k in (1, 2, 3)], 7)
    total = recv_d[zi % 4]
    for j in (1, 2, 3):
        total = total + recv_d[(zi - j + 4) % 4]
    own = core * half + xi * eighth + yi * piece
    full[rows_at(own, piece), :] = total
    block = full.at[rows_at(own, piece)]
    exchange([(block, block, y_peer(k)) for k in (1, 2, 3)], 10)
    block = full.at[rows_at(core * half + xi * eighth, eighth)]
    exchange([(block, block, x_peer(k)) for k in (1, 2, 3)], 13)
    block = full.at[rows_at(core * half, half)]
    exchange([(block, block, partner)], 16)
    o_ref[...] = full[...]


def all_reduce(parts):
    flat = jnp.concatenate([p.reshape(-1) for p in parts])
    count = flat.shape[0]
    unit = 128 * 256
    rows = -(-count // unit) * 256
    flat = jnp.pad(flat, (0, rows * 128 - count)).reshape(rows, 128)
    half, eighth, piece = rows // 2, rows // 8, rows // 32
    f32 = jnp.float32
    summed = pl.pallas_call(
        _all_reduce_kernel,
        out_shape=jax.ShapeDtypeStruct((rows, 128), f32),
        in_specs=[pl.BlockSpec(memory_space=pltpu.VMEM)],
        out_specs=pl.BlockSpec(memory_space=pltpu.VMEM),
        scratch_shapes=[
            pltpu.VMEM((rows, 128), f32),
            pltpu.VMEM((half, 128), f32),
            pltpu.VMEM((half, 128), f32),
            pltpu.VMEM((3, eighth, 128), f32),
            pltpu.VMEM((eighth, 128), f32),
            pltpu.VMEM((3, piece, 128), f32),
            pltpu.VMEM((piece, 128), f32),
            pltpu.VMEM((4, piece, 128), f32),
            pltpu.SemaphoreType.DMA((17,)),
            pltpu.SemaphoreType.DMA((17,)),
        ],
        compiler_params=pltpu.CompilerParams(collective_id=0, has_side_effects=True),
    )(flat)
    summed = summed.reshape(-1)
    out, start = [], 0
    for p in parts:
        out.append(summed[start : start + p.size].reshape(p.shape))
        start += p.size
    return out


def per_device(layer_input, hidden_pre, output_pre, output_grad, weight_a, weight_b):
    side = math.isqrt(layer_input.shape[3])
    half = side // 2
    depth_a = layer_input.shape[2]
    depth_b = depth_a // 2
    source = layer_input[0]
    hidden = hidden_pre[0]
    outer = output_pre[0]
    upstream = output_grad[0]
    chan_in = source.shape[0]
    width_a = hidden.shape[0]
    width_b = outer.shape[0]
    grad_outer = (upstream.astype(jnp.float32) * slopes(outer.astype(jnp.float32))).astype(
        jnp.bfloat16
    )
    hidden_f = hidden.astype(jnp.float32)
    active = jnp.where(hidden_f > 0, hidden_f, negative_slope * hidden_f)
    pooled = (
        active.reshape(width_a, depth_b, 2, half, 2, half, 2)
        .mean(axis=(2, 4, 6))
        .astype(jnp.bfloat16)
    )
    pooled = pooled.reshape(width_a, depth_b, half * half)
    outer_pad = padded_2(grad_outer, (("space", 1),), 1)
    pooled_pad = padded_2(pooled, (("space", 1),), 1)
    grad_flat = grad_outer.reshape(width_b, depth_b * half * half)
    back_b = jnp.zeros((width_a, depth_b * half * half), jnp.float32)
    terms_b = []
    for tap in range(27):
        tap_z, tap_y, tap_x = (tap // 9, tap // 3 % 3, tap % 3)
        mirror = window(outer_pad, 2 - tap_z, 2 - tap_y, 2 - tap_x, depth_b, half)
        back_b = back_b + jnp.dot(weight_b[tap], mirror, preferred_element_type=jnp.float32)
        terms_b.append(
            outer_product(window(pooled_pad, tap_z, tap_y, tap_x, depth_b, half), grad_flat)
        )
    sums_b = jnp.stack(terms_b)
    coarse = back_b.reshape(width_a, depth_b, half, half)
    upward = jnp.repeat(jnp.repeat(jnp.repeat(coarse, 2, 1), 2, 2), 2, 3) * 0.125
    upward = upward.reshape(width_a, depth_a * side * side)
    grad_hidden = (upward * slopes(hidden_f.reshape(width_a, depth_a * side * side))).astype(
        jnp.bfloat16
    )
    grad_hidden = grad_hidden.reshape(width_a, depth_a, side * side)
    hidden_pad = padded_2(grad_hidden, (("space", 1),), 1)
    source_pad = padded_2(source, (("space", 1),), 1)
    hidden_flat = grad_hidden.reshape(width_a, depth_a * side * side)
    back_a = jnp.zeros((chan_in, depth_a * side * side), jnp.float32)
    terms_a = []
    for tap in range(27):
        tap_z, tap_y, tap_x = (tap // 9, tap // 3 % 3, tap % 3)
        mirror = window(hidden_pad, 2 - tap_z, 2 - tap_y, 2 - tap_x, depth_a, side)
        back_a = back_a + jnp.dot(weight_a[tap], mirror, preferred_element_type=jnp.float32)
        terms_a.append(
            outer_product(window(source_pad, tap_z, tap_y, tap_x, depth_a, side), hidden_flat)
        )
    sums_a = jnp.stack(terms_a)
    input_grad = back_a.astype(jnp.bfloat16).reshape(1, chan_in, depth_a, side * side)
    total_a, total_b = all_reduce((sums_a, sums_b))
    samples = lax.axis_size("dp")
    planes_a = depth_a * lax.axis_size("space")
    scale_a = 1.0 / math.sqrt(samples * planes_a * side * side)
    scale_b = 1.0 / math.sqrt(samples * (planes_a // 2) * half * half)
    return (input_grad, total_a * scale_a, total_b * scale_b)


def solution(mesh):
    in_specs = (
        P("dp", None, "space", None),
        P("dp", None, "space", None),
        P("dp", None, "space", None),
        P("dp", None, "space", None),
        P(),
        P(),
    )
    out_specs = (P("dp", None, "space", None), P(), P())
    return jax.shard_map(
        per_device, mesh=mesh, in_specs=in_specs, out_specs=out_specs, check_vma=False
    )
```

```python
import math

import jax
import jax.numpy as jnp
from jax import lax
from jax.sharding import PartitionSpec as P
from jax.experimental import pallas as pl
from jax.experimental.pallas import tpu as pltpu

negative_slope = 0.3


def padded_2(cells, sides, width):
    for axis, dim in sides:
        count = lax.axis_size(axis)
        ends = count - 1
        head = lax.slice_in_dim(cells, 0, width, axis=dim)
        tail = lax.slice_in_dim(cells, cells.shape[dim] - width, cells.shape[dim], axis=dim)
        cells = jnp.concatenate(
            [
                lax.ppermute(tail, axis, [(i, (i + 1) % count) for i in range(ends)]),
                cells,
                lax.ppermute(head, axis, [((i + 1) % count, i) for i in range(ends)]),
            ],
            axis=dim,
        )
    return cells


def slopes(values):
    return jnp.where(values > 0, jnp.ones_like(values), negative_slope * jnp.ones_like(values))


def window(padded, tap_z, tap_y, tap_x, depth, side):
    planes = padded[:, tap_z : tap_z + depth, :]
    margin = side + 1
    wider = jnp.pad(planes, ((0, 0), (0, 0), (margin, margin)))
    offset = (tap_y - 1) * side + (tap_x - 1)
    piece = wider[:, :, margin + offset : margin + offset + side * side]
    column = jnp.arange(side * side, dtype=jnp.int32) % side + (tap_x - 1)
    inside = (column >= 0) & (column < side)
    piece = jnp.where(inside, piece, jnp.zeros_like(piece))
    return piece.reshape(padded.shape[0], depth * side * side)


def outer_product(left, right):
    return lax.dot_general(
        left, right, (((1,), (1,)), ((), ())), preferred_element_type=jnp.float32
    )


def _all_reduce_kernel(x_ref, o_ref, full, recv_a, acc_a, recv_1, acc_1, recv_2, acc_2, recv_3, sends, recvs):
    rows = x_ref.shape[0]
    half = rows // 2
    part = half // 3
    quarter, piece = part // 4, part // 16
    mesh_id = pl.DeviceIdType.MESH
    dp = lax.axis_index("dp")
    sp = lax.axis_index("space")
    core = dp % 2
    spot = {"x": dp // 2, "y": sp // 4, "z": sp % 4}
    partner = (spot["x"] * 2 + (1 - core), sp)

    def peer(axis, k):
        moved = dict(spot)
        moved[axis] = (spot[axis] + k) % 4
        return (moved["x"] * 2 + core, moved["y"] * 4 + moved["z"])

    orders = (("x", "y", "z"), ("y", "z", "x"), ("z", "x", "y"))
    peers = [partner] + [peer(axis, k) for axis in "xyz" for k in (1, 2, 3)]
    barrier = pltpu.get_barrier_semaphore()
    for other in peers:
        pl.semaphore_signal(barrier, inc=1, device_id=other, device_id_type=mesh_id)
    pl.semaphore_wait(barrier, len(peers))

    def rows_at(start, size):
        return pl.ds(pl.multiple_of(start, 8), size)

    used = [0]

    def exchange(triples):
        copies = []
        for src, dst, other in triples:
            copy = pltpu.make_async_remote_copy(
                src_ref=src,
                dst_ref=dst,
                send_sem=sends.at[used[0]],
                recv_sem=recvs.at[used[0]],
                device_id=other,
                device_id_type=mesh_id,
            )
            used[0] += 1
            copy.start()
            copies.append(copy)
        for copy in copies:
            copy.wait()

    exchange([(x_ref.at[rows_at((1 - core) * half, half)], recv_a, partner)])
    acc_a[...] = x_ref[rows_at(core * half, half), :] + recv_a[...]
    triples = []
    for p, order in enumerate(orders):
        for k in (1, 2, 3):
            block = p * part + ((spot[order[0]] + k) % 4) * quarter
            triples.append((acc_a.at[rows_at(block, quarter)], recv_1.at[p, k - 1], peer(order[0], k)))
    exchange(triples)
    for p, order in enumerate(orders):
        mine = p * part + spot[order[0]] * quarter
        acc_1[p] = acc_a[rows_at(mine, quarter), :] + recv_1[p, 0] + recv_1[p, 1] + recv_1[p, 2]
    triples = []
    for p, order in enumerate(orders):
        for k in (1, 2, 3):
            block = ((spot[order[1]] + k) % 4) * piece
            triples.append((acc_1.at[p, rows_at(block, piece)], recv_2.at[p, k - 1], peer(order[1], k)))
    exchange(triples)
    for p, order in enumerate(orders):
        mine = spot[order[1]] * piece
        recv_3[p, 0] = acc_1[p, rows_at(mine, piece), :] + recv_2[p, 0] + recv_2[p, 1] + recv_2[p, 2]
    exchange([(recv_3.at[p, 0], recv_3.at[p, k], peer(order[2], k)) for p, order in enumerate(orders) for k in (1, 2, 3)])
    spans = []
    for p, order in enumerate(orders):
        last = spot[order[2]]
        total = recv_3[p, last % 4]
        for j in (1, 2, 3):
            total = total + recv_3[p, (last - j + 4) % 4]
        outer = core * half + p * part + spot[order[0]] * quarter
        own = outer + spot[order[1]] * piece
        full[rows_at(own, piece), :] = total
        spans.append((outer, own, order))
    exchange([(full.at[rows_at(own, piece)], full.at[rows_at(own, piece)], peer(order[1], k)) for outer, own, order in spans for k in (1, 2, 3)])
    exchange([(full.at[rows_at(outer, quarter)], full.at[rows_at(outer, quarter)], peer(order[0], k)) for outer, own, order in spans for k in (1, 2, 3)])
    block = full.at[rows_at(core * half, half)]
    exchange([(block, block, partner)])
    o_ref[...] = full[...]


def all_reduce(parts):
    flat = jnp.concatenate([p.reshape(-1) for p in parts])
    count = flat.shape[0]
    unit = 128 * 6 * 16 * 8
    rows = -(-count // unit) * 6 * 16 * 8
    flat = jnp.pad(flat, (0, rows * 128 - count)).reshape(rows, 128)
    half = rows // 2
    part = half // 3
    quarter, piece = part // 4, part // 16
    f32 = jnp.float32
    summed = pl.pallas_call(
        _all_reduce_kernel,
        out_shape=jax.ShapeDtypeStruct((rows, 128), f32),
        in_specs=[pl.BlockSpec(memory_space=pltpu.VMEM)],
        out_specs=pl.BlockSpec(memory_space=pltpu.VMEM),
        scratch_shapes=[
            pltpu.VMEM((rows, 128), f32),
            pltpu.VMEM((half, 128), f32),
            pltpu.VMEM((half, 128), f32),
            pltpu.VMEM((3, 3, quarter, 128), f32),
            pltpu.VMEM((3, quarter, 128), f32),
            pltpu.VMEM((3, 3, piece, 128), f32),
            pltpu.VMEM((3, piece, 128), f32),
            pltpu.VMEM((3, 4, piece, 128), f32),
            pltpu.SemaphoreType.DMA((47,)),
            pltpu.SemaphoreType.DMA((47,)),
        ],
        compiler_params=pltpu.CompilerParams(collective_id=0, has_side_effects=True),
    )(flat)
    summed = summed.reshape(-1)
    out, start = [], 0
    for p in parts:
        out.append(summed[start : start + p.size].reshape(p.shape))
        start += p.size
    return out


def per_device(layer_input, hidden_pre, output_pre, output_grad, weight_a, weight_b):
    side = math.isqrt(layer_input.shape[3])
    half = side // 2
    depth_a = layer_input.shape[2]
    depth_b = depth_a // 2
    source = layer_input[0]
    hidden = hidden_pre[0]
    outer = output_pre[0]
    upstream = output_grad[0]
    chan_in = source.shape[0]
    width_a = hidden.shape[0]
    width_b = outer.shape[0]
    grad_outer = (upstream.astype(jnp.float32) * slopes(outer.astype(jnp.float32))).astype(
        jnp.bfloat16
    )
    hidden_f = hidden.astype(jnp.float32)
    active = jnp.where(hidden_f > 0, hidden_f, negative_slope * hidden_f)
    pooled = (
        active.reshape(width_a, depth_b, 2, half, 2, half, 2)
        .mean(axis=(2, 4, 6))
        .astype(jnp.bfloat16)
    )
    pooled = pooled.reshape(width_a, depth_b, half * half)
    outer_pad = padded_2(grad_outer, (("space", 1),), 1)
    pooled_pad = padded_2(pooled, (("space", 1),), 1)
    grad_flat = grad_outer.reshape(width_b, depth_b * half * half)
    back_b = jnp.zeros((width_a, depth_b * half * half), jnp.float32)
    terms_b = []
    for tap in range(27):
        tap_z, tap_y, tap_x = (tap // 9, tap // 3 % 3, tap % 3)
        mirror = window(outer_pad, 2 - tap_z, 2 - tap_y, 2 - tap_x, depth_b, half)
        back_b = back_b + jnp.dot(weight_b[tap], mirror, preferred_element_type=jnp.float32)
        terms_b.append(
            outer_product(window(pooled_pad, tap_z, tap_y, tap_x, depth_b, half), grad_flat)
        )
    sums_b = jnp.stack(terms_b)
    coarse = back_b.reshape(width_a, depth_b, half, half)
    upward = jnp.repeat(jnp.repeat(jnp.repeat(coarse, 2, 1), 2, 2), 2, 3) * 0.125
    upward = upward.reshape(width_a, depth_a * side * side)
    grad_hidden = (upward * slopes(hidden_f.reshape(width_a, depth_a * side * side))).astype(
        jnp.bfloat16
    )
    grad_hidden = grad_hidden.reshape(width_a, depth_a, side * side)
    hidden_pad = padded_2(grad_hidden, (("space", 1),), 1)
    source_pad = padded_2(source, (("space", 1),), 1)
    hidden_flat = grad_hidden.reshape(width_a, depth_a * side * side)
    back_a = jnp.zeros((chan_in, depth_a * side * side), jnp.float32)
    terms_a = []
    for tap in range(27):
        tap_z, tap_y, tap_x = (tap // 9, tap // 3 % 3, tap % 3)
        mirror = window(hidden_pad, 2 - tap_z, 2 - tap_y, 2 - tap_x, depth_a, side)
        back_a = back_a + jnp.dot(weight_a[tap], mirror, preferred_element_type=jnp.float32)
        terms_a.append(
            outer_product(window(source_pad, tap_z, tap_y, tap_x, depth_a, side), hidden_flat)
        )
    sums_a = jnp.stack(terms_a)
    input_grad = back_a.astype(jnp.bfloat16).reshape(1, chan_in, depth_a, side * side)
    total_a, total_b = all_reduce((sums_a, sums_b))
    samples = lax.axis_size("dp")
    planes_a = depth_a * lax.axis_size("space")
    scale_a = 1.0 / math.sqrt(samples * planes_a * side * side)
    scale_b = 1.0 / math.sqrt(samples * (planes_a // 2) * half * half)
    return (input_grad, total_a * scale_a, total_b * scale_b)


def solution(mesh):
    in_specs = (
        P("dp", None, "space", None),
        P("dp", None, "space", None),
        P("dp", None, "space", None),
        P("dp", None, "space", None),
        P(),
        P(),
    )
    out_specs = (P("dp", None, "space", None), P(), P())
    return jax.shard_map(
        per_device, mesh=mesh, in_specs=in_specs, out_specs=out_specs, check_vma=False
    )
```

```python
import math

import jax
import jax.numpy as jnp
from jax import lax
from jax.sharding import PartitionSpec as P
from jax.experimental import pallas as pl
from jax.experimental.pallas import tpu as pltpu

negative_slope = 0.3


def padded_2(cells, sides, width):
    for axis, dim in sides:
        count = lax.axis_size(axis)
        ends = count - 1
        head = lax.slice_in_dim(cells, 0, width, axis=dim)
        tail = lax.slice_in_dim(cells, cells.shape[dim] - width, cells.shape[dim], axis=dim)
        cells = jnp.concatenate(
            [
                lax.ppermute(tail, axis, [(i, (i + 1) % count) for i in range(ends)]),
                cells,
                lax.ppermute(head, axis, [((i + 1) % count, i) for i in range(ends)]),
            ],
            axis=dim,
        )
    return cells


def slopes(values):
    return jnp.where(values > 0, jnp.ones_like(values), negative_slope * jnp.ones_like(values))


def window(padded, tap_z, tap_y, tap_x, depth, side):
    planes = padded[:, tap_z : tap_z + depth, :]
    margin = side + 1
    wider = jnp.pad(planes, ((0, 0), (0, 0), (margin, margin)))
    offset = (tap_y - 1) * side + (tap_x - 1)
    piece = wider[:, :, margin + offset : margin + offset + side * side]
    column = jnp.arange(side * side, dtype=jnp.int32) % side + (tap_x - 1)
    inside = (column >= 0) & (column < side)
    piece = jnp.where(inside, piece, jnp.zeros_like(piece))
    return piece.reshape(padded.shape[0], depth * side * side)


def outer_product(left, right):
    return lax.dot_general(
        left, right, (((1,), (1,)), ((), ())), preferred_element_type=jnp.float32
    )


def _all_reduce_kernel(x_ref, o_ref, full, recv_a, acc_a, recv_1, acc_1, recv_2, acc_2, recv_3, sends, recvs):
    rows = x_ref.shape[0]
    half = rows // 2
    part = half // 3
    quarter, piece = part // 4, part // 16
    mesh_id = pl.DeviceIdType.MESH
    dp = lax.axis_index("dp")
    sp = lax.axis_index("space")
    core = dp % 2
    spot = {"x": dp // 2, "y": sp // 4, "z": sp % 4}
    partner = (spot["x"] * 2 + (1 - core), sp)

    def peer(axis, k):
        moved = dict(spot)
        moved[axis] = (spot[axis] + k) % 4
        return (moved["x"] * 2 + core, moved["y"] * 4 + moved["z"])

    orders = (("x", "y", "z"), ("y", "z", "x"), ("z", "x", "y"))
    peers = [partner] + [peer(axis, k) for axis in "xyz" for k in (1, 2, 3)]
    barrier = pltpu.get_barrier_semaphore()
    for other in peers:
        pl.semaphore_signal(barrier, inc=1, device_id=other, device_id_type=mesh_id)
    pl.semaphore_wait(barrier, len(peers))

    def rows_at(start, size):
        return pl.ds(pl.multiple_of(start, 8), size)

    used = [0]

    def exchange(triples):
        copies = []
        for src, dst, other in triples:
            copy = pltpu.make_async_remote_copy(
                src_ref=src,
                dst_ref=dst,
                send_sem=sends.at[used[0]],
                recv_sem=recvs.at[used[0]],
                device_id=other,
                device_id_type=mesh_id,
            )
            used[0] += 1
            copy.start()
            copies.append(copy)
        for copy in copies:
            copy.wait()

    exchange([(x_ref.at[rows_at((1 - core) * half, half)], recv_a, partner)])
    acc_a[...] = x_ref[rows_at(core * half, half), :] + recv_a[...]
    triples = []
    for p, order in enumerate(orders):
        for k in (1, 2, 3):
            block = p * part + ((spot[order[0]] + k) % 4) * quarter
            triples.append((acc_a.at[rows_at(block, quarter)], recv_1.at[p, k - 1], peer(order[0], k)))
    exchange(triples)
    for p, order in enumerate(orders):
        mine = p * part + spot[order[0]] * quarter
        acc_1[p] = acc_a[rows_at(mine, quarter), :] + recv_1[p, 0] + recv_1[p, 1] + recv_1[p, 2]
    triples = []
    for p, order in enumerate(orders):
        for k in (1, 2, 3):
            block = ((spot[order[1]] + k) % 4) * piece
            triples.append((acc_1.at[p, rows_at(block, piece)], recv_2.at[p, k - 1], peer(order[1], k)))
    exchange(triples)
    for p, order in enumerate(orders):
        mine = spot[order[1]] * piece
        recv_3[p, 0] = acc_1[p, rows_at(mine, piece), :] + recv_2[p, 0] + recv_2[p, 1] + recv_2[p, 2]
    exchange([(recv_3.at[p, 0], recv_3.at[p, k], peer(order[2], k)) for p, order in enumerate(orders) for k in (1, 2, 3)])
    spans = []
    for p, order in enumerate(orders):
        last = spot[order[2]]
        total = recv_3[p, last % 4]
        for j in (1, 2, 3):
            total = total + recv_3[p, (last - j + 4) % 4]
        outer = core * half + p * part + spot[order[0]] * quarter
        own = outer + spot[order[1]] * piece
        full[rows_at(own, piece), :] = total
        spans.append((outer, own, order))
    exchange([(full.at[rows_at(own, piece)], full.at[rows_at(own, piece)], peer(order[1], k)) for outer, own, order in spans for k in (1, 2, 3)])
    exchange([(full.at[rows_at(outer, quarter)], full.at[rows_at(outer, quarter)], peer(order[0], k)) for outer, own, order in spans for k in (1, 2, 3)])
    block = full.at[rows_at(core * half, half)]
    exchange([(block, block, partner)])
    o_ref[...] = full[...]


def all_reduce(parts):
    flat = jnp.concatenate([p.reshape(-1) for p in parts])
    count = flat.shape[0]
    unit = 128 * 6 * 16 * 8
    rows = -(-count // unit) * 6 * 16 * 8
    flat = jnp.pad(flat, (0, rows * 128 - count)).reshape(rows, 128)
    half = rows // 2
    part = half // 3
    quarter, piece = part // 4, part // 16
    f32 = jnp.float32
    summed = pl.pallas_call(
        _all_reduce_kernel,
        out_shape=jax.ShapeDtypeStruct((rows, 128), f32),
        in_specs=[pl.BlockSpec(memory_space=pltpu.VMEM)],
        out_specs=pl.BlockSpec(memory_space=pltpu.VMEM),
        scratch_shapes=[
            pltpu.VMEM((rows, 128), f32),
            pltpu.VMEM((half, 128), f32),
            pltpu.VMEM((half, 128), f32),
            pltpu.VMEM((3, 3, quarter, 128), f32),
            pltpu.VMEM((3, quarter, 128), f32),
            pltpu.VMEM((3, 3, piece, 128), f32),
            pltpu.VMEM((3, piece, 128), f32),
            pltpu.VMEM((3, 4, piece, 128), f32),
            pltpu.SemaphoreType.DMA((47,)),
            pltpu.SemaphoreType.DMA((47,)),
        ],
        compiler_params=pltpu.CompilerParams(collective_id=0, has_side_effects=True),
    )(flat)
    summed = summed.reshape(-1)
    out, start = [], 0
    for p in parts:
        out.append(summed[start : start + p.size].reshape(p.shape))
        start += p.size
    return out


def conv_cells(field, kernel):
    shaped = kernel.reshape(3, 3, 3, kernel.shape[1], kernel.shape[2])
    result = lax.conv_general_dilated(
        field[None],
        shaped,
        (1, 1, 1),
        ((0, 0), (1, 1), (1, 1)),
        dimension_numbers=("NCDHW", "DHWIO", "NCDHW"),
        preferred_element_type=jnp.float32,
    )
    return result[0]


def back_cells(padded, kernel):
    flipped = kernel[::-1].transpose(0, 2, 1)
    return conv_cells(padded, flipped)


def kernel_terms(padded, upstream):
    taps, chan_in, chan_out = 27, padded.shape[0], upstream.shape[0]
    start = jnp.zeros((taps, chan_in, chan_out), jnp.float32)
    field = padded.astype(jnp.float32)
    unused, pull = jax.vjp(lambda w: conv_cells(field, w), start)
    return pull(upstream.astype(jnp.float32))[0]


def per_device(layer_input, hidden_pre, output_pre, output_grad, weight_a, weight_b):
    side = math.isqrt(layer_input.shape[3])
    half = side // 2
    depth_a = layer_input.shape[2]
    depth_b = depth_a // 2
    source = layer_input[0]
    hidden = hidden_pre[0]
    outer = output_pre[0]
    upstream = output_grad[0]
    chan_in = source.shape[0]
    width_a = hidden.shape[0]
    width_b = outer.shape[0]
    grad_outer = (upstream.astype(jnp.float32) * slopes(outer.astype(jnp.float32))).astype(
        jnp.bfloat16
    )
    hidden_f = hidden.astype(jnp.float32)
    active = jnp.where(hidden_f > 0, hidden_f, negative_slope * hidden_f)
    pooled = (
        active.reshape(width_a, depth_b, 2, half, 2, half, 2)
        .mean(axis=(2, 4, 6))
        .astype(jnp.bfloat16)
    )
    pooled = pooled.reshape(width_a, depth_b, half * half)
    outer_pad = padded_2(grad_outer, (("space", 1),), 1).reshape(width_b, depth_b + 2, half, half)
    pooled_pad = padded_2(pooled, (("space", 1),), 1).reshape(width_a, depth_b + 2, half, half)
    back_b = back_cells(outer_pad, weight_b)
    sums_b = kernel_terms(pooled_pad, grad_outer.reshape(width_b, depth_b, half, half))
    upward = jnp.repeat(jnp.repeat(jnp.repeat(back_b, 2, 1), 2, 2), 2, 3) * 0.125
    upward = upward.reshape(width_a, depth_a * side * side)
    grad_hidden = (upward * slopes(hidden_f.reshape(width_a, depth_a * side * side))).astype(
        jnp.bfloat16
    )
    grad_hidden = grad_hidden.reshape(width_a, depth_a, side * side)
    hidden_pad = padded_2(grad_hidden, (("space", 1),), 1).reshape(width_a, depth_a + 2, side, side)
    source_pad = padded_2(source, (("space", 1),), 1).reshape(chan_in, depth_a + 2, side, side)
    back_a = back_cells(hidden_pad, weight_a)
    sums_a = kernel_terms(source_pad, grad_hidden.reshape(width_a, depth_a, side, side))
    input_grad = back_a.astype(jnp.bfloat16).reshape(1, chan_in, depth_a, side * side)
    total_a, total_b = all_reduce((sums_a, sums_b))
    samples = lax.axis_size("dp")
    planes_a = depth_a * lax.axis_size("space")
    scale_a = 1.0 / math.sqrt(samples * planes_a * side * side)
    scale_b = 1.0 / math.sqrt(samples * (planes_a // 2) * half * half)
    return (input_grad, total_a * scale_a, total_b * scale_b)


def solution(mesh):
    in_specs = (
        P("dp", None, "space", None),
        P("dp", None, "space", None),
        P("dp", None, "space", None),
        P("dp", None, "space", None),
        P(),
        P(),
    )
    out_specs = (P("dp", None, "space", None), P(), P())
    return jax.shard_map(
        per_device, mesh=mesh, in_specs=in_specs, out_specs=out_specs, check_vma=False
    )
```

```python
import math

import jax
import jax.numpy as jnp
from jax import lax
from jax.sharding import PartitionSpec as P
from jax.experimental import pallas as pl
from jax.experimental.pallas import tpu as pltpu

negative_slope = 0.3


def padded_2(cells, sides, width):
    for axis, dim in sides:
        count = lax.axis_size(axis)
        ends = count - 1
        head = lax.slice_in_dim(cells, 0, width, axis=dim)
        tail = lax.slice_in_dim(cells, cells.shape[dim] - width, cells.shape[dim], axis=dim)
        cells = jnp.concatenate(
            [
                lax.ppermute(tail, axis, [(i, (i + 1) % count) for i in range(ends)]),
                cells,
                lax.ppermute(head, axis, [((i + 1) % count, i) for i in range(ends)]),
            ],
            axis=dim,
        )
    return cells


def slopes(values):
    return jnp.where(values > 0, jnp.ones_like(values), negative_slope * jnp.ones_like(values))


def window(padded, tap_z, tap_y, tap_x, depth, side):
    planes = padded[:, tap_z : tap_z + depth, :]
    margin = side + 1
    wider = jnp.pad(planes, ((0, 0), (0, 0), (margin, margin)))
    offset = (tap_y - 1) * side + (tap_x - 1)
    piece = wider[:, :, margin + offset : margin + offset + side * side]
    column = jnp.arange(side * side, dtype=jnp.int32) % side + (tap_x - 1)
    inside = (column >= 0) & (column < side)
    piece = jnp.where(inside, piece, jnp.zeros_like(piece))
    return piece.reshape(padded.shape[0], depth * side * side)


def outer_product(left, right):
    return lax.dot_general(
        left, right, (((1,), (1,)), ((), ())), preferred_element_type=jnp.float32
    )


def _all_reduce_kernel(x_ref, o_a, o_b, full, recv_a, acc_a, recv_1, acc_1, recv_2, acc_2, recv_3, sends, recvs):
    rows = x_ref.shape[0]
    half = rows // 2
    part = half // 3
    quarter, piece = part // 4, part // 16
    mesh_id = pl.DeviceIdType.MESH
    dp = lax.axis_index("dp")
    sp = lax.axis_index("space")
    core = dp % 2
    spot = {"x": dp // 2, "y": sp // 4, "z": sp % 4}
    partner = (spot["x"] * 2 + (1 - core), sp)

    def peer(axis, k):
        moved = dict(spot)
        moved[axis] = (spot[axis] + k) % 4
        return (moved["x"] * 2 + core, moved["y"] * 4 + moved["z"])

    orders = (("x", "y", "z"), ("y", "z", "x"), ("z", "x", "y"))
    peers = [partner] + [peer(axis, k) for axis in "xyz" for k in (1, 2, 3)]
    barrier = pltpu.get_barrier_semaphore()
    for other in peers:
        pl.semaphore_signal(barrier, inc=1, device_id=other, device_id_type=mesh_id)
    pl.semaphore_wait(barrier, len(peers))

    def rows_at(start, size):
        return pl.ds(pl.multiple_of(start, 8), size)

    used = [0]

    def exchange(triples):
        copies = []
        for src, dst, other in triples:
            copy = pltpu.make_async_remote_copy(
                src_ref=src,
                dst_ref=dst,
                send_sem=sends.at[used[0]],
                recv_sem=recvs.at[used[0]],
                device_id=other,
                device_id_type=mesh_id,
            )
            used[0] += 1
            copy.start()
            copies.append(copy)
        for copy in copies:
            copy.wait()

    exchange([(x_ref.at[rows_at((1 - core) * half, half)], recv_a, partner)])
    acc_a[...] = x_ref[rows_at(core * half, half), :] + recv_a[...]
    triples = []
    for p, order in enumerate(orders):
        for k in (1, 2, 3):
            block = p * part + ((spot[order[0]] + k) % 4) * quarter
            triples.append((acc_a.at[rows_at(block, quarter)], recv_1.at[p, k - 1], peer(order[0], k)))
    exchange(triples)
    for p, order in enumerate(orders):
        mine = p * part + spot[order[0]] * quarter
        acc_1[p] = acc_a[rows_at(mine, quarter), :] + recv_1[p, 0] + recv_1[p, 1] + recv_1[p, 2]
    triples = []
    for p, order in enumerate(orders):
        for k in (1, 2, 3):
            block = ((spot[order[1]] + k) % 4) * piece
            triples.append((acc_1.at[p, rows_at(block, piece)], recv_2.at[p, k - 1], peer(order[1], k)))
    exchange(triples)
    for p, order in enumerate(orders):
        mine = spot[order[1]] * piece
        recv_3[p, 0] = acc_1[p, rows_at(mine, piece), :] + recv_2[p, 0] + recv_2[p, 1] + recv_2[p, 2]
    exchange([(recv_3.at[p, 0], recv_3.at[p, k], peer(order[2], k)) for p, order in enumerate(orders) for k in (1, 2, 3)])
    spans = []
    for p, order in enumerate(orders):
        last = spot[order[2]]
        total = recv_3[p, last % 4]
        for j in (1, 2, 3):
            total = total + recv_3[p, (last - j + 4) % 4]
        outer = core * half + p * part + spot[order[0]] * quarter
        own = outer + spot[order[1]] * piece
        full[rows_at(own, piece), :] = total
        spans.append((outer, own, order))
    exchange([(full.at[rows_at(own, piece)], full.at[rows_at(own, piece)], peer(order[1], k)) for outer, own, order in spans for k in (1, 2, 3)])
    exchange([(full.at[rows_at(outer, quarter)], full.at[rows_at(outer, quarter)], peer(order[0], k)) for outer, own, order in spans for k in (1, 2, 3)])
    block = full.at[rows_at(core * half, half)]
    exchange([(block, block, partner)])
    rows_a, rows_b = o_a.shape[0], o_b.shape[0]
    o_a[...] = full[0:rows_a, :]
    o_b[:, 0:128] = full[rows_a : rows_a + rows_b, :]
    o_b[:, 128:256] = full[rows_a + rows_b : rows_a + 2 * rows_b, :]


def all_reduce(sums_a, sums_b, scale_a, scale_b):
    rows_a = sums_a.shape[0] * sums_a.shape[1]
    rows_b = sums_b.shape[0] * sums_b.shape[1]
    wide = sums_b.reshape(rows_b, 256) * scale_b
    flat = jnp.concatenate([sums_a.reshape(rows_a, 128) * scale_a, wide[:, :128], wide[:, 128:]])
    count = flat.shape[0]
    unit = 6 * 16 * 8
    rows = -(-count // unit) * unit
    flat = jnp.pad(flat, ((0, rows - count), (0, 0)))
    half = rows // 2
    part = half // 3
    quarter, piece = part // 4, part // 16
    f32 = jnp.float32
    out_a, out_b = pl.pallas_call(
        _all_reduce_kernel,
        out_shape=(jax.ShapeDtypeStruct((rows_a, 128), f32), jax.ShapeDtypeStruct((rows_b, 256), f32)),
        in_specs=[pl.BlockSpec(memory_space=pltpu.VMEM)],
        out_specs=(pl.BlockSpec(memory_space=pltpu.VMEM), pl.BlockSpec(memory_space=pltpu.VMEM)),
        scratch_shapes=[
            pltpu.VMEM((rows, 128), f32),
            pltpu.VMEM((half, 128), f32),
            pltpu.VMEM((half, 128), f32),
            pltpu.VMEM((3, 3, quarter, 128), f32),
            pltpu.VMEM((3, quarter, 128), f32),
            pltpu.VMEM((3, 3, piece, 128), f32),
            pltpu.VMEM((3, piece, 128), f32),
            pltpu.VMEM((3, 4, piece, 128), f32),
            pltpu.SemaphoreType.DMA((47,)),
            pltpu.SemaphoreType.DMA((47,)),
        ],
        compiler_params=pltpu.CompilerParams(collective_id=0, has_side_effects=True),
    )(flat)
    return out_a.reshape(sums_a.shape), out_b.reshape(sums_b.shape)


def conv_cells(field, kernel):
    shaped = kernel.reshape(3, 3, 3, kernel.shape[1], kernel.shape[2])
    result = lax.conv_general_dilated(
        field[None],
        shaped,
        (1, 1, 1),
        ((0, 0), (1, 1), (1, 1)),
        dimension_numbers=("NCDHW", "DHWIO", "NCDHW"),
        preferred_element_type=jnp.float32,
    )
    return result[0]


def back_cells(padded, kernel):
    flipped = kernel[::-1].transpose(0, 2, 1)
    return conv_cells(padded, flipped)


def kernel_terms(padded, upstream):
    taps, chan_in, chan_out = 27, padded.shape[0], upstream.shape[0]
    start = jnp.zeros((taps, chan_in, chan_out), jnp.float32)
    field = padded.astype(jnp.float32)
    unused, pull = jax.vjp(lambda w: conv_cells(field, w), start)
    return pull(upstream.astype(jnp.float32))[0]


def per_device(layer_input, hidden_pre, output_pre, output_grad, weight_a, weight_b):
    side = math.isqrt(layer_input.shape[3])
    half = side // 2
    depth_a = layer_input.shape[2]
    depth_b = depth_a // 2
    source = layer_input[0]
    hidden = hidden_pre[0]
    outer = output_pre[0]
    upstream = output_grad[0]
    chan_in = source.shape[0]
    width_a = hidden.shape[0]
    width_b = outer.shape[0]
    grad_outer = (upstream.astype(jnp.float32) * slopes(outer.astype(jnp.float32))).astype(
        jnp.bfloat16
    )
    hidden_f = hidden.astype(jnp.float32)
    active = jnp.where(hidden_f > 0, hidden_f, negative_slope * hidden_f)
    pooled = (
        active.reshape(width_a, depth_b, 2, half, 2, half, 2)
        .mean(axis=(2, 4, 6))
        .astype(jnp.bfloat16)
    )
    pooled = pooled.reshape(width_a, depth_b, half * half)
    outer_pad = padded_2(grad_outer, (("space", 1),), 1).reshape(width_b, depth_b + 2, half, half)
    pooled_pad = padded_2(pooled, (("space", 1),), 1).reshape(width_a, depth_b + 2, half, half)
    back_b = back_cells(outer_pad, weight_b)
    sums_b = kernel_terms(pooled_pad, grad_outer.reshape(width_b, depth_b, half, half))
    upward = jnp.repeat(jnp.repeat(jnp.repeat(back_b, 2, 1), 2, 2), 2, 3) * 0.125
    upward = upward.reshape(width_a, depth_a * side * side)
    grad_hidden = (upward * slopes(hidden_f.reshape(width_a, depth_a * side * side))).astype(
        jnp.bfloat16
    )
    grad_hidden = grad_hidden.reshape(width_a, depth_a, side * side)
    hidden_pad = padded_2(grad_hidden, (("space", 1),), 1).reshape(width_a, depth_a + 2, side, side)
    source_pad = padded_2(source, (("space", 1),), 1).reshape(chan_in, depth_a + 2, side, side)
    back_a = back_cells(hidden_pad, weight_a)
    sums_a = kernel_terms(source_pad, grad_hidden.reshape(width_a, depth_a, side, side))
    input_grad = back_a.astype(jnp.bfloat16).reshape(1, chan_in, depth_a, side * side)
    samples = lax.axis_size("dp")
    planes_a = depth_a * lax.axis_size("space")
    scale_a = 1.0 / math.sqrt(samples * planes_a * side * side)
    scale_b = 1.0 / math.sqrt(samples * (planes_a // 2) * half * half)
    total_a, total_b = all_reduce(sums_a, sums_b, scale_a, scale_b)
    return (input_grad, total_a, total_b)


def solution(mesh):
    in_specs = (
        P("dp", None, "space", None),
        P("dp", None, "space", None),
        P("dp", None, "space", None),
        P("dp", None, "space", None),
        P(),
        P(),
    )
    out_specs = (P("dp", None, "space", None), P(), P())
    return jax.shard_map(
        per_device, mesh=mesh, in_specs=in_specs, out_specs=out_specs, check_vma=False
    )
```

```python
import math

import jax
import jax.numpy as jnp
from jax import lax
from jax.sharding import PartitionSpec as P
from jax.experimental import pallas as pl
from jax.experimental.pallas import tpu as pltpu

negative_slope = 0.3


def padded_2(cells, sides, width):
    for axis, dim in sides:
        count = lax.axis_size(axis)
        ends = count - 1
        head = lax.slice_in_dim(cells, 0, width, axis=dim)
        tail = lax.slice_in_dim(cells, cells.shape[dim] - width, cells.shape[dim], axis=dim)
        cells = jnp.concatenate(
            [
                lax.ppermute(tail, axis, [(i, (i + 1) % count) for i in range(ends)]),
                cells,
                lax.ppermute(head, axis, [((i + 1) % count, i) for i in range(ends)]),
            ],
            axis=dim,
        )
    return cells


def slopes(values):
    return jnp.where(values > 0, jnp.ones_like(values), negative_slope * jnp.ones_like(values))


def window(padded, tap_z, tap_y, tap_x, depth, side):
    planes = padded[:, tap_z : tap_z + depth, :]
    margin = side + 1
    wider = jnp.pad(planes, ((0, 0), (0, 0), (margin, margin)))
    offset = (tap_y - 1) * side + (tap_x - 1)
    piece = wider[:, :, margin + offset : margin + offset + side * side]
    column = jnp.arange(side * side, dtype=jnp.int32) % side + (tap_x - 1)
    inside = (column >= 0) & (column < side)
    piece = jnp.where(inside, piece, jnp.zeros_like(piece))
    return piece.reshape(padded.shape[0], depth * side * side)


def outer_product(left, right):
    return lax.dot_general(
        left, right, (((1,), (1,)), ((), ())), preferred_element_type=jnp.float32
    )


def _all_reduce_kernel(
    x_ref, o_a, o_b, full, out_a, recv_a, acc_a, send_1, recv_1, acc_1, recv_2, recv_3, sends, recvs
):
    rows = x_ref.shape[0]
    half = rows // 2
    part = half // 3
    quarter, piece = part // 4, part // 16
    wire = full.dtype
    mesh_id = pl.DeviceIdType.MESH
    dp = lax.axis_index("dp")
    sp = lax.axis_index("space")
    core = dp % 2
    spot = {"x": dp // 2, "y": sp // 4, "z": sp % 4}
    partner = (spot["x"] * 2 + (1 - core), sp)

    def peer(axis, k):
        moved = dict(spot)
        moved[axis] = (spot[axis] + k) % 4
        return (moved["x"] * 2 + core, moved["y"] * 4 + moved["z"])

    orders = (("x", "y", "z"), ("y", "z", "x"), ("z", "x", "y"))
    peers = [partner] + [peer(axis, k) for axis in "xyz" for k in (1, 2, 3)]
    barrier = pltpu.get_barrier_semaphore()
    for other in peers:
        pl.semaphore_signal(barrier, inc=1, device_id=other, device_id_type=mesh_id)
    pl.semaphore_wait(barrier, len(peers))

    def rows_at(start, size):
        return pl.ds(pl.multiple_of(start, 16), size)

    used = [0]

    def exchange(triples):
        copies = []
        for src, dst, other in triples:
            copy = pltpu.make_async_remote_copy(
                src_ref=src,
                dst_ref=dst,
                send_sem=sends.at[used[0]],
                recv_sem=recvs.at[used[0]],
                device_id=other,
                device_id_type=mesh_id,
            )
            used[0] += 1
            copy.start()
            copies.append(copy)
        for copy in copies:
            copy.wait()

    out_a[...] = x_ref[rows_at((1 - core) * half, half), :].astype(wire)
    exchange([(out_a, recv_a, partner)])
    acc_a[...] = x_ref[rows_at(core * half, half), :] + recv_a[...].astype(jnp.float32)
    out_a[...] = acc_a[...].astype(wire)
    triples = []
    for p, order in enumerate(orders):
        for k in (1, 2, 3):
            block = p * part + ((spot[order[0]] + k) % 4) * quarter
            triples.append((out_a.at[rows_at(block, quarter)], recv_1.at[p, k - 1], peer(order[0], k)))
    exchange(triples)
    for p, order in enumerate(orders):
        mine = p * part + spot[order[0]] * quarter
        total = acc_a[rows_at(mine, quarter), :]
        for k in range(3):
            total = total + recv_1[p, k].astype(jnp.float32)
        acc_1[p] = total
        send_1[p] = total.astype(wire)
    triples = []
    for p, order in enumerate(orders):
        for k in (1, 2, 3):
            block = ((spot[order[1]] + k) % 4) * piece
            triples.append((send_1.at[p, rows_at(block, piece)], recv_2.at[p, k - 1], peer(order[1], k)))
    exchange(triples)
    for p, order in enumerate(orders):
        mine = spot[order[1]] * piece
        total = acc_1[p, rows_at(mine, piece), :]
        for k in range(3):
            total = total + recv_2[p, k].astype(jnp.float32)
        recv_3[p, 0] = total.astype(wire)
    exchange([(recv_3.at[p, 0], recv_3.at[p, k], peer(order[2], k)) for p, order in enumerate(orders) for k in (1, 2, 3)])
    spans = []
    for p, order in enumerate(orders):
        last = spot[order[2]]
        total = recv_3[p, last % 4].astype(jnp.float32)
        for j in (1, 2, 3):
            total = total + recv_3[p, (last - j + 4) % 4].astype(jnp.float32)
        outer = core * half + p * part + spot[order[0]] * quarter
        own = outer + spot[order[1]] * piece
        full[rows_at(own, piece), :] = total.astype(wire)
        spans.append((outer, own, order))
    exchange([(full.at[rows_at(own, piece)], full.at[rows_at(own, piece)], peer(order[1], k)) for outer, own, order in spans for k in (1, 2, 3)])
    exchange([(full.at[rows_at(outer, quarter)], full.at[rows_at(outer, quarter)], peer(order[0], k)) for outer, own, order in spans for k in (1, 2, 3)])
    block = full.at[rows_at(core * half, half)]
    exchange([(block, block, partner)])
    rows_a, rows_b = o_a.shape[0], o_b.shape[0]
    o_a[...] = full[0:rows_a, :].astype(jnp.float32)
    o_b[:, 0:128] = full[rows_a : rows_a + rows_b, :].astype(jnp.float32)
    o_b[:, 128:256] = full[rows_a + rows_b : rows_a + 2 * rows_b, :].astype(jnp.float32)


def all_reduce(sums_a, sums_b, scale_a, scale_b):
    rows_a = sums_a.shape[0] * sums_a.shape[1]
    rows_b = sums_b.shape[0] * sums_b.shape[1]
    wide = sums_b.reshape(rows_b, 256) * scale_b
    flat = jnp.concatenate([sums_a.reshape(rows_a, 128) * scale_a, wide[:, :128], wide[:, 128:]])
    count = flat.shape[0]
    unit = 6 * 16 * 16
    rows = -(-count // unit) * unit
    flat = jnp.pad(flat, ((0, rows - count), (0, 0)))
    half = rows // 2
    part = half // 3
    quarter, piece = part // 4, part // 16
    f32, wire = jnp.float32, jnp.bfloat16
    out_a, out_b = pl.pallas_call(
        _all_reduce_kernel,
        out_shape=(jax.ShapeDtypeStruct((rows_a, 128), f32), jax.ShapeDtypeStruct((rows_b, 256), f32)),
        in_specs=[pl.BlockSpec(memory_space=pltpu.VMEM)],
        out_specs=(pl.BlockSpec(memory_space=pltpu.VMEM), pl.BlockSpec(memory_space=pltpu.VMEM)),
        scratch_shapes=[
            pltpu.VMEM((rows, 128), wire),
            pltpu.VMEM((half, 128), wire),
            pltpu.VMEM((half, 128), wire),
            pltpu.VMEM((half, 128), f32),
            pltpu.VMEM((3, quarter, 128), wire),
            pltpu.VMEM((3, 3, quarter, 128), wire),
            pltpu.VMEM((3, quarter, 128), f32),
            pltpu.VMEM((3, 3, piece, 128), wire),
            pltpu.VMEM((3, 4, piece, 128), wire),
            pltpu.SemaphoreType.DMA((47,)),
            pltpu.SemaphoreType.DMA((47,)),
        ],
        compiler_params=pltpu.CompilerParams(collective_id=0, has_side_effects=True),
    )(flat)
    return out_a.reshape(sums_a.shape), out_b.reshape(sums_b.shape)


def conv_cells(field, kernel):
    shaped = kernel.reshape(3, 3, 3, kernel.shape[1], kernel.shape[2])
    result = lax.conv_general_dilated(
        field[None],
        shaped,
        (1, 1, 1),
        ((0, 0), (1, 1), (1, 1)),
        dimension_numbers=("NCDHW", "DHWIO", "NCDHW"),
        preferred_element_type=jnp.float32,
    )
    return result[0]


def back_cells(padded, kernel):
    flipped = kernel[::-1].transpose(0, 2, 1)
    return conv_cells(padded, flipped)


def kernel_terms(padded, upstream):
    taps, chan_in, chan_out = 27, padded.shape[0], upstream.shape[0]
    start = jnp.zeros((taps, chan_in, chan_out), jnp.float32)
    field = padded.astype(jnp.float32)
    unused, pull = jax.vjp(lambda w: conv_cells(field, w), start)
    return pull(upstream.astype(jnp.float32))[0]


def per_device(layer_input, hidden_pre, output_pre, output_grad, weight_a, weight_b):
    side = math.isqrt(layer_input.shape[3])
    half = side // 2
    depth_a = layer_input.shape[2]
    depth_b = depth_a // 2
    source = layer_input[0]
    hidden = hidden_pre[0]
    outer = output_pre[0]
    upstream = output_grad[0]
    chan_in = source.shape[0]
    width_a = hidden.shape[0]
    width_b = outer.shape[0]
    grad_outer = (upstream.astype(jnp.float32) * slopes(outer.astype(jnp.float32))).astype(
        jnp.bfloat16
    )
    hidden_f = hidden.astype(jnp.float32)
    active = jnp.where(hidden_f > 0, hidden_f, negative_slope * hidden_f)
    pooled = (
        active.reshape(width_a, depth_b, 2, half, 2, half, 2)
        .mean(axis=(2, 4, 6))
        .astype(jnp.bfloat16)
    )
    pooled = pooled.reshape(width_a, depth_b, half * half)
    outer_pad = padded_2(grad_outer, (("space", 1),), 1).reshape(width_b, depth_b + 2, half, half)
    pooled_pad = padded_2(pooled, (("space", 1),), 1).reshape(width_a, depth_b + 2, half, half)
    back_b = back_cells(outer_pad, weight_b)
    sums_b = kernel_terms(pooled_pad, grad_outer.reshape(width_b, depth_b, half, half))
    upward = jnp.repeat(jnp.repeat(jnp.repeat(back_b, 2, 1), 2, 2), 2, 3) * 0.125
    upward = upward.reshape(width_a, depth_a * side * side)
    grad_hidden = (upward * slopes(hidden_f.reshape(width_a, depth_a * side * side))).astype(
        jnp.bfloat16
    )
    grad_hidden = grad_hidden.reshape(width_a, depth_a, side * side)
    hidden_pad = padded_2(grad_hidden, (("space", 1),), 1).reshape(width_a, depth_a + 2, side, side)
    source_pad = padded_2(source, (("space", 1),), 1).reshape(chan_in, depth_a + 2, side, side)
    back_a = back_cells(hidden_pad, weight_a)
    sums_a = kernel_terms(source_pad, grad_hidden.reshape(width_a, depth_a, side, side))
    input_grad = back_a.astype(jnp.bfloat16).reshape(1, chan_in, depth_a, side * side)
    samples = lax.axis_size("dp")
    planes_a = depth_a * lax.axis_size("space")
    scale_a = 1.0 / math.sqrt(samples * planes_a * side * side)
    scale_b = 1.0 / math.sqrt(samples * (planes_a // 2) * half * half)
    total_a, total_b = all_reduce(sums_a, sums_b, scale_a, scale_b)
    return (input_grad, total_a, total_b)


def solution(mesh):
    in_specs = (
        P("dp", None, "space", None),
        P("dp", None, "space", None),
        P("dp", None, "space", None),
        P("dp", None, "space", None),
        P(),
        P(),
    )
    out_specs = (P("dp", None, "space", None), P(), P())
    return jax.shard_map(
        per_device, mesh=mesh, in_specs=in_specs, out_specs=out_specs, check_vma=False
    )
```

```python
import math

import jax
import jax.numpy as jnp
from jax import lax
from jax.sharding import PartitionSpec as P
from jax.experimental import pallas as pl
from jax.experimental.pallas import tpu as pltpu

negative_slope = 0.3


def padded_2(cells, sides, width):
    for axis, dim in sides:
        count = lax.axis_size(axis)
        ends = count - 1
        head = lax.slice_in_dim(cells, 0, width, axis=dim)
        tail = lax.slice_in_dim(cells, cells.shape[dim] - width, cells.shape[dim], axis=dim)
        cells = jnp.concatenate(
            [
                lax.ppermute(tail, axis, [(i, (i + 1) % count) for i in range(ends)]),
                cells,
                lax.ppermute(head, axis, [((i + 1) % count, i) for i in range(ends)]),
            ],
            axis=dim,
        )
    return cells


def slopes(values):
    return jnp.where(values > 0, jnp.ones_like(values), negative_slope * jnp.ones_like(values))


def window(padded, tap_z, tap_y, tap_x, depth, side):
    planes = padded[:, tap_z : tap_z + depth, :]
    margin = side + 1
    wider = jnp.pad(planes, ((0, 0), (0, 0), (margin, margin)))
    offset = (tap_y - 1) * side + (tap_x - 1)
    piece = wider[:, :, margin + offset : margin + offset + side * side]
    column = jnp.arange(side * side, dtype=jnp.int32) % side + (tap_x - 1)
    inside = (column >= 0) & (column < side)
    piece = jnp.where(inside, piece, jnp.zeros_like(piece))
    return piece.reshape(padded.shape[0], depth * side * side)


def outer_product(left, right):
    return lax.dot_general(
        left, right, (((1,), (1,)), ((), ())), preferred_element_type=jnp.float32
    )


def _all_reduce_kernel(x_ref, o_a, o_b, full, recv_a, acc_a, recv_1, acc_1, recv_2, acc_2, recv_3, sends, recvs):
    rows = x_ref.shape[0]
    half = rows // 2
    part = half // 3
    quarter, piece = part // 4, part // 16
    mesh_id = pl.DeviceIdType.MESH
    dp = lax.axis_index("dp")
    sp = lax.axis_index("space")
    core = dp % 2
    spot = {"x": dp // 2, "y": sp // 4, "z": sp % 4}
    partner = (spot["x"] * 2 + (1 - core), sp)

    def peer(axis, k):
        moved = dict(spot)
        moved[axis] = (spot[axis] + k) % 4
        return (moved["x"] * 2 + core, moved["y"] * 4 + moved["z"])

    orders = (("x", "y", "z"), ("y", "z", "x"), ("z", "x", "y"))
    peers = [partner] + [peer(axis, k) for axis in "xyz" for k in (1, 2, 3)]
    barrier = pltpu.get_barrier_semaphore()
    for other in peers:
        pl.semaphore_signal(barrier, inc=1, device_id=other, device_id_type=mesh_id)
    pl.semaphore_wait(barrier, len(peers))

    def rows_at(start, size):
        return pl.ds(pl.multiple_of(start, 8), size)

    used = [0]

    def exchange(triples):
        copies = []
        for src, dst, other in triples:
            copy = pltpu.make_async_remote_copy(
                src_ref=src,
                dst_ref=dst,
                send_sem=sends.at[used[0]],
                recv_sem=recvs.at[used[0]],
                device_id=other,
                device_id_type=mesh_id,
            )
            used[0] += 1
            copy.start()
            copies.append(copy)
        for copy in copies:
            copy.wait()

    exchange([(x_ref.at[rows_at((1 - core) * half, half)], recv_a, partner)])
    acc_a[...] = x_ref[rows_at(core * half, half), :] + recv_a[...]
    triples = []
    for p, order in enumerate(orders):
        for k in (1, 2, 3):
            block = p * part + ((spot[order[0]] + k) % 4) * quarter
            triples.append((acc_a.at[rows_at(block, quarter)], recv_1.at[p, k - 1], peer(order[0], k)))
    exchange(triples)
    for p, order in enumerate(orders):
        mine = p * part + spot[order[0]] * quarter
        acc_1[p] = acc_a[rows_at(mine, quarter), :] + recv_1[p, 0] + recv_1[p, 1] + recv_1[p, 2]
    triples = []
    for p, order in enumerate(orders):
        for k in (1, 2, 3):
            block = ((spot[order[1]] + k) % 4) * piece
            triples.append((acc_1.at[p, rows_at(block, piece)], recv_2.at[p, k - 1], peer(order[1], k)))
    exchange(triples)
    for p, order in enumerate(orders):
        mine = spot[order[1]] * piece
        recv_3[p, 0] = acc_1[p, rows_at(mine, piece), :] + recv_2[p, 0] + recv_2[p, 1] + recv_2[p, 2]
    exchange([(recv_3.at[p, 0], recv_3.at[p, k], peer(order[2], k)) for p, order in enumerate(orders) for k in (1, 2, 3)])
    spans = []
    for p, order in enumerate(orders):
        last = spot[order[2]]
        total = recv_3[p, last % 4]
        for j in (1, 2, 3):
            total = total + recv_3[p, (last - j + 4) % 4]
        outer = core * half + p * part + spot[order[0]] * quarter
        own = outer + spot[order[1]] * piece
        full[rows_at(own, piece), :] = total
        spans.append((outer, own, order))
    exchange([(full.at[rows_at(own, piece)], full.at[rows_at(own, piece)], peer(order[1], k)) for outer, own, order in spans for k in (1, 2, 3)])
    exchange([(full.at[rows_at(outer, quarter)], full.at[rows_at(outer, quarter)], peer(order[0], k)) for outer, own, order in spans for k in (1, 2, 3)])
    block = full.at[rows_at(core * half, half)]
    exchange([(block, block, partner)])
    rows_a, rows_b = o_a.shape[0], o_b.shape[0]
    o_a[...] = full[0:rows_a, :]
    o_b[:, 0:128] = full[rows_a : rows_a + rows_b, :]
    o_b[:, 128:256] = full[rows_a + rows_b : rows_a + 2 * rows_b, :]


def all_reduce(sums_a, sums_b, scale_a, scale_b):
    rows_a = sums_a.shape[0] * sums_a.shape[1]
    rows_b = sums_b.shape[0] * sums_b.shape[1]
    wide = sums_b.reshape(rows_b, 256) * scale_b
    flat = jnp.concatenate([sums_a.reshape(rows_a, 128) * scale_a, wide[:, :128], wide[:, 128:]])
    count = flat.shape[0]
    unit = 6 * 16 * 8
    rows = -(-count // unit) * unit
    flat = jnp.pad(flat, ((0, rows - count), (0, 0)))
    half = rows // 2
    part = half // 3
    quarter, piece = part // 4, part // 16
    f32 = jnp.float32
    out_a, out_b = pl.pallas_call(
        _all_reduce_kernel,
        out_shape=(jax.ShapeDtypeStruct((rows_a, 128), f32), jax.ShapeDtypeStruct((rows_b, 256), f32)),
        in_specs=[pl.BlockSpec(memory_space=pltpu.VMEM)],
        out_specs=(pl.BlockSpec(memory_space=pltpu.VMEM), pl.BlockSpec(memory_space=pltpu.VMEM)),
        scratch_shapes=[
            pltpu.VMEM((rows, 128), f32),
            pltpu.VMEM((half, 128), f32),
            pltpu.VMEM((half, 128), f32),
            pltpu.VMEM((3, 3, quarter, 128), f32),
            pltpu.VMEM((3, quarter, 128), f32),
            pltpu.VMEM((3, 3, piece, 128), f32),
            pltpu.VMEM((3, piece, 128), f32),
            pltpu.VMEM((3, 4, piece, 128), f32),
            pltpu.SemaphoreType.DMA((47,)),
            pltpu.SemaphoreType.DMA((47,)),
        ],
        compiler_params=pltpu.CompilerParams(collective_id=0, has_side_effects=True),
    )(flat)
    return out_a.reshape(sums_a.shape), out_b.reshape(sums_b.shape)


def conv_cells(field, kernel):
    shaped = kernel.reshape(3, 3, 3, kernel.shape[1], kernel.shape[2])
    result = lax.conv_general_dilated(
        field[None],
        shaped,
        (1, 1, 1),
        ((0, 0), (1, 1), (1, 1)),
        dimension_numbers=("NCDHW", "DHWIO", "NCDHW"),
        preferred_element_type=jnp.float32,
    )
    return result[0]


def back_cells(padded, kernel):
    flipped = kernel[::-1].transpose(0, 2, 1)
    return conv_cells(padded, flipped)


def kernel_terms(padded, upstream):
    result = lax.conv_general_dilated(
        padded[None],
        upstream[None],
        (1, 1, 1),
        ((0, 0), (1, 1), (1, 1)),
        dimension_numbers=("CNDHW", "IODHW", "DHWNC"),
        preferred_element_type=jnp.float32,
    )
    return result.reshape(27, padded.shape[0], upstream.shape[0])


def halos(arrays):
    count = lax.axis_size("space")
    tails = jnp.concatenate([a[:, -1:].reshape(-1) for a in arrays])
    heads = jnp.concatenate([a[:, :1].reshape(-1) for a in arrays])
    below = lax.ppermute(tails, "space", [(i, i + 1) for i in range(count - 1)])
    above = lax.ppermute(heads, "space", [(i + 1, i) for i in range(count - 1)])
    out, start = [], 0
    for a in arrays:
        size = a.shape[0] * a.shape[2]
        shape = (a.shape[0], 1, a.shape[2])
        low = below[start : start + size].reshape(shape)
        high = above[start : start + size].reshape(shape)
        out.append(jnp.concatenate([low, a, high], axis=1))
        start += size
    return out


def per_device(layer_input, hidden_pre, output_pre, output_grad, weight_a, weight_b):
    side = math.isqrt(layer_input.shape[3])
    half = side // 2
    depth_a = layer_input.shape[2]
    depth_b = depth_a // 2
    source = layer_input[0]
    hidden = hidden_pre[0]
    outer = output_pre[0]
    upstream = output_grad[0]
    chan_in = source.shape[0]
    width_a = hidden.shape[0]
    width_b = outer.shape[0]
    grad_outer = (upstream.astype(jnp.float32) * slopes(outer.astype(jnp.float32))).astype(
        jnp.bfloat16
    )
    hidden_f = hidden.astype(jnp.float32)
    active = jnp.where(hidden_f > 0, hidden_f, negative_slope * hidden_f)
    pooled = (
        active.reshape(width_a, depth_b, 2, half, 2, half, 2)
        .mean(axis=(2, 4, 6))
        .astype(jnp.bfloat16)
    )
    pooled = pooled.reshape(width_a, depth_b, half * half)
    outer_pad, pooled_pad, source_pad = halos([grad_outer, pooled, source])
    outer_pad = outer_pad.reshape(width_b, depth_b + 2, half, half)
    pooled_pad = pooled_pad.reshape(width_a, depth_b + 2, half, half)
    source_pad = source_pad.reshape(chan_in, depth_a + 2, side, side)
    back_b = back_cells(outer_pad, weight_b)
    sums_b = kernel_terms(pooled_pad, grad_outer.reshape(width_b, depth_b, half, half))
    upward = jnp.repeat(jnp.repeat(jnp.repeat(back_b, 2, 1), 2, 2), 2, 3) * 0.125
    upward = upward.reshape(width_a, depth_a * side * side)
    grad_hidden = (upward * slopes(hidden_f.reshape(width_a, depth_a * side * side))).astype(
        jnp.bfloat16
    )
    grad_hidden = grad_hidden.reshape(width_a, depth_a, side * side)
    (hidden_pad,) = halos([grad_hidden])
    hidden_pad = hidden_pad.reshape(width_a, depth_a + 2, side, side)
    back_a = back_cells(hidden_pad, weight_a)
    sums_a = kernel_terms(source_pad, grad_hidden.reshape(width_a, depth_a, side, side))
    input_grad = back_a.astype(jnp.bfloat16).reshape(1, chan_in, depth_a, side * side)
    samples = lax.axis_size("dp")
    planes_a = depth_a * lax.axis_size("space")
    scale_a = 1.0 / math.sqrt(samples * planes_a * side * side)
    scale_b = 1.0 / math.sqrt(samples * (planes_a // 2) * half * half)
    total_a, total_b = all_reduce(sums_a, sums_b, scale_a, scale_b)
    return (input_grad, total_a, total_b)


def solution(mesh):
    in_specs = (
        P("dp", None, "space", None),
        P("dp", None, "space", None),
        P("dp", None, "space", None),
        P("dp", None, "space", None),
        P(),
        P(),
    )
    out_specs = (P("dp", None, "space", None), P(), P())
    return jax.shard_map(
        per_device, mesh=mesh, in_specs=in_specs, out_specs=out_specs, check_vma=False
    )
```

```python
import math

import jax
import jax.numpy as jnp
from jax import lax
from jax.sharding import PartitionSpec as P
from jax.experimental import pallas as pl
from jax.experimental.pallas import tpu as pltpu

negative_slope = 0.3


def padded_2(cells, sides, width):
    for axis, dim in sides:
        count = lax.axis_size(axis)
        ends = count - 1
        head = lax.slice_in_dim(cells, 0, width, axis=dim)
        tail = lax.slice_in_dim(cells, cells.shape[dim] - width, cells.shape[dim], axis=dim)
        cells = jnp.concatenate(
            [
                lax.ppermute(tail, axis, [(i, (i + 1) % count) for i in range(ends)]),
                cells,
                lax.ppermute(head, axis, [((i + 1) % count, i) for i in range(ends)]),
            ],
            axis=dim,
        )
    return cells


def slopes(values):
    return jnp.where(values > 0, jnp.ones_like(values), negative_slope * jnp.ones_like(values))


def window(padded, tap_z, tap_y, tap_x, depth, side):
    planes = padded[:, tap_z : tap_z + depth, :]
    margin = side + 1
    wider = jnp.pad(planes, ((0, 0), (0, 0), (margin, margin)))
    offset = (tap_y - 1) * side + (tap_x - 1)
    piece = wider[:, :, margin + offset : margin + offset + side * side]
    column = jnp.arange(side * side, dtype=jnp.int32) % side + (tap_x - 1)
    inside = (column >= 0) & (column < side)
    piece = jnp.where(inside, piece, jnp.zeros_like(piece))
    return piece.reshape(padded.shape[0], depth * side * side)


def outer_product(left, right):
    return lax.dot_general(
        left, right, (((1,), (1,)), ((), ())), preferred_element_type=jnp.float32
    )


def _all_reduce_kernel(x_ref, o_a, o_b, full, recv_a, acc_a, recv_1, acc_1, recv_2, acc_2, recv_3, sends, recvs):
    rows = x_ref.shape[0]
    half = rows // 2
    part = half // 3
    quarter, piece = part // 4, part // 16
    mesh_id = pl.DeviceIdType.MESH
    dp = lax.axis_index("dp")
    sp = lax.axis_index("space")
    core = dp % 2
    spot = {"x": dp // 2, "y": sp // 4, "z": sp % 4}
    partner = (spot["x"] * 2 + (1 - core), sp)

    def peer(axis, k):
        moved = dict(spot)
        moved[axis] = (spot[axis] + k) % 4
        return (moved["x"] * 2 + core, moved["y"] * 4 + moved["z"])

    orders = (("x", "y", "z"), ("y", "z", "x"), ("z", "x", "y"))
    peers = [partner] + [peer(axis, k) for axis in "xyz" for k in (1, 2, 3)]
    barrier = pltpu.get_barrier_semaphore()
    for other in peers:
        pl.semaphore_signal(barrier, inc=1, device_id=other, device_id_type=mesh_id)
    pl.semaphore_wait(barrier, len(peers))

    def rows_at(start, size):
        return pl.ds(pl.multiple_of(start, 8), size)

    used = [0]

    def exchange(triples):
        copies = []
        for src, dst, other in triples:
            copy = pltpu.make_async_remote_copy(
                src_ref=src,
                dst_ref=dst,
                send_sem=sends.at[used[0]],
                recv_sem=recvs.at[used[0]],
                device_id=other,
                device_id_type=mesh_id,
            )
            used[0] += 1
            copy.start()
            copies.append(copy)
        for copy in copies:
            copy.wait()

    chunk = half // 8
    exchange(
        [
            (x_ref.at[rows_at((1 - core) * half + n * chunk, chunk)], recv_a.at[rows_at(n * chunk, chunk)], partner)
            for n in range(8)
        ]
    )
    acc_a[...] = x_ref[rows_at(core * half, half), :] + recv_a[...]
    triples = []
    for p, order in enumerate(orders):
        for k in (1, 2, 3):
            block = p * part + ((spot[order[0]] + k) % 4) * quarter
            triples.append((acc_a.at[rows_at(block, quarter)], recv_1.at[p, k - 1], peer(order[0], k)))
    exchange(triples)
    for p, order in enumerate(orders):
        mine = p * part + spot[order[0]] * quarter
        acc_1[p] = acc_a[rows_at(mine, quarter), :] + recv_1[p, 0] + recv_1[p, 1] + recv_1[p, 2]
    triples = []
    for p, order in enumerate(orders):
        for k in (1, 2, 3):
            block = ((spot[order[1]] + k) % 4) * piece
            triples.append((acc_1.at[p, rows_at(block, piece)], recv_2.at[p, k - 1], peer(order[1], k)))
    exchange(triples)
    for p, order in enumerate(orders):
        mine = spot[order[1]] * piece
        recv_3[p, 0] = acc_1[p, rows_at(mine, piece), :] + recv_2[p, 0] + recv_2[p, 1] + recv_2[p, 2]
    exchange([(recv_3.at[p, 0], recv_3.at[p, k], peer(order[2], k)) for p, order in enumerate(orders) for k in (1, 2, 3)])
    spans = []
    for p, order in enumerate(orders):
        last = spot[order[2]]
        total = recv_3[p, last % 4]
        for j in (1, 2, 3):
            total = total + recv_3[p, (last - j + 4) % 4]
        outer = core * half + p * part + spot[order[0]] * quarter
        own = outer + spot[order[1]] * piece
        full[rows_at(own, piece), :] = total
        spans.append((outer, own, order))
    exchange([(full.at[rows_at(own, piece)], full.at[rows_at(own, piece)], peer(order[1], k)) for outer, own, order in spans for k in (1, 2, 3)])
    exchange([(full.at[rows_at(outer, quarter)], full.at[rows_at(outer, quarter)], peer(order[0], k)) for outer, own, order in spans for k in (1, 2, 3)])
    exchange(
        [
            (full.at[rows_at(core * half + n * chunk, chunk)], full.at[rows_at(core * half + n * chunk, chunk)], partner)
            for n in range(8)
        ]
    )
    rows_a, rows_b = o_a.shape[0], o_b.shape[0]
    o_a[...] = full[0:rows_a, :]
    o_b[:, 0:128] = full[rows_a : rows_a + rows_b, :]
    o_b[:, 128:256] = full[rows_a + rows_b : rows_a + 2 * rows_b, :]


def all_reduce(sums_a, sums_b, scale_a, scale_b):
    rows_a = sums_a.shape[0] * sums_a.shape[1]
    rows_b = sums_b.shape[0] * sums_b.shape[1]
    wide = sums_b.reshape(rows_b, 256) * scale_b
    flat = jnp.concatenate([sums_a.reshape(rows_a, 128) * scale_a, wide[:, :128], wide[:, 128:]])
    count = flat.shape[0]
    unit = 6 * 16 * 8
    rows = -(-count // unit) * unit
    flat = jnp.pad(flat, ((0, rows - count), (0, 0)))
    half = rows // 2
    part = half // 3
    quarter, piece = part // 4, part // 16
    f32 = jnp.float32
    out_a, out_b = pl.pallas_call(
        _all_reduce_kernel,
        out_shape=(jax.ShapeDtypeStruct((rows_a, 128), f32), jax.ShapeDtypeStruct((rows_b, 256), f32)),
        in_specs=[pl.BlockSpec(memory_space=pltpu.VMEM)],
        out_specs=(pl.BlockSpec(memory_space=pltpu.VMEM), pl.BlockSpec(memory_space=pltpu.VMEM)),
        scratch_shapes=[
            pltpu.VMEM((rows, 128), f32),
            pltpu.VMEM((half, 128), f32),
            pltpu.VMEM((half, 128), f32),
            pltpu.VMEM((3, 3, quarter, 128), f32),
            pltpu.VMEM((3, quarter, 128), f32),
            pltpu.VMEM((3, 3, piece, 128), f32),
            pltpu.VMEM((3, piece, 128), f32),
            pltpu.VMEM((3, 4, piece, 128), f32),
            pltpu.SemaphoreType.DMA((61,)),
            pltpu.SemaphoreType.DMA((61,)),
        ],
        compiler_params=pltpu.CompilerParams(collective_id=0, has_side_effects=True),
    )(flat)
    return out_a.reshape(sums_a.shape), out_b.reshape(sums_b.shape)


def conv_cells(field, kernel):
    shaped = kernel.reshape(3, 3, 3, kernel.shape[1], kernel.shape[2])
    result = lax.conv_general_dilated(
        field[None],
        shaped,
        (1, 1, 1),
        ((0, 0), (1, 1), (1, 1)),
        dimension_numbers=("NCDHW", "DHWIO", "NCDHW"),
        preferred_element_type=jnp.float32,
    )
    return result[0]


def back_cells(padded, kernel):
    flipped = kernel[::-1].transpose(0, 2, 1)
    return conv_cells(padded, flipped)


def kernel_terms(padded, upstream):
    taps, chan_in, chan_out = 27, padded.shape[0], upstream.shape[0]
    start = jnp.zeros((taps, chan_in, chan_out), jnp.float32)
    field = padded.astype(jnp.float32)
    unused, pull = jax.vjp(lambda w: conv_cells(field, w), start)
    return pull(upstream.astype(jnp.float32))[0]


def per_device(layer_input, hidden_pre, output_pre, output_grad, weight_a, weight_b):
    side = math.isqrt(layer_input.shape[3])
    half = side // 2
    depth_a = layer_input.shape[2]
    depth_b = depth_a // 2
    source = layer_input[0]
    hidden = hidden_pre[0]
    outer = output_pre[0]
    upstream = output_grad[0]
    chan_in = source.shape[0]
    width_a = hidden.shape[0]
    width_b = outer.shape[0]
    grad_outer = (upstream.astype(jnp.float32) * slopes(outer.astype(jnp.float32))).astype(
        jnp.bfloat16
    )
    hidden_f = hidden.astype(jnp.float32)
    active = jnp.where(hidden_f > 0, hidden_f, negative_slope * hidden_f)
    pooled = (
        active.reshape(width_a, depth_b, 2, half, 2, half, 2)
        .mean(axis=(2, 4, 6))
        .astype(jnp.bfloat16)
    )
    pooled = pooled.reshape(width_a, depth_b, half * half)
    outer_pad = padded_2(grad_outer, (("space", 1),), 1).reshape(width_b, depth_b + 2, half, half)
    pooled_pad = padded_2(pooled, (("space", 1),), 1).reshape(width_a, depth_b + 2, half, half)
    back_b = back_cells(outer_pad, weight_b)
    sums_b = kernel_terms(pooled_pad, grad_outer.reshape(width_b, depth_b, half, half))
    upward = jnp.repeat(jnp.repeat(jnp.repeat(back_b, 2, 1), 2, 2), 2, 3) * 0.125
    upward = upward.reshape(width_a, depth_a * side * side)
    grad_hidden = (upward * slopes(hidden_f.reshape(width_a, depth_a * side * side))).astype(
        jnp.bfloat16
    )
    grad_hidden = grad_hidden.reshape(width_a, depth_a, side * side)
    hidden_pad = padded_2(grad_hidden, (("space", 1),), 1).reshape(width_a, depth_a + 2, side, side)
    source_pad = padded_2(source, (("space", 1),), 1).reshape(chan_in, depth_a + 2, side, side)
    back_a = back_cells(hidden_pad, weight_a)
    sums_a = kernel_terms(source_pad, grad_hidden.reshape(width_a, depth_a, side, side))
    input_grad = back_a.astype(jnp.bfloat16).reshape(1, chan_in, depth_a, side * side)
    samples = lax.axis_size("dp")
    planes_a = depth_a * lax.axis_size("space")
    scale_a = 1.0 / math.sqrt(samples * planes_a * side * side)
    scale_b = 1.0 / math.sqrt(samples * (planes_a // 2) * half * half)
    total_a, total_b = all_reduce(sums_a, sums_b, scale_a, scale_b)
    return (input_grad, total_a, total_b)


def solution(mesh):
    in_specs = (
        P("dp", None, "space", None),
        P("dp", None, "space", None),
        P("dp", None, "space", None),
        P("dp", None, "space", None),
        P(),
        P(),
    )
    out_specs = (P("dp", None, "space", None), P(), P())
    return jax.shard_map(
        per_device, mesh=mesh, in_specs=in_specs, out_specs=out_specs, check_vma=False
    )
```

```python
import math

import jax
import jax.numpy as jnp
from jax import lax
from jax.sharding import PartitionSpec as P
from jax.experimental import pallas as pl
from jax.experimental.pallas import tpu as pltpu

negative_slope = 0.3


def padded_2(cells, sides, width):
    for axis, dim in sides:
        count = lax.axis_size(axis)
        ends = count - 1
        head = lax.slice_in_dim(cells, 0, width, axis=dim)
        tail = lax.slice_in_dim(cells, cells.shape[dim] - width, cells.shape[dim], axis=dim)
        cells = jnp.concatenate(
            [
                lax.ppermute(tail, axis, [(i, (i + 1) % count) for i in range(ends)]),
                cells,
                lax.ppermute(head, axis, [((i + 1) % count, i) for i in range(ends)]),
            ],
            axis=dim,
        )
    return cells


def slopes(values):
    return jnp.where(values > 0, jnp.ones_like(values), negative_slope * jnp.ones_like(values))


def window(padded, tap_z, tap_y, tap_x, depth, side):
    planes = padded[:, tap_z : tap_z + depth, :]
    margin = side + 1
    wider = jnp.pad(planes, ((0, 0), (0, 0), (margin, margin)))
    offset = (tap_y - 1) * side + (tap_x - 1)
    piece = wider[:, :, margin + offset : margin + offset + side * side]
    column = jnp.arange(side * side, dtype=jnp.int32) % side + (tap_x - 1)
    inside = (column >= 0) & (column < side)
    piece = jnp.where(inside, piece, jnp.zeros_like(piece))
    return piece.reshape(padded.shape[0], depth * side * side)


def outer_product(left, right):
    return lax.dot_general(
        left, right, (((1,), (1,)), ((), ())), preferred_element_type=jnp.float32
    )


def _all_reduce_kernel(x_ref, o_a, o_b, full, recv_a, acc_a, recv_1, acc_1, recv_2, acc_2, recv_3, sends, recvs):
    rows = x_ref.shape[0]
    half = rows // 2
    part = half // 3
    quarter, piece = part // 4, part // 16
    mesh_id = pl.DeviceIdType.MESH
    dp = lax.axis_index("dp")
    sp = lax.axis_index("space")
    core = dp % 2
    spot = {"x": dp // 2, "y": sp // 4, "z": sp % 4}
    partner = (spot["x"] * 2 + (1 - core), sp)

    def peer(axis, k):
        moved = dict(spot)
        moved[axis] = (spot[axis] + k) % 4
        return (moved["x"] * 2 + core, moved["y"] * 4 + moved["z"])

    orders = (("x", "y", "z"), ("y", "z", "x"), ("z", "x", "y"))
    peers = [partner] + [peer(axis, k) for axis in "xyz" for k in (1, 2, 3)]
    barrier = pltpu.get_barrier_semaphore()
    for other in peers:
        pl.semaphore_signal(barrier, inc=1, device_id=other, device_id_type=mesh_id)
    pl.semaphore_wait(barrier, len(peers))

    def rows_at(start, size):
        return pl.ds(pl.multiple_of(start, 8), size)

    used = [0]

    def exchange(triples):
        copies = []
        for src, dst, other in triples:
            copy = pltpu.make_async_remote_copy(
                src_ref=src,
                dst_ref=dst,
                send_sem=sends.at[used[0]],
                recv_sem=recvs.at[used[0]],
                device_id=other,
                device_id_type=mesh_id,
            )
            used[0] += 1
            copy.start()
            copies.append(copy)
        for copy in copies:
            copy.wait()

    exchange([(x_ref.at[rows_at((1 - core) * half, half)], recv_a, partner)])
    acc_a[...] = x_ref[rows_at(core * half, half), :] + recv_a[...]
    triples = []
    for p, order in enumerate(orders):
        for k in (1, 2, 3):
            block = p * part + ((spot[order[0]] + k) % 4) * quarter
            triples.append((acc_a.at[rows_at(block, quarter)], recv_1.at[p, k - 1], peer(order[0], k)))
    exchange(triples)
    for p, order in enumerate(orders):
        mine = p * part + spot[order[0]] * quarter
        acc_1[p] = acc_a[rows_at(mine, quarter), :] + recv_1[p, 0] + recv_1[p, 1] + recv_1[p, 2]
    triples = []
    for p, order in enumerate(orders):
        for k in (1, 2, 3):
            block = ((spot[order[1]] + k) % 4) * piece
            triples.append((acc_1.at[p, rows_at(block, piece)], recv_2.at[p, k - 1], peer(order[1], k)))
    exchange(triples)
    for p, order in enumerate(orders):
        mine = spot[order[1]] * piece
        recv_3[p, 0] = acc_1[p, rows_at(mine, piece), :] + recv_2[p, 0] + recv_2[p, 1] + recv_2[p, 2]
    exchange([(recv_3.at[p, 0], recv_3.at[p, k], peer(order[2], k)) for p, order in enumerate(orders) for k in (1, 2, 3)])
    spans = []
    for p, order in enumerate(orders):
        last = spot[order[2]]
        total = recv_3[p, last % 4]
        for j in (1, 2, 3):
            total = total + recv_3[p, (last - j + 4) % 4]
        outer = core * half + p * part + spot[order[0]] * quarter
        own = outer + spot[order[1]] * piece
        full[rows_at(own, piece), :] = total
        spans.append((outer, own, order))
    exchange([(full.at[rows_at(own, piece)], full.at[rows_at(own, piece)], peer(order[1], k)) for outer, own, order in spans for k in (1, 2, 3)])
    exchange([(full.at[rows_at(outer, quarter)], full.at[rows_at(outer, quarter)], peer(order[0], k)) for outer, own, order in spans for k in (1, 2, 3)])
    block = full.at[rows_at(core * half, half)]
    exchange([(block, block, partner)])
    rows_a, rows_b = o_a.shape[0], o_b.shape[0]
    o_a[...] = full[0:rows_a, :]
    o_b[:, 0:128] = full[rows_a : rows_a + rows_b, :]
    o_b[:, 128:256] = full[rows_a + rows_b : rows_a + 2 * rows_b, :]


def all_reduce(sums_a, sums_b, scale_a, scale_b):
    rows_a = sums_a.shape[0] * sums_a.shape[1]
    rows_b = sums_b.shape[0] * sums_b.shape[1]
    wide = sums_b.reshape(rows_b, 256) * scale_b
    flat = jnp.concatenate([sums_a.reshape(rows_a, 128) * scale_a, wide[:, :128], wide[:, 128:]])
    count = flat.shape[0]
    unit = 6 * 16 * 8
    rows = -(-count // unit) * unit
    flat = jnp.pad(flat, ((0, rows - count), (0, 0)))
    half = rows // 2
    part = half // 3
    quarter, piece = part // 4, part // 16
    f32 = jnp.float32
    out_a, out_b = pl.pallas_call(
        _all_reduce_kernel,
        out_shape=(jax.ShapeDtypeStruct((rows_a, 128), f32), jax.ShapeDtypeStruct((rows_b, 256), f32)),
        in_specs=[pl.BlockSpec(memory_space=pltpu.VMEM)],
        out_specs=(pl.BlockSpec(memory_space=pltpu.VMEM), pl.BlockSpec(memory_space=pltpu.VMEM)),
        scratch_shapes=[
            pltpu.VMEM((rows, 128), f32),
            pltpu.VMEM((half, 128), f32),
            pltpu.VMEM((half, 128), f32),
            pltpu.VMEM((3, 3, quarter, 128), f32),
            pltpu.VMEM((3, quarter, 128), f32),
            pltpu.VMEM((3, 3, piece, 128), f32),
            pltpu.VMEM((3, piece, 128), f32),
            pltpu.VMEM((3, 4, piece, 128), f32),
            pltpu.SemaphoreType.DMA((47,)),
            pltpu.SemaphoreType.DMA((47,)),
        ],
        compiler_params=pltpu.CompilerParams(collective_id=0, has_side_effects=True),
    )(flat)
    return out_a.reshape(sums_a.shape), out_b.reshape(sums_b.shape)


def conv_cells(field, kernel):
    shaped = kernel.reshape(3, 3, 3, kernel.shape[1], kernel.shape[2])
    result = lax.conv_general_dilated(
        field[None],
        shaped,
        (1, 1, 1),
        ((0, 0), (1, 1), (1, 1)),
        dimension_numbers=("NCDHW", "DHWIO", "NCDHW"),
        preferred_element_type=jnp.float32,
    )
    return result[0]


def back_cells(padded, kernel):
    flipped = kernel[::-1].transpose(0, 2, 1)
    return conv_cells(padded, flipped)


def kernel_terms(padded, upstream):
    chan_in, chan_out = padded.shape[0], upstream.shape[0]
    depth, rows, cols = upstream.shape[1:]
    wider = jnp.pad(padded, ((0, 0), (0, 0), (1, 1), (1, 1)))
    windows = jnp.stack(
        [
            wider[:, a : a + depth, b : b + rows, c : c + cols]
            for a in range(3)
            for b in range(3)
            for c in range(3)
        ]
    )
    cells = depth * rows * cols
    sums = lax.dot_general(
        windows.reshape(27 * chan_in, cells),
        upstream.reshape(chan_out, cells),
        (((1,), (1,)), ((), ())),
        preferred_element_type=jnp.float32,
    )
    return sums.reshape(27, chan_in, chan_out)


def per_device(layer_input, hidden_pre, output_pre, output_grad, weight_a, weight_b):
    side = math.isqrt(layer_input.shape[3])
    half = side // 2
    depth_a = layer_input.shape[2]
    depth_b = depth_a // 2
    source = layer_input[0]
    hidden = hidden_pre[0]
    outer = output_pre[0]
    upstream = output_grad[0]
    chan_in = source.shape[0]
    width_a = hidden.shape[0]
    width_b = outer.shape[0]
    grad_outer = (upstream.astype(jnp.float32) * slopes(outer.astype(jnp.float32))).astype(
        jnp.bfloat16
    )
    hidden_f = hidden.astype(jnp.float32)
    active = jnp.where(hidden_f > 0, hidden_f, negative_slope * hidden_f)
    pooled = (
        active.reshape(width_a, depth_b, 2, half, 2, half, 2)
        .mean(axis=(2, 4, 6))
        .astype(jnp.bfloat16)
    )
    pooled = pooled.reshape(width_a, depth_b, half * half)
    outer_pad = padded_2(grad_outer, (("space", 1),), 1).reshape(width_b, depth_b + 2, half, half)
    pooled_pad = padded_2(pooled, (("space", 1),), 1).reshape(width_a, depth_b + 2, half, half)
    back_b = back_cells(outer_pad, weight_b)
    sums_b = kernel_terms(pooled_pad, grad_outer.reshape(width_b, depth_b, half, half))
    upward = jnp.repeat(jnp.repeat(jnp.repeat(back_b, 2, 1), 2, 2), 2, 3) * 0.125
    upward = upward.reshape(width_a, depth_a * side * side)
    grad_hidden = (upward * slopes(hidden_f.reshape(width_a, depth_a * side * side))).astype(
        jnp.bfloat16
    )
    grad_hidden = grad_hidden.reshape(width_a, depth_a, side * side)
    hidden_pad = padded_2(grad_hidden, (("space", 1),), 1).reshape(width_a, depth_a + 2, side, side)
    source_pad = padded_2(source, (("space", 1),), 1).reshape(chan_in, depth_a + 2, side, side)
    back_a = back_cells(hidden_pad, weight_a)
    sums_a = kernel_terms(source_pad, grad_hidden.reshape(width_a, depth_a, side, side))
    input_grad = back_a.astype(jnp.bfloat16).reshape(1, chan_in, depth_a, side * side)
    samples = lax.axis_size("dp")
    planes_a = depth_a * lax.axis_size("space")
    scale_a = 1.0 / math.sqrt(samples * planes_a * side * side)
    scale_b = 1.0 / math.sqrt(samples * (planes_a // 2) * half * half)
    total_a, total_b = all_reduce(sums_a, sums_b, scale_a, scale_b)
    return (input_grad, total_a, total_b)


def solution(mesh):
    in_specs = (
        P("dp", None, "space", None),
        P("dp", None, "space", None),
        P("dp", None, "space", None),
        P("dp", None, "space", None),
        P(),
        P(),
    )
    out_specs = (P("dp", None, "space", None), P(), P())
    return jax.shard_map(
        per_device, mesh=mesh, in_specs=in_specs, out_specs=out_specs, check_vma=False
    )
```

```python
import math

import jax
import jax.numpy as jnp
from jax import lax
from jax.sharding import PartitionSpec as P
from jax.experimental import pallas as pl
from jax.experimental.pallas import tpu as pltpu

negative_slope = 0.3


def padded_2(cells, sides, width):
    for axis, dim in sides:
        count = lax.axis_size(axis)
        ends = count - 1
        head = lax.slice_in_dim(cells, 0, width, axis=dim)
        tail = lax.slice_in_dim(cells, cells.shape[dim] - width, cells.shape[dim], axis=dim)
        cells = jnp.concatenate(
            [
                lax.ppermute(tail, axis, [(i, (i + 1) % count) for i in range(ends)]),
                cells,
                lax.ppermute(head, axis, [((i + 1) % count, i) for i in range(ends)]),
            ],
            axis=dim,
        )
    return cells


def slopes(values):
    return jnp.where(values > 0, jnp.ones_like(values), negative_slope * jnp.ones_like(values))


def window(padded, tap_z, tap_y, tap_x, depth, side):
    planes = padded[:, tap_z : tap_z + depth, :]
    margin = side + 1
    wider = jnp.pad(planes, ((0, 0), (0, 0), (margin, margin)))
    offset = (tap_y - 1) * side + (tap_x - 1)
    piece = wider[:, :, margin + offset : margin + offset + side * side]
    column = jnp.arange(side * side, dtype=jnp.int32) % side + (tap_x - 1)
    inside = (column >= 0) & (column < side)
    piece = jnp.where(inside, piece, jnp.zeros_like(piece))
    return piece.reshape(padded.shape[0], depth * side * side)


def outer_product(left, right):
    return lax.dot_general(
        left, right, (((1,), (1,)), ((), ())), preferred_element_type=jnp.float32
    )


def _all_reduce_kernel(x_ref, o_a, o_b, full, recv_a, acc_a, recv_1, acc_1, recv_2, acc_2, recv_3, sends, recvs):
    rows = x_ref.shape[0]
    half = rows // 2
    part = half // 3
    quarter, piece = part // 4, part // 16
    mesh_id = pl.DeviceIdType.MESH
    dp = lax.axis_index("dp")
    sp = lax.axis_index("space")
    core = dp % 2
    spot = {"x": dp // 2, "y": sp // 4, "z": sp % 4}
    partner = (spot["x"] * 2 + (1 - core), sp)

    def peer(axis, k):
        moved = dict(spot)
        moved[axis] = (spot[axis] + k) % 4
        return (moved["x"] * 2 + core, moved["y"] * 4 + moved["z"])

    orders = (("x", "y", "z"), ("y", "z", "x"), ("z", "x", "y"))
    peers = [partner] + [peer(axis, k) for axis in "xyz" for k in (1, 2, 3)]
    barrier = pltpu.get_barrier_semaphore()
    for other in peers:
        pl.semaphore_signal(barrier, inc=1, device_id=other, device_id_type=mesh_id)
    pl.semaphore_wait(barrier, len(peers))

    def rows_at(start, size):
        return pl.ds(pl.multiple_of(start, 16), size)

    used = [0]

    def exchange(triples):
        copies = []
        for src, dst, other in triples:
            copy = pltpu.make_async_remote_copy(
                src_ref=src,
                dst_ref=dst,
                send_sem=sends.at[used[0]],
                recv_sem=recvs.at[used[0]],
                device_id=other,
                device_id_type=mesh_id,
            )
            used[0] += 1
            copy.start()
            copies.append(copy)
        for copy in copies:
            copy.wait()

    exchange([(x_ref.at[rows_at((1 - core) * half, half)], recv_a, partner)])
    acc_a[...] = x_ref[rows_at(core * half, half), :] + recv_a[...]
    triples = []
    for p, order in enumerate(orders):
        for k in (1, 2, 3):
            block = p * part + ((spot[order[0]] + k) % 4) * quarter
            triples.append((acc_a.at[rows_at(block, quarter)], recv_1.at[p, k - 1], peer(order[0], k)))
    exchange(triples)
    for p, order in enumerate(orders):
        mine = p * part + spot[order[0]] * quarter
        acc_1[p] = acc_a[rows_at(mine, quarter), :] + recv_1[p, 0] + recv_1[p, 1] + recv_1[p, 2]
    triples = []
    for p, order in enumerate(orders):
        for k in (1, 2, 3):
            block = ((spot[order[1]] + k) % 4) * piece
            triples.append((acc_1.at[p, rows_at(block, piece)], recv_2.at[p, k - 1], peer(order[1], k)))
    exchange(triples)
    for p, order in enumerate(orders):
        mine = spot[order[1]] * piece
        recv_3[p, 0] = acc_1[p, rows_at(mine, piece), :] + recv_2[p, 0] + recv_2[p, 1] + recv_2[p, 2]
    exchange([(recv_3.at[p, 0], recv_3.at[p, k], peer(order[2], k)) for p, order in enumerate(orders) for k in (1, 2, 3)])
    spans = []
    for p, order in enumerate(orders):
        last = spot[order[2]]
        total = recv_3[p, last % 4]
        for j in (1, 2, 3):
            total = total + recv_3[p, (last - j + 4) % 4]
        outer = core * half + p * part + spot[order[0]] * quarter
        own = outer + spot[order[1]] * piece
        full[rows_at(own, piece), :] = total.astype(full.dtype)
        spans.append((outer, own, order))
    exchange([(full.at[rows_at(own, piece)], full.at[rows_at(own, piece)], peer(order[1], k)) for outer, own, order in spans for k in (1, 2, 3)])
    exchange([(full.at[rows_at(outer, quarter)], full.at[rows_at(outer, quarter)], peer(order[0], k)) for outer, own, order in spans for k in (1, 2, 3)])
    block = full.at[rows_at(core * half, half)]
    exchange([(block, block, partner)])
    rows_a, rows_b = o_a.shape[0], o_b.shape[0]
    o_a[...] = full[0:rows_a, :].astype(jnp.float32)
    o_b[:, 0:128] = full[rows_a : rows_a + rows_b, :].astype(jnp.float32)
    o_b[:, 128:256] = full[rows_a + rows_b : rows_a + 2 * rows_b, :].astype(jnp.float32)


def all_reduce(sums_a, sums_b, scale_a, scale_b):
    rows_a = sums_a.shape[0] * sums_a.shape[1]
    rows_b = sums_b.shape[0] * sums_b.shape[1]
    wide = sums_b.reshape(rows_b, 256) * scale_b
    flat = jnp.concatenate([sums_a.reshape(rows_a, 128) * scale_a, wide[:, :128], wide[:, 128:]])
    count = flat.shape[0]
    unit = 6 * 16 * 16
    rows = -(-count // unit) * unit
    flat = jnp.pad(flat, ((0, rows - count), (0, 0)))
    half = rows // 2
    part = half // 3
    quarter, piece = part // 4, part // 16
    f32 = jnp.float32
    out_a, out_b = pl.pallas_call(
        _all_reduce_kernel,
        out_shape=(jax.ShapeDtypeStruct((rows_a, 128), f32), jax.ShapeDtypeStruct((rows_b, 256), f32)),
        in_specs=[pl.BlockSpec(memory_space=pltpu.VMEM)],
        out_specs=(pl.BlockSpec(memory_space=pltpu.VMEM), pl.BlockSpec(memory_space=pltpu.VMEM)),
        scratch_shapes=[
            pltpu.VMEM((rows, 128), jnp.bfloat16),
            pltpu.VMEM((half, 128), f32),
            pltpu.VMEM((half, 128), f32),
            pltpu.VMEM((3, 3, quarter, 128), f32),
            pltpu.VMEM((3, quarter, 128), f32),
            pltpu.VMEM((3, 3, piece, 128), f32),
            pltpu.VMEM((3, piece, 128), f32),
            pltpu.VMEM((3, 4, piece, 128), f32),
            pltpu.SemaphoreType.DMA((47,)),
            pltpu.SemaphoreType.DMA((47,)),
        ],
        compiler_params=pltpu.CompilerParams(collective_id=0, has_side_effects=True),
    )(flat)
    return out_a.reshape(sums_a.shape), out_b.reshape(sums_b.shape)


def conv_cells(field, kernel):
    shaped = kernel.reshape(3, 3, 3, kernel.shape[1], kernel.shape[2])
    result = lax.conv_general_dilated(
        field[None],
        shaped,
        (1, 1, 1),
        ((0, 0), (1, 1), (1, 1)),
        dimension_numbers=("NCDHW", "DHWIO", "NCDHW"),
        preferred_element_type=jnp.float32,
    )
    return result[0]


def back_cells(padded, kernel):
    flipped = kernel[::-1].transpose(0, 2, 1)
    return conv_cells(padded, flipped)


def kernel_terms(padded, upstream):
    taps, chan_in, chan_out = 27, padded.shape[0], upstream.shape[0]
    start = jnp.zeros((taps, chan_in, chan_out), jnp.float32)
    field = padded.astype(jnp.float32)
    unused, pull = jax.vjp(lambda w: conv_cells(field, w), start)
    return pull(upstream.astype(jnp.float32))[0]


def per_device(layer_input, hidden_pre, output_pre, output_grad, weight_a, weight_b):
    side = math.isqrt(layer_input.shape[3])
    half = side // 2
    depth_a = layer_input.shape[2]
    depth_b = depth_a // 2
    source = layer_input[0]
    hidden = hidden_pre[0]
    outer = output_pre[0]
    upstream = output_grad[0]
    chan_in = source.shape[0]
    width_a = hidden.shape[0]
    width_b = outer.shape[0]
    grad_outer = (upstream.astype(jnp.float32) * slopes(outer.astype(jnp.float32))).astype(
        jnp.bfloat16
    )
    hidden_f = hidden.astype(jnp.float32)
    active = jnp.where(hidden_f > 0, hidden_f, negative_slope * hidden_f)
    pooled = (
        active.reshape(width_a, depth_b, 2, half, 2, half, 2)
        .mean(axis=(2, 4, 6))
        .astype(jnp.bfloat16)
    )
    pooled = pooled.reshape(width_a, depth_b, half * half)
    outer_pad = padded_2(grad_outer, (("space", 1),), 1).reshape(width_b, depth_b + 2, half, half)
    pooled_pad = padded_2(pooled, (("space", 1),), 1).reshape(width_a, depth_b + 2, half, half)
    back_b = back_cells(outer_pad, weight_b)
    sums_b = kernel_terms(pooled_pad, grad_outer.reshape(width_b, depth_b, half, half))
    upward = jnp.repeat(jnp.repeat(jnp.repeat(back_b, 2, 1), 2, 2), 2, 3) * 0.125
    upward = upward.reshape(width_a, depth_a * side * side)
    grad_hidden = (upward * slopes(hidden_f.reshape(width_a, depth_a * side * side))).astype(
        jnp.bfloat16
    )
    grad_hidden = grad_hidden.reshape(width_a, depth_a, side * side)
    hidden_pad = padded_2(grad_hidden, (("space", 1),), 1).reshape(width_a, depth_a + 2, side, side)
    source_pad = padded_2(source, (("space", 1),), 1).reshape(chan_in, depth_a + 2, side, side)
    back_a = back_cells(hidden_pad, weight_a)
    sums_a = kernel_terms(source_pad, grad_hidden.reshape(width_a, depth_a, side, side))
    input_grad = back_a.astype(jnp.bfloat16).reshape(1, chan_in, depth_a, side * side)
    samples = lax.axis_size("dp")
    planes_a = depth_a * lax.axis_size("space")
    scale_a = 1.0 / math.sqrt(samples * planes_a * side * side)
    scale_b = 1.0 / math.sqrt(samples * (planes_a // 2) * half * half)
    total_a, total_b = all_reduce(sums_a, sums_b, scale_a, scale_b)
    return (input_grad, total_a, total_b)


def solution(mesh):
    in_specs = (
        P("dp", None, "space", None),
        P("dp", None, "space", None),
        P("dp", None, "space", None),
        P("dp", None, "space", None),
        P(),
        P(),
    )
    out_specs = (P("dp", None, "space", None), P(), P())
    return jax.shard_map(
        per_device, mesh=mesh, in_specs=in_specs, out_specs=out_specs, check_vma=False
    )
```

```python
import math

import jax
import jax.numpy as jnp
from jax import lax
from jax.sharding import PartitionSpec as P
from jax.experimental import pallas as pl
from jax.experimental.pallas import tpu as pltpu

negative_slope = 0.3


def padded_2(cells, sides, width):
    for axis, dim in sides:
        count = lax.axis_size(axis)
        ends = count - 1
        head = lax.slice_in_dim(cells, 0, width, axis=dim)
        tail = lax.slice_in_dim(cells, cells.shape[dim] - width, cells.shape[dim], axis=dim)
        cells = jnp.concatenate(
            [
                lax.ppermute(tail, axis, [(i, (i + 1) % count) for i in range(ends)]),
                cells,
                lax.ppermute(head, axis, [((i + 1) % count, i) for i in range(ends)]),
            ],
            axis=dim,
        )
    return cells


def slopes(values):
    return jnp.where(values > 0, jnp.ones_like(values), negative_slope * jnp.ones_like(values))


def window(padded, tap_z, tap_y, tap_x, depth, side):
    planes = padded[:, tap_z : tap_z + depth, :]
    margin = side + 1
    wider = jnp.pad(planes, ((0, 0), (0, 0), (margin, margin)))
    offset = (tap_y - 1) * side + (tap_x - 1)
    piece = wider[:, :, margin + offset : margin + offset + side * side]
    column = jnp.arange(side * side, dtype=jnp.int32) % side + (tap_x - 1)
    inside = (column >= 0) & (column < side)
    piece = jnp.where(inside, piece, jnp.zeros_like(piece))
    return piece.reshape(padded.shape[0], depth * side * side)


def outer_product(left, right):
    return lax.dot_general(
        left, right, (((1,), (1,)), ((), ())), preferred_element_type=jnp.float32
    )


def _all_reduce_kernel(x_ref, o_a, o_b, full, recv_a, acc_a, recv_1, acc_1, recv_2, acc_2, recv_3, sends, recvs):
    rows = x_ref.shape[0]
    half = rows // 2
    part = half // 3
    quarter, piece = part // 4, part // 16
    mesh_id = pl.DeviceIdType.MESH
    dp = lax.axis_index("dp")
    sp = lax.axis_index("space")
    core = dp % 2
    spot = {"x": dp // 2, "y": sp // 4, "z": sp % 4}
    partner = (spot["x"] * 2 + (1 - core), sp)

    def peer(axis, k):
        moved = dict(spot)
        moved[axis] = (spot[axis] + k) % 4
        return (moved["x"] * 2 + core, moved["y"] * 4 + moved["z"])

    orders = (("x", "y", "z"), ("y", "z", "x"), ("z", "x", "y"))
    peers = [partner] + [peer(axis, k) for axis in "xyz" for k in (1, 2, 3)]
    barrier = pltpu.get_barrier_semaphore()
    for other in peers:
        pl.semaphore_signal(barrier, inc=1, device_id=other, device_id_type=mesh_id)
    pl.semaphore_wait(barrier, len(peers))

    def rows_at(start, size):
        return pl.ds(pl.multiple_of(start, 16), size)

    used = [0]

    def exchange(triples):
        copies = []
        for src, dst, other in triples:
            copy = pltpu.make_async_remote_copy(
                src_ref=src,
                dst_ref=dst,
                send_sem=sends.at[used[0]],
                recv_sem=recvs.at[used[0]],
                device_id=other,
                device_id_type=mesh_id,
            )
            used[0] += 1
            copy.start()
            copies.append(copy)
        for copy in copies:
            copy.wait()

    exchange([(x_ref.at[rows_at((1 - core) * half, half)], recv_a, partner)])
    acc_a[...] = x_ref[rows_at(core * half, half), :] + recv_a[...]
    triples = []
    for p, order in enumerate(orders):
        for k in (1, 2, 3):
            block = p * part + ((spot[order[0]] + k) % 4) * quarter
            triples.append((acc_a.at[rows_at(block, quarter)], recv_1.at[p, k - 1], peer(order[0], k)))
    exchange(triples)
    for p, order in enumerate(orders):
        mine = p * part + spot[order[0]] * quarter
        acc_1[p] = acc_a[rows_at(mine, quarter), :] + recv_1[p, 0] + recv_1[p, 1] + recv_1[p, 2]
    triples = []
    for p, order in enumerate(orders):
        for k in (1, 2, 3):
            block = ((spot[order[1]] + k) % 4) * piece
            triples.append((acc_1.at[p, rows_at(block, piece)], recv_2.at[p, k - 1], peer(order[1], k)))
    exchange(triples)
    for p, order in enumerate(orders):
        mine = spot[order[1]] * piece
        recv_3[p, 0] = acc_1[p, rows_at(mine, piece), :] + recv_2[p, 0] + recv_2[p, 1] + recv_2[p, 2]
    exchange([(recv_3.at[p, 0], recv_3.at[p, k], peer(order[2], k)) for p, order in enumerate(orders) for k in (1, 2, 3)])
    spans = []
    for p, order in enumerate(orders):
        last = spot[order[2]]
        total = recv_3[p, last % 4]
        for j in (1, 2, 3):
            total = total + recv_3[p, (last - j + 4) % 4]
        outer = core * half + p * part + spot[order[0]] * quarter
        own = outer + spot[order[1]] * piece
        full[rows_at(own, piece), :] = total.astype(full.dtype)
        spans.append((outer, own, order))
    exchange([(full.at[rows_at(own, piece)], full.at[rows_at(own, piece)], peer(order[1], k)) for outer, own, order in spans for k in (1, 2, 3)])
    exchange([(full.at[rows_at(outer, quarter)], full.at[rows_at(outer, quarter)], peer(order[0], k)) for outer, own, order in spans for k in (1, 2, 3)])
    block = full.at[rows_at(core * half, half)]
    exchange([(block, block, partner)])
    rows_a, rows_b = o_a.shape[0], o_b.shape[0]
    o_a[...] = full[0:rows_a, :].astype(jnp.float32)
    o_b[:, 0:128] = full[rows_a : rows_a + rows_b, :].astype(jnp.float32)
    o_b[:, 128:256] = full[rows_a + rows_b : rows_a + 2 * rows_b, :].astype(jnp.float32)


def all_reduce(sums_a, sums_b, scale_a, scale_b):
    rows_a = sums_a.shape[0] * sums_a.shape[1]
    rows_b = sums_b.shape[0] * sums_b.shape[1]
    wide = sums_b.reshape(rows_b, 256) * scale_b
    flat = jnp.concatenate([sums_a.reshape(rows_a, 128) * scale_a, wide[:, :128], wide[:, 128:]])
    count = flat.shape[0]
    unit = 6 * 16 * 16
    rows = -(-count // unit) * unit
    flat = jnp.pad(flat, ((0, rows - count), (0, 0)))
    half = rows // 2
    part = half // 3
    quarter, piece = part // 4, part // 16
    f32 = jnp.float32
    out_a, out_b = pl.pallas_call(
        _all_reduce_kernel,
        out_shape=(jax.ShapeDtypeStruct((rows_a, 128), f32), jax.ShapeDtypeStruct((rows_b, 256), f32)),
        in_specs=[pl.BlockSpec(memory_space=pltpu.VMEM)],
        out_specs=(pl.BlockSpec(memory_space=pltpu.VMEM), pl.BlockSpec(memory_space=pltpu.VMEM)),
        scratch_shapes=[
            pltpu.VMEM((rows, 128), jnp.bfloat16),
            pltpu.VMEM((half, 128), f32),
            pltpu.VMEM((half, 128), f32),
            pltpu.VMEM((3, 3, quarter, 128), f32),
            pltpu.VMEM((3, quarter, 128), f32),
            pltpu.VMEM((3, 3, piece, 128), f32),
            pltpu.VMEM((3, piece, 128), f32),
            pltpu.VMEM((3, 4, piece, 128), f32),
            pltpu.SemaphoreType.DMA((47,)),
            pltpu.SemaphoreType.DMA((47,)),
        ],
        compiler_params=pltpu.CompilerParams(collective_id=0, has_side_effects=True),
    )(flat)
    return out_a.reshape(sums_a.shape), out_b.reshape(sums_b.shape)


def conv_cells(field, kernel):
    shaped = kernel.reshape(3, 3, 3, kernel.shape[1], kernel.shape[2])
    result = lax.conv_general_dilated(
        field[None],
        shaped,
        (1, 1, 1),
        ((0, 0), (1, 1), (1, 1)),
        dimension_numbers=("NCDHW", "DHWIO", "NCDHW"),
        preferred_element_type=jnp.float32,
    )
    return result[0]


def back_cells(padded, kernel):
    flipped = kernel[::-1].transpose(0, 2, 1)
    return conv_cells(padded, flipped)


def kernel_terms(padded, upstream):
    taps, chan_in, chan_out = 27, padded.shape[0], upstream.shape[0]
    start = jnp.zeros((taps, chan_in, chan_out), jnp.float32)
    field = padded.astype(jnp.float32)
    unused, pull = jax.vjp(lambda w: conv_cells(field, w), start)
    return pull(upstream.astype(jnp.float32))[0]


def _kernel_terms_body(src_ref, up_ref, out_ref):
    cells = up_ref.shape[1]
    width = src_ref.shape[1]
    margin = 128
    plane = 1024
    side = 32
    spot = lax.broadcasted_iota(jnp.int32, (1, cells), 1)
    column = spot % side
    row = (spot // side) % side
    upstream = up_ref[...]
    for b in range(3):
        for c in range(3):
            shift = (b - 1) * side + (c - 1)
            moved = pltpu.roll(src_ref[...], (width - shift) % width, 1)
            inside = (column + c - 1 >= 0) & (column + c - 1 < side) & (row + b - 1 >= 0) & (row + b - 1 < side)
            for a in range(3):
                window = moved[:, margin + a * plane : margin + a * plane + cells]
                window = jnp.where(inside, window, 0.0).astype(jnp.bfloat16)
                out_ref[9 * a + 3 * b + c] = lax.dot_general(
                    window, upstream, (((1,), (1,)), ((), ())), preferred_element_type=jnp.float32
                )


def kernel_terms_flat(padded, upstream):
    chan_in, chan_out = padded.shape[0], upstream.shape[0]
    field = jnp.pad(padded.reshape(chan_in, -1).astype(jnp.float32), ((0, 0), (128, 128)))
    return pl.pallas_call(
        _kernel_terms_body,
        out_shape=jax.ShapeDtypeStruct((27, chan_in, chan_out), jnp.float32),
        in_specs=[pl.BlockSpec(memory_space=pltpu.VMEM)] * 2,
        out_specs=pl.BlockSpec(memory_space=pltpu.VMEM),
    )(field, upstream.reshape(chan_out, -1))


def per_device(layer_input, hidden_pre, output_pre, output_grad, weight_a, weight_b):
    side = math.isqrt(layer_input.shape[3])
    half = side // 2
    depth_a = layer_input.shape[2]
    depth_b = depth_a // 2
    source = layer_input[0]
    hidden = hidden_pre[0]
    outer = output_pre[0]
    upstream = output_grad[0]
    chan_in = source.shape[0]
    width_a = hidden.shape[0]
    width_b = outer.shape[0]
    grad_outer = (upstream.astype(jnp.float32) * slopes(outer.astype(jnp.float32))).astype(
        jnp.bfloat16
    )
    hidden_f = hidden.astype(jnp.float32)
    active = jnp.where(hidden_f > 0, hidden_f, negative_slope * hidden_f)
    pooled = (
        active.reshape(width_a, depth_b, 2, half, 2, half, 2)
        .mean(axis=(2, 4, 6))
        .astype(jnp.bfloat16)
    )
    pooled = pooled.reshape(width_a, depth_b, half * half)
    outer_pad = padded_2(grad_outer, (("space", 1),), 1).reshape(width_b, depth_b + 2, half, half)
    pooled_pad = padded_2(pooled, (("space", 1),), 1).reshape(width_a, depth_b + 2, half, half)
    back_b = back_cells(outer_pad, weight_b)
    sums_b = kernel_terms(pooled_pad, grad_outer.reshape(width_b, depth_b, half, half))
    upward = jnp.repeat(jnp.repeat(jnp.repeat(back_b, 2, 1), 2, 2), 2, 3) * 0.125
    upward = upward.reshape(width_a, depth_a * side * side)
    grad_hidden = (upward * slopes(hidden_f.reshape(width_a, depth_a * side * side))).astype(
        jnp.bfloat16
    )
    grad_hidden = grad_hidden.reshape(width_a, depth_a, side * side)
    hidden_pad = padded_2(grad_hidden, (("space", 1),), 1).reshape(width_a, depth_a + 2, side, side)
    source_pad = padded_2(source, (("space", 1),), 1).reshape(chan_in, depth_a + 2, side, side)
    back_a = back_cells(hidden_pad, weight_a)
    sums_a = kernel_terms_flat(source_pad, grad_hidden)
    input_grad = back_a.astype(jnp.bfloat16).reshape(1, chan_in, depth_a, side * side)
    samples = lax.axis_size("dp")
    planes_a = depth_a * lax.axis_size("space")
    scale_a = 1.0 / math.sqrt(samples * planes_a * side * side)
    scale_b = 1.0 / math.sqrt(samples * (planes_a // 2) * half * half)
    total_a, total_b = all_reduce(sums_a, sums_b, scale_a, scale_b)
    return (input_grad, total_a, total_b)


def solution(mesh):
    in_specs = (
        P("dp", None, "space", None),
        P("dp", None, "space", None),
        P("dp", None, "space", None),
        P("dp", None, "space", None),
        P(),
        P(),
    )
    out_specs = (P("dp", None, "space", None), P(), P())
    return jax.shard_map(
        per_device, mesh=mesh, in_specs=in_specs, out_specs=out_specs, check_vma=False
    )
```

```python
import math

import jax
import jax.numpy as jnp
from jax import lax
from jax.sharding import PartitionSpec as P
from jax.experimental import pallas as pl
from jax.experimental.pallas import tpu as pltpu

negative_slope = 0.3


def padded_2(cells, sides, width):
    for axis, dim in sides:
        count = lax.axis_size(axis)
        ends = count - 1
        head = lax.slice_in_dim(cells, 0, width, axis=dim)
        tail = lax.slice_in_dim(cells, cells.shape[dim] - width, cells.shape[dim], axis=dim)
        cells = jnp.concatenate(
            [
                lax.ppermute(tail, axis, [(i, (i + 1) % count) for i in range(ends)]),
                cells,
                lax.ppermute(head, axis, [((i + 1) % count, i) for i in range(ends)]),
            ],
            axis=dim,
        )
    return cells


def slopes(values):
    return jnp.where(values > 0, jnp.ones_like(values), negative_slope * jnp.ones_like(values))


def window(padded, tap_z, tap_y, tap_x, depth, side):
    planes = padded[:, tap_z : tap_z + depth, :]
    margin = side + 1
    wider = jnp.pad(planes, ((0, 0), (0, 0), (margin, margin)))
    offset = (tap_y - 1) * side + (tap_x - 1)
    piece = wider[:, :, margin + offset : margin + offset + side * side]
    column = jnp.arange(side * side, dtype=jnp.int32) % side + (tap_x - 1)
    inside = (column >= 0) & (column < side)
    piece = jnp.where(inside, piece, jnp.zeros_like(piece))
    return piece.reshape(padded.shape[0], depth * side * side)


def outer_product(left, right):
    return lax.dot_general(
        left, right, (((1,), (1,)), ((), ())), preferred_element_type=jnp.float32
    )


def _all_reduce_kernel(x_ref, o_a, o_b, full, recv_a, acc_a, recv_1, acc_1, recv_2, acc_2, recv_3, sends, recvs):
    rows = x_ref.shape[0]
    half = rows // 2
    part = half // 3
    quarter, piece = part // 4, part // 16
    mesh_id = pl.DeviceIdType.MESH
    dp = lax.axis_index("dp")
    sp = lax.axis_index("space")
    core = dp % 2
    spot = {"x": dp // 2, "y": sp // 4, "z": sp % 4}
    partner = (spot["x"] * 2 + (1 - core), sp)

    def peer(axis, k):
        moved = dict(spot)
        moved[axis] = (spot[axis] + k) % 4
        return (moved["x"] * 2 + core, moved["y"] * 4 + moved["z"])

    orders = (("x", "y", "z"), ("y", "z", "x"), ("z", "x", "y"))
    peers = [partner] + [peer(axis, k) for axis in "xyz" for k in (1, 2, 3)]
    barrier = pltpu.get_barrier_semaphore()
    for other in peers:
        pl.semaphore_signal(barrier, inc=1, device_id=other, device_id_type=mesh_id)
    pl.semaphore_wait(barrier, len(peers))

    def rows_at(start, size):
        return pl.ds(pl.multiple_of(start, 16), size)

    used = [0]

    def exchange(triples):
        copies = []
        for src, dst, other in triples:
            copy = pltpu.make_async_remote_copy(
                src_ref=src,
                dst_ref=dst,
                send_sem=sends.at[used[0]],
                recv_sem=recvs.at[used[0]],
                device_id=other,
                device_id_type=mesh_id,
            )
            used[0] += 1
            copy.start()
            copies.append(copy)
        for copy in copies:
            copy.wait()

    exchange([(x_ref.at[rows_at((1 - core) * half, half)], recv_a, partner)])
    acc_a[...] = x_ref[rows_at(core * half, half), :] + recv_a[...]
    triples = []
    for p, order in enumerate(orders):
        for k in (1, 2, 3):
            block = p * part + ((spot[order[0]] + k) % 4) * quarter
            triples.append((acc_a.at[rows_at(block, quarter)], recv_1.at[p, k - 1], peer(order[0], k)))
    exchange(triples)
    for p, order in enumerate(orders):
        mine = p * part + spot[order[0]] * quarter
        acc_1[p] = acc_a[rows_at(mine, quarter), :] + recv_1[p, 0] + recv_1[p, 1] + recv_1[p, 2]
    triples = []
    for p, order in enumerate(orders):
        for k in (1, 2, 3):
            block = ((spot[order[1]] + k) % 4) * piece
            triples.append((acc_1.at[p, rows_at(block, piece)], recv_2.at[p, k - 1], peer(order[1], k)))
    exchange(triples)
    for p, order in enumerate(orders):
        mine = spot[order[1]] * piece
        recv_3[p, 0] = acc_1[p, rows_at(mine, piece), :] + recv_2[p, 0] + recv_2[p, 1] + recv_2[p, 2]
    exchange([(recv_3.at[p, 0], recv_3.at[p, k], peer(order[2], k)) for p, order in enumerate(orders) for k in (1, 2, 3)])
    spans = []
    for p, order in enumerate(orders):
        last = spot[order[2]]
        total = recv_3[p, last % 4]
        for j in (1, 2, 3):
            total = total + recv_3[p, (last - j + 4) % 4]
        outer = core * half + p * part + spot[order[0]] * quarter
        own = outer + spot[order[1]] * piece
        full[rows_at(own, piece), :] = total.astype(full.dtype)
        spans.append((outer, own, order))
    exchange([(full.at[rows_at(own, piece)], full.at[rows_at(own, piece)], peer(order[1], k)) for outer, own, order in spans for k in (1, 2, 3)])
    exchange([(full.at[rows_at(outer, quarter)], full.at[rows_at(outer, quarter)], peer(order[0], k)) for outer, own, order in spans for k in (1, 2, 3)])
    block = full.at[rows_at(core * half, half)]
    exchange([(block, block, partner)])
    rows_a, rows_b = o_a.shape[0], o_b.shape[0]
    o_a[...] = full[0:rows_a, :].astype(jnp.float32)
    o_b[:, 0:128] = full[rows_a : rows_a + rows_b, :].astype(jnp.float32)
    o_b[:, 128:256] = full[rows_a + rows_b : rows_a + 2 * rows_b, :].astype(jnp.float32)


def all_reduce(sums_a, sums_b, scale_a, scale_b):
    rows_a = sums_a.shape[0] * sums_a.shape[1]
    rows_b = sums_b.shape[0] * sums_b.shape[1]
    wide = sums_b.reshape(rows_b, 256) * scale_b
    flat = jnp.concatenate([sums_a.reshape(rows_a, 128) * scale_a, wide[:, :128], wide[:, 128:]])
    count = flat.shape[0]
    unit = 6 * 16 * 16
    rows = -(-count // unit) * unit
    flat = jnp.pad(flat, ((0, rows - count), (0, 0)))
    half = rows // 2
    part = half // 3
    quarter, piece = part // 4, part // 16
    f32 = jnp.float32
    out_a, out_b = pl.pallas_call(
        _all_reduce_kernel,
        out_shape=(jax.ShapeDtypeStruct((rows_a, 128), f32), jax.ShapeDtypeStruct((rows_b, 256), f32)),
        in_specs=[pl.BlockSpec(memory_space=pltpu.VMEM)],
        out_specs=(pl.BlockSpec(memory_space=pltpu.VMEM), pl.BlockSpec(memory_space=pltpu.VMEM)),
        scratch_shapes=[
            pltpu.VMEM((rows, 128), jnp.bfloat16),
            pltpu.VMEM((half, 128), f32),
            pltpu.VMEM((half, 128), f32),
            pltpu.VMEM((3, 3, quarter, 128), f32),
            pltpu.VMEM((3, quarter, 128), f32),
            pltpu.VMEM((3, 3, piece, 128), f32),
            pltpu.VMEM((3, piece, 128), f32),
            pltpu.VMEM((3, 4, piece, 128), f32),
            pltpu.SemaphoreType.DMA((47,)),
            pltpu.SemaphoreType.DMA((47,)),
        ],
        compiler_params=pltpu.CompilerParams(collective_id=0, has_side_effects=True),
    )(flat)
    return out_a.reshape(sums_a.shape), out_b.reshape(sums_b.shape)


def conv_cells(field, kernel):
    shaped = kernel.reshape(3, 3, 3, kernel.shape[1], kernel.shape[2])
    result = lax.conv_general_dilated(
        field[None],
        shaped,
        (1, 1, 1),
        ((0, 0), (1, 1), (1, 1)),
        dimension_numbers=("NCDHW", "DHWIO", "NCDHW"),
        preferred_element_type=jnp.float32,
    )
    return result[0]


def back_cells(padded, kernel):
    flipped = kernel[::-1].transpose(0, 2, 1)
    return conv_cells(padded, flipped)


def kernel_terms(padded, upstream):
    taps, chan_in, chan_out = 27, padded.shape[0], upstream.shape[0]
    start = jnp.zeros((taps, chan_in, chan_out), jnp.float32)
    field = padded.astype(jnp.float32)
    unused, pull = jax.vjp(lambda w: conv_cells(field, w), start)
    return pull(upstream.astype(jnp.float32))[0]


def _layer_a_body(src_ref, up_ref, pad_ref, w_ref, terms_ref, back_ref):
    cells = up_ref.shape[1]
    width = src_ref.shape[1]
    plane = width // 4
    side = 32
    spot = lax.broadcasted_iota(jnp.int32, (1, cells), 1)
    column = spot % side
    row = (spot // side) % side
    upstream = up_ref[...]
    field = src_ref[...].astype(jnp.float32)
    back = jnp.zeros((back_ref.shape[0], cells), jnp.float32)
    for b in range(3):
        for c in range(3):
            shift = (b - 1) * side + (c - 1)
            moved = pltpu.roll(field, (width - shift) % width, 1)
            inside = (column + c - 1 >= 0) & (column + c - 1 < side) & (row + b - 1 >= 0) & (row + b - 1 < side)
            total = jnp.zeros_like(back)
            for a in range(3):
                tap = 9 * a + 3 * b + c
                window = moved[:, a * plane : a * plane + cells]
                window = jnp.where(inside, window, 0.0).astype(jnp.bfloat16)
                terms_ref[tap] = lax.dot_general(
                    window, upstream, (((1,), (1,)), ((), ())), preferred_element_type=jnp.float32
                )
                total = total + jnp.dot(
                    w_ref[tap], pad_ref[:, (2 - a) * plane : (2 - a) * plane + cells], preferred_element_type=jnp.float32
                )
            back_in = (column - c + 1 >= 0) & (column - c + 1 < side) & (row - b + 1 >= 0) & (row - b + 1 < side)
            back = back + jnp.where(back_in, pltpu.roll(total, shift % cells, 1), 0.0)
    back_ref[...] = back.astype(back_ref.dtype)


def layer_a_grads(source_pad, hidden_pad, grad_hidden, weight_a):
    chan_in, chan_out = source_pad.shape[0], grad_hidden.shape[0]
    cells = grad_hidden.shape[1] * grad_hidden.shape[2]
    return pl.pallas_call(
        _layer_a_body,
        out_shape=(
            jax.ShapeDtypeStruct((27, chan_in, chan_out), jnp.float32),
            jax.ShapeDtypeStruct((chan_in, cells), jnp.bfloat16),
        ),
        in_specs=[pl.BlockSpec(memory_space=pltpu.VMEM)] * 4,
        out_specs=(pl.BlockSpec(memory_space=pltpu.VMEM), pl.BlockSpec(memory_space=pltpu.VMEM)),
    )(source_pad.reshape(chan_in, -1), grad_hidden.reshape(chan_out, -1), hidden_pad.reshape(chan_out, -1), weight_a)


def per_device(layer_input, hidden_pre, output_pre, output_grad, weight_a, weight_b):
    side = math.isqrt(layer_input.shape[3])
    half = side // 2
    depth_a = layer_input.shape[2]
    depth_b = depth_a // 2
    source = layer_input[0]
    hidden = hidden_pre[0]
    outer = output_pre[0]
    upstream = output_grad[0]
    chan_in = source.shape[0]
    width_a = hidden.shape[0]
    width_b = outer.shape[0]
    grad_outer = (upstream.astype(jnp.float32) * slopes(outer.astype(jnp.float32))).astype(
        jnp.bfloat16
    )
    hidden_f = hidden.astype(jnp.float32)
    active = jnp.where(hidden_f > 0, hidden_f, negative_slope * hidden_f)
    pooled = (
        active.reshape(width_a, depth_b, 2, half, 2, half, 2)
        .mean(axis=(2, 4, 6))
        .astype(jnp.bfloat16)
    )
    pooled = pooled.reshape(width_a, depth_b, half * half)
    outer_pad = padded_2(grad_outer, (("space", 1),), 1).reshape(width_b, depth_b + 2, half, half)
    pooled_pad = padded_2(pooled, (("space", 1),), 1).reshape(width_a, depth_b + 2, half, half)
    back_b = back_cells(outer_pad, weight_b)
    sums_b = kernel_terms(pooled_pad, grad_outer.reshape(width_b, depth_b, half, half))
    upward = jnp.repeat(jnp.repeat(jnp.repeat(back_b, 2, 1), 2, 2), 2, 3) * 0.125
    upward = upward.reshape(width_a, depth_a * side * side)
    grad_hidden = (upward * slopes(hidden_f.reshape(width_a, depth_a * side * side))).astype(
        jnp.bfloat16
    )
    grad_hidden = grad_hidden.reshape(width_a, depth_a, side * side)
    hidden_pad = padded_2(grad_hidden, (("space", 1),), 1)
    source_pad = padded_2(source, (("space", 1),), 1)
    sums_a, back_a = layer_a_grads(source_pad, hidden_pad, grad_hidden, weight_a)
    input_grad = back_a.astype(jnp.bfloat16).reshape(1, chan_in, depth_a, side * side)
    samples = lax.axis_size("dp")
    planes_a = depth_a * lax.axis_size("space")
    scale_a = 1.0 / math.sqrt(samples * planes_a * side * side)
    scale_b = 1.0 / math.sqrt(samples * (planes_a // 2) * half * half)
    total_a, total_b = all_reduce(sums_a, sums_b, scale_a, scale_b)
    return (input_grad, total_a, total_b)


def solution(mesh):
    in_specs = (
        P("dp", None, "space", None),
        P("dp", None, "space", None),
        P("dp", None, "space", None),
        P("dp", None, "space", None),
        P(),
        P(),
    )
    out_specs = (P("dp", None, "space", None), P(), P())
    return jax.shard_map(
        per_device, mesh=mesh, in_specs=in_specs, out_specs=out_specs, check_vma=False
    )
```

```python
import math

import jax
import jax.numpy as jnp
from jax import lax
from jax.sharding import PartitionSpec as P
from jax.experimental import pallas as pl
from jax.experimental.pallas import tpu as pltpu

negative_slope = 0.3


def padded_2(cells, sides, width):
    for axis, dim in sides:
        count = lax.axis_size(axis)
        ends = count - 1
        head = lax.slice_in_dim(cells, 0, width, axis=dim)
        tail = lax.slice_in_dim(cells, cells.shape[dim] - width, cells.shape[dim], axis=dim)
        cells = jnp.concatenate(
            [
                lax.ppermute(tail, axis, [(i, (i + 1) % count) for i in range(ends)]),
                cells,
                lax.ppermute(head, axis, [((i + 1) % count, i) for i in range(ends)]),
            ],
            axis=dim,
        )
    return cells


def slopes(values):
    return jnp.where(values > 0, jnp.ones_like(values), negative_slope * jnp.ones_like(values))


def window(padded, tap_z, tap_y, tap_x, depth, side):
    planes = padded[:, tap_z : tap_z + depth, :]
    margin = side + 1
    wider = jnp.pad(planes, ((0, 0), (0, 0), (margin, margin)))
    offset = (tap_y - 1) * side + (tap_x - 1)
    piece = wider[:, :, margin + offset : margin + offset + side * side]
    column = jnp.arange(side * side, dtype=jnp.int32) % side + (tap_x - 1)
    inside = (column >= 0) & (column < side)
    piece = jnp.where(inside, piece, jnp.zeros_like(piece))
    return piece.reshape(padded.shape[0], depth * side * side)


def outer_product(left, right):
    return lax.dot_general(
        left, right, (((1,), (1,)), ((), ())), preferred_element_type=jnp.float32
    )


def _all_reduce_kernel(x_ref, o_a, o_b, full, recv_a, acc_a, recv_1, acc_1, recv_2, acc_2, recv_3, sends, recvs):
    rows = x_ref.shape[0]
    half = rows // 2
    part = half // 3
    quarter, piece = part // 4, part // 16
    mesh_id = pl.DeviceIdType.MESH
    dp = lax.axis_index("dp")
    sp = lax.axis_index("space")
    core = dp % 2
    spot = {"x": dp // 2, "y": sp // 4, "z": sp % 4}
    partner = (spot["x"] * 2 + (1 - core), sp)

    def peer(axis, k):
        moved = dict(spot)
        moved[axis] = (spot[axis] + k) % 4
        return (moved["x"] * 2 + core, moved["y"] * 4 + moved["z"])

    orders = (("x", "y", "z"), ("y", "z", "x"), ("z", "x", "y"))
    peers = [partner] + [peer(axis, k) for axis in "xyz" for k in (1, 2, 3)]
    barrier = pltpu.get_barrier_semaphore()
    for other in peers:
        pl.semaphore_signal(barrier, inc=1, device_id=other, device_id_type=mesh_id)
    pl.semaphore_wait(barrier, len(peers))

    def rows_at(start, size):
        return pl.ds(pl.multiple_of(start, 16), size)

    used = [0]

    def exchange(triples):
        copies = []
        for src, dst, other in triples:
            copy = pltpu.make_async_remote_copy(
                src_ref=src,
                dst_ref=dst,
                send_sem=sends.at[used[0]],
                recv_sem=recvs.at[used[0]],
                device_id=other,
                device_id_type=mesh_id,
            )
            used[0] += 1
            copy.start()
            copies.append(copy)
        for copy in copies:
            copy.wait()

    exchange([(x_ref.at[rows_at((1 - core) * half, half)], recv_a, partner)])
    acc_a[...] = x_ref[rows_at(core * half, half), :] + recv_a[...]
    triples = []
    for p, order in enumerate(orders):
        for k in (1, 2, 3):
            block = p * part + ((spot[order[0]] + k) % 4) * quarter
            triples.append((acc_a.at[rows_at(block, quarter)], recv_1.at[p, k - 1], peer(order[0], k)))
    exchange(triples)
    for p, order in enumerate(orders):
        mine = p * part + spot[order[0]] * quarter
        acc_1[p] = acc_a[rows_at(mine, quarter), :] + recv_1[p, 0] + recv_1[p, 1] + recv_1[p, 2]
    triples = []
    for p, order in enumerate(orders):
        for k in (1, 2, 3):
            block = ((spot[order[1]] + k) % 4) * piece
            triples.append((acc_1.at[p, rows_at(block, piece)], recv_2.at[p, k - 1], peer(order[1], k)))
    exchange(triples)
    for p, order in enumerate(orders):
        mine = spot[order[1]] * piece
        recv_3[p, 0] = acc_1[p, rows_at(mine, piece), :] + recv_2[p, 0] + recv_2[p, 1] + recv_2[p, 2]
    exchange([(recv_3.at[p, 0], recv_3.at[p, k], peer(order[2], k)) for p, order in enumerate(orders) for k in (1, 2, 3)])
    spans = []
    for p, order in enumerate(orders):
        last = spot[order[2]]
        total = recv_3[p, last % 4]
        for j in (1, 2, 3):
            total = total + recv_3[p, (last - j + 4) % 4]
        outer = core * half + p * part + spot[order[0]] * quarter
        own = outer + spot[order[1]] * piece
        full[rows_at(own, piece), :] = total.astype(full.dtype)
        spans.append((outer, own, order))
    exchange([(full.at[rows_at(own, piece)], full.at[rows_at(own, piece)], peer(order[1], k)) for outer, own, order in spans for k in (1, 2, 3)])
    exchange([(full.at[rows_at(outer, quarter)], full.at[rows_at(outer, quarter)], peer(order[0], k)) for outer, own, order in spans for k in (1, 2, 3)])
    block = full.at[rows_at(core * half, half)]
    exchange([(block, block, partner)])
    rows_a, rows_b = o_a.shape[0], o_b.shape[0]
    o_a[...] = full[0:rows_a, :].astype(jnp.float32)
    o_b[:, 0:128] = full[rows_a : rows_a + rows_b, :].astype(jnp.float32)
    o_b[:, 128:256] = full[rows_a + rows_b : rows_a + 2 * rows_b, :].astype(jnp.float32)


def all_reduce(sums_a, sums_b, scale_a, scale_b):
    rows_a = sums_a.shape[0] * sums_a.shape[1]
    rows_b = sums_b.shape[0] * sums_b.shape[1]
    wide = sums_b.reshape(rows_b, 256) * scale_b
    flat = jnp.concatenate([sums_a.reshape(rows_a, 128) * scale_a, wide[:, :128], wide[:, 128:]])
    count = flat.shape[0]
    unit = 6 * 16 * 16
    rows = -(-count // unit) * unit
    flat = jnp.pad(flat, ((0, rows - count), (0, 0)))
    half = rows // 2
    part = half // 3
    quarter, piece = part // 4, part // 16
    f32 = jnp.float32
    out_a, out_b = pl.pallas_call(
        _all_reduce_kernel,
        out_shape=(jax.ShapeDtypeStruct((rows_a, 128), f32), jax.ShapeDtypeStruct((rows_b, 256), f32)),
        in_specs=[pl.BlockSpec(memory_space=pltpu.VMEM)],
        out_specs=(pl.BlockSpec(memory_space=pltpu.VMEM), pl.BlockSpec(memory_space=pltpu.VMEM)),
        scratch_shapes=[
            pltpu.VMEM((rows, 128), jnp.bfloat16),
            pltpu.VMEM((half, 128), f32),
            pltpu.VMEM((half, 128), f32),
            pltpu.VMEM((3, 3, quarter, 128), f32),
            pltpu.VMEM((3, quarter, 128), f32),
            pltpu.VMEM((3, 3, piece, 128), f32),
            pltpu.VMEM((3, piece, 128), f32),
            pltpu.VMEM((3, 4, piece, 128), f32),
            pltpu.SemaphoreType.DMA((47,)),
            pltpu.SemaphoreType.DMA((47,)),
        ],
        compiler_params=pltpu.CompilerParams(collective_id=0, has_side_effects=True),
    )(flat)
    return out_a.reshape(sums_a.shape), out_b.reshape(sums_b.shape)


def conv_cells(field, kernel):
    shaped = kernel.reshape(3, 3, 3, kernel.shape[1], kernel.shape[2])
    result = lax.conv_general_dilated(
        field[None],
        shaped,
        (1, 1, 1),
        ((0, 0), (1, 1), (1, 1)),
        dimension_numbers=("NCDHW", "DHWIO", "NCDHW"),
        preferred_element_type=jnp.float32,
    )
    return result[0]


def back_cells(padded, kernel):
    flipped = kernel[::-1].transpose(0, 2, 1)
    return conv_cells(padded, flipped)


def kernel_terms(padded, upstream):
    taps, chan_in, chan_out = 27, padded.shape[0], upstream.shape[0]
    start = jnp.zeros((taps, chan_in, chan_out), jnp.float32)
    field = padded.astype(jnp.float32)
    unused, pull = jax.vjp(lambda w: conv_cells(field, w), start)
    return pull(upstream.astype(jnp.float32))[0]


def _layer_a_body(src_ref, up_ref, pad_ref, w_ref, terms_ref, back_ref):
    cells = up_ref.shape[1]
    width = src_ref.shape[1]
    plane = width // 4
    side = 32
    spot = lax.broadcasted_iota(jnp.int32, (1, cells), 1)
    column = spot % side
    row = (spot // side) % side
    upstream = up_ref[...]
    field = src_ref[...].astype(jnp.float32)
    back = jnp.zeros((back_ref.shape[0], cells), jnp.float32)
    for b in range(3):
        for c in range(3):
            shift = (b - 1) * side + (c - 1)
            moved = pltpu.roll(field, (width - shift) % width, 1)
            inside = (column + c - 1 >= 0) & (column + c - 1 < side) & (row + b - 1 >= 0) & (row + b - 1 < side)
            total = jnp.zeros_like(back)
            for a in range(3):
                tap = 9 * a + 3 * b + c
                window = moved[:, a * plane : a * plane + cells]
                window = jnp.where(inside, window, 0.0).astype(jnp.bfloat16)
                terms_ref[tap] = lax.dot_general(
                    window, upstream, (((1,), (1,)), ((), ())), preferred_element_type=jnp.float32
                )
                total = total + jnp.dot(
                    w_ref[tap], pad_ref[:, (2 - a) * plane : (2 - a) * plane + cells], preferred_element_type=jnp.float32
                )
            back_in = (column - c + 1 >= 0) & (column - c + 1 < side) & (row - b + 1 >= 0) & (row - b + 1 < side)
            back = back + jnp.where(back_in, pltpu.roll(total, shift % cells, 1), 0.0)
    back_ref[...] = back.astype(back_ref.dtype)


def layer_a_grads(source_pad, hidden_pad, grad_hidden, weight_a):
    chan_in, chan_out = source_pad.shape[0], grad_hidden.shape[0]
    cells = grad_hidden.shape[1] * grad_hidden.shape[2]
    return pl.pallas_call(
        _layer_a_body,
        out_shape=(
            jax.ShapeDtypeStruct((27, chan_in, chan_out), jnp.float32),
            jax.ShapeDtypeStruct((chan_in, cells), jnp.bfloat16),
        ),
        in_specs=[pl.BlockSpec(memory_space=pltpu.VMEM)] * 4,
        out_specs=(pl.BlockSpec(memory_space=pltpu.VMEM), pl.BlockSpec(memory_space=pltpu.VMEM)),
    )(source_pad.reshape(chan_in, -1), grad_hidden.reshape(chan_out, -1), hidden_pad.reshape(chan_out, -1), weight_a)


def _halo_body(heads_ref, tails_ref, below_ref, above_ref, got_below, got_above, sends, recvs):
    mesh_id = pl.DeviceIdType.MESH
    count = lax.axis_size("space")
    dp = lax.axis_index("dp")
    sp = lax.axis_index("space")
    up = (dp, (sp + 1) % count)
    down = (dp, (sp + count - 1) % count)
    barrier = pltpu.get_barrier_semaphore()
    for other in (up, down):
        pl.semaphore_signal(barrier, inc=1, device_id=other, device_id_type=mesh_id)
    pl.semaphore_wait(barrier, 2)
    copies = [
        pltpu.make_async_remote_copy(
            src_ref=tails_ref, dst_ref=got_below, send_sem=sends.at[0], recv_sem=recvs.at[0], device_id=up, device_id_type=mesh_id
        ),
        pltpu.make_async_remote_copy(
            src_ref=heads_ref, dst_ref=got_above, send_sem=sends.at[1], recv_sem=recvs.at[1], device_id=down, device_id_type=mesh_id
        ),
    ]
    for copy in copies:
        copy.start()
    for copy in copies:
        copy.wait()
    below_ref[...] = jnp.where(sp > 0, got_below[...], jnp.zeros_like(got_below[...]))
    above_ref[...] = jnp.where(sp < count - 1, got_above[...], jnp.zeros_like(got_above[...]))


def halos(arrays, tag):
    heads = jnp.concatenate([a[:, :1].reshape(-1) for a in arrays])
    tails = jnp.concatenate([a[:, -1:].reshape(-1) for a in arrays])
    count = heads.shape[0]
    unit = 16 * 128
    size = -(-count // unit) * unit
    heads = jnp.pad(heads, (0, size - count)).reshape(size // 128, 128)
    tails = jnp.pad(tails, (0, size - count)).reshape(size // 128, 128)
    block = jax.ShapeDtypeStruct(heads.shape, heads.dtype)
    below, above = pl.pallas_call(
        _halo_body,
        out_shape=(block, block),
        in_specs=[pl.BlockSpec(memory_space=pltpu.VMEM)] * 2,
        out_specs=(pl.BlockSpec(memory_space=pltpu.VMEM), pl.BlockSpec(memory_space=pltpu.VMEM)),
        scratch_shapes=[
            pltpu.VMEM(heads.shape, heads.dtype),
            pltpu.VMEM(heads.shape, heads.dtype),
            pltpu.SemaphoreType.DMA((2,)),
            pltpu.SemaphoreType.DMA((2,)),
        ],
        compiler_params=pltpu.CompilerParams(collective_id=tag, has_side_effects=True),
    )(heads, tails)
    below, above = below.reshape(-1), above.reshape(-1)
    out, start = [], 0
    for a in arrays:
        plane = a.shape[0] * a.shape[2]
        shape = (a.shape[0], 1, a.shape[2])
        low = below[start : start + plane].reshape(shape)
        high = above[start : start + plane].reshape(shape)
        out.append(jnp.concatenate([low, a, high], axis=1))
        start += plane
    return out


def per_device(layer_input, hidden_pre, output_pre, output_grad, weight_a, weight_b):
    side = math.isqrt(layer_input.shape[3])
    half = side // 2
    depth_a = layer_input.shape[2]
    depth_b = depth_a // 2
    source = layer_input[0]
    hidden = hidden_pre[0]
    outer = output_pre[0]
    upstream = output_grad[0]
    chan_in = source.shape[0]
    width_a = hidden.shape[0]
    width_b = outer.shape[0]
    grad_outer = (upstream.astype(jnp.float32) * slopes(outer.astype(jnp.float32))).astype(
        jnp.bfloat16
    )
    hidden_f = hidden.astype(jnp.float32)
    active = jnp.where(hidden_f > 0, hidden_f, negative_slope * hidden_f)
    pooled = (
        active.reshape(width_a, depth_b, 2, half, 2, half, 2)
        .mean(axis=(2, 4, 6))
        .astype(jnp.bfloat16)
    )
    pooled = pooled.reshape(width_a, depth_b, half * half)
    outer_pad, pooled_pad, source_pad = halos([grad_outer, pooled, source], 1)
    outer_pad = outer_pad.reshape(width_b, depth_b + 2, half, half)
    pooled_pad = pooled_pad.reshape(width_a, depth_b + 2, half, half)
    back_b = back_cells(outer_pad, weight_b)
    sums_b = kernel_terms(pooled_pad, grad_outer.reshape(width_b, depth_b, half, half))
    upward = jnp.repeat(jnp.repeat(jnp.repeat(back_b, 2, 1), 2, 2), 2, 3) * 0.125
    upward = upward.reshape(width_a, depth_a * side * side)
    grad_hidden = (upward * slopes(hidden_f.reshape(width_a, depth_a * side * side))).astype(
        jnp.bfloat16
    )
    grad_hidden = grad_hidden.reshape(width_a, depth_a, side * side)
    (hidden_pad,) = halos([grad_hidden], 2)
    sums_a, back_a = layer_a_grads(source_pad, hidden_pad, grad_hidden, weight_a)
    input_grad = back_a.astype(jnp.bfloat16).reshape(1, chan_in, depth_a, side * side)
    samples = lax.axis_size("dp")
    planes_a = depth_a * lax.axis_size("space")
    scale_a = 1.0 / math.sqrt(samples * planes_a * side * side)
    scale_b = 1.0 / math.sqrt(samples * (planes_a // 2) * half * half)
    total_a, total_b = all_reduce(sums_a, sums_b, scale_a, scale_b)
    return (input_grad, total_a, total_b)


def solution(mesh):
    in_specs = (
        P("dp", None, "space", None),
        P("dp", None, "space", None),
        P("dp", None, "space", None),
        P("dp", None, "space", None),
        P(),
        P(),
    )
    out_specs = (P("dp", None, "space", None), P(), P())
    return jax.shard_map(
        per_device, mesh=mesh, in_specs=in_specs, out_specs=out_specs, check_vma=False
    )
```

```python
import math

import jax
import jax.numpy as jnp
from jax import lax
from jax.sharding import PartitionSpec as P
from jax.experimental import pallas as pl
from jax.experimental.pallas import tpu as pltpu

negative_slope = 0.3


def padded_2(cells, sides, width):
    for axis, dim in sides:
        count = lax.axis_size(axis)
        ends = count - 1
        head = lax.slice_in_dim(cells, 0, width, axis=dim)
        tail = lax.slice_in_dim(cells, cells.shape[dim] - width, cells.shape[dim], axis=dim)
        cells = jnp.concatenate(
            [
                lax.ppermute(tail, axis, [(i, (i + 1) % count) for i in range(ends)]),
                cells,
                lax.ppermute(head, axis, [((i + 1) % count, i) for i in range(ends)]),
            ],
            axis=dim,
        )
    return cells


def slopes(values):
    return jnp.where(values > 0, jnp.ones_like(values), negative_slope * jnp.ones_like(values))


def window(padded, tap_z, tap_y, tap_x, depth, side):
    planes = padded[:, tap_z : tap_z + depth, :]
    margin = side + 1
    wider = jnp.pad(planes, ((0, 0), (0, 0), (margin, margin)))
    offset = (tap_y - 1) * side + (tap_x - 1)
    piece = wider[:, :, margin + offset : margin + offset + side * side]
    column = jnp.arange(side * side, dtype=jnp.int32) % side + (tap_x - 1)
    inside = (column >= 0) & (column < side)
    piece = jnp.where(inside, piece, jnp.zeros_like(piece))
    return piece.reshape(padded.shape[0], depth * side * side)


def outer_product(left, right):
    return lax.dot_general(
        left, right, (((1,), (1,)), ((), ())), preferred_element_type=jnp.float32
    )


def _all_reduce_kernel(x_ref, o_ref, full, recv_a, acc_a, recv_1, acc_1, recv_2, acc_2, recv_3, sends, recvs):
    rows = x_ref.shape[0]
    half = rows // 2
    part = half // 3
    quarter, piece = part // 4, part // 16
    mesh_id = pl.DeviceIdType.MESH
    dp = lax.axis_index("dp")
    sp = lax.axis_index("space")
    core = dp % 2
    spot = {"x": dp // 2, "y": sp // 4, "z": sp % 4}
    partner = (spot["x"] * 2 + (1 - core), sp)

    def peer(axis, k):
        moved = dict(spot)
        moved[axis] = (spot[axis] + k) % 4
        return (moved["x"] * 2 + core, moved["y"] * 4 + moved["z"])

    orders = (("x", "y", "z"), ("y", "z", "x"), ("z", "x", "y"))
    peers = [partner] + [peer(axis, k) for axis in "xyz" for k in (1, 2, 3)]
    barrier = pltpu.get_barrier_semaphore()
    for other in peers:
        pl.semaphore_signal(barrier, inc=1, device_id=other, device_id_type=mesh_id)
    pl.semaphore_wait(barrier, len(peers))

    def rows_at(start, size):
        return pl.ds(pl.multiple_of(start, 16), size)

    used = [0]

    def exchange(triples):
        copies = []
        for src, dst, other in triples:
            copy = pltpu.make_async_remote_copy(
                src_ref=src,
                dst_ref=dst,
                send_sem=sends.at[used[0]],
                recv_sem=recvs.at[used[0]],
                device_id=other,
                device_id_type=mesh_id,
            )
            used[0] += 1
            copy.start()
            copies.append(copy)
        for copy in copies:
            copy.wait()

    exchange([(x_ref.at[rows_at((1 - core) * half, half)], recv_a, partner)])
    acc_a[...] = x_ref[rows_at(core * half, half), :] + recv_a[...]
    triples = []
    for p, order in enumerate(orders):
        for k in (1, 2, 3):
            block = p * part + ((spot[order[0]] + k) % 4) * quarter
            triples.append((acc_a.at[rows_at(block, quarter)], recv_1.at[p, k - 1], peer(order[0], k)))
    exchange(triples)
    for p, order in enumerate(orders):
        mine = p * part + spot[order[0]] * quarter
        acc_1[p] = acc_a[rows_at(mine, quarter), :] + recv_1[p, 0] + recv_1[p, 1] + recv_1[p, 2]
    triples = []
    for p, order in enumerate(orders):
        for k in (1, 2, 3):
            block = ((spot[order[1]] + k) % 4) * piece
            triples.append((acc_1.at[p, rows_at(block, piece)], recv_2.at[p, k - 1], peer(order[1], k)))
    exchange(triples)
    for p, order in enumerate(orders):
        mine = spot[order[1]] * piece
        recv_3[p, 0] = acc_1[p, rows_at(mine, piece), :] + recv_2[p, 0] + recv_2[p, 1] + recv_2[p, 2]
    exchange([(recv_3.at[p, 0], recv_3.at[p, k], peer(order[2], k)) for p, order in enumerate(orders) for k in (1, 2, 3)])
    spans = []
    for p, order in enumerate(orders):
        last = spot[order[2]]
        total = recv_3[p, last % 4]
        for j in (1, 2, 3):
            total = total + recv_3[p, (last - j + 4) % 4]
        outer = core * half + p * part + spot[order[0]] * quarter
        own = outer + spot[order[1]] * piece
        full[rows_at(own, piece), :] = total.astype(full.dtype)
        spans.append((outer, own, order))
    exchange([(full.at[rows_at(own, piece)], full.at[rows_at(own, piece)], peer(order[1], k)) for outer, own, order in spans for k in (1, 2, 3)])
    exchange([(full.at[rows_at(outer, quarter)], full.at[rows_at(outer, quarter)], peer(order[0], k)) for outer, own, order in spans for k in (1, 2, 3)])
    block = full.at[rows_at(core * half, half)]
    exchange([(block, block, partner)])
    o_ref[...] = full[...]


def all_reduce(sums_a, sums_b, scale_a, scale_b):
    rows_a = sums_a.shape[0] * sums_a.shape[1]
    rows_b = sums_b.shape[0] * sums_b.shape[1]
    wide = sums_b.reshape(rows_b, 256) * scale_b
    flat = jnp.concatenate([sums_a.reshape(rows_a, 128) * scale_a, wide[:, :128], wide[:, 128:]])
    count = flat.shape[0]
    unit = 6 * 16 * 16
    rows = -(-count // unit) * unit
    flat = jnp.pad(flat, ((0, rows - count), (0, 0)))
    half = rows // 2
    part = half // 3
    quarter, piece = part // 4, part // 16
    f32 = jnp.float32
    full = pl.pallas_call(
        _all_reduce_kernel,
        out_shape=jax.ShapeDtypeStruct((rows, 128), jnp.bfloat16),
        in_specs=[pl.BlockSpec(memory_space=pltpu.VMEM)],
        out_specs=pl.BlockSpec(memory_space=pltpu.VMEM),
        scratch_shapes=[
            pltpu.VMEM((rows, 128), jnp.bfloat16),
            pltpu.VMEM((half, 128), f32),
            pltpu.VMEM((half, 128), f32),
            pltpu.VMEM((3, 3, quarter, 128), f32),
            pltpu.VMEM((3, quarter, 128), f32),
            pltpu.VMEM((3, 3, piece, 128), f32),
            pltpu.VMEM((3, piece, 128), f32),
            pltpu.VMEM((3, 4, piece, 128), f32),
            pltpu.SemaphoreType.DMA((47,)),
            pltpu.SemaphoreType.DMA((47,)),
        ],
        compiler_params=pltpu.CompilerParams(collective_id=0, has_side_effects=True),
    )(flat)
    full = full.astype(f32)
    out_a = full[:rows_a]
    out_b = jnp.concatenate([full[rows_a : rows_a + rows_b], full[rows_a + rows_b : rows_a + 2 * rows_b]], axis=1)
    return out_a.reshape(sums_a.shape), out_b.reshape(sums_b.shape)


def conv_cells(field, kernel):
    shaped = kernel.reshape(3, 3, 3, kernel.shape[1], kernel.shape[2])
    result = lax.conv_general_dilated(
        field[None],
        shaped,
        (1, 1, 1),
        ((0, 0), (1, 1), (1, 1)),
        dimension_numbers=("NCDHW", "DHWIO", "NCDHW"),
        preferred_element_type=jnp.float32,
    )
    return result[0]


def back_cells(padded, kernel):
    flipped = kernel[::-1].transpose(0, 2, 1)
    return conv_cells(padded, flipped)


def kernel_terms(padded, upstream):
    taps, chan_in, chan_out = 27, padded.shape[0], upstream.shape[0]
    start = jnp.zeros((taps, chan_in, chan_out), jnp.float32)
    field = padded.astype(jnp.float32)
    unused, pull = jax.vjp(lambda w: conv_cells(field, w), start)
    return pull(upstream.astype(jnp.float32))[0]


def per_device(layer_input, hidden_pre, output_pre, output_grad, weight_a, weight_b):
    side = math.isqrt(layer_input.shape[3])
    half = side // 2
    depth_a = layer_input.shape[2]
    depth_b = depth_a // 2
    source = layer_input[0]
    hidden = hidden_pre[0]
    outer = output_pre[0]
    upstream = output_grad[0]
    chan_in = source.shape[0]
    width_a = hidden.shape[0]
    width_b = outer.shape[0]
    grad_outer = (upstream.astype(jnp.float32) * slopes(outer.astype(jnp.float32))).astype(
        jnp.bfloat16
    )
    hidden_f = hidden.astype(jnp.float32)
    active = jnp.where(hidden_f > 0, hidden_f, negative_slope * hidden_f)
    pooled = (
        active.reshape(width_a, depth_b, 2, half, 2, half, 2)
        .mean(axis=(2, 4, 6))
        .astype(jnp.bfloat16)
    )
    pooled = pooled.reshape(width_a, depth_b, half * half)
    outer_pad = padded_2(grad_outer, (("space", 1),), 1).reshape(width_b, depth_b + 2, half, half)
    pooled_pad = padded_2(pooled, (("space", 1),), 1).reshape(width_a, depth_b + 2, half, half)
    back_b = back_cells(outer_pad, weight_b)
    sums_b = kernel_terms(pooled_pad, grad_outer.reshape(width_b, depth_b, half, half))
    upward = jnp.repeat(jnp.repeat(jnp.repeat(back_b, 2, 1), 2, 2), 2, 3) * 0.125
    upward = upward.reshape(width_a, depth_a * side * side)
    grad_hidden = (upward * slopes(hidden_f.reshape(width_a, depth_a * side * side))).astype(
        jnp.bfloat16
    )
    grad_hidden = grad_hidden.reshape(width_a, depth_a, side * side)
    hidden_pad = padded_2(grad_hidden, (("space", 1),), 1).reshape(width_a, depth_a + 2, side, side)
    source_pad = padded_2(source, (("space", 1),), 1).reshape(chan_in, depth_a + 2, side, side)
    back_a = back_cells(hidden_pad, weight_a)
    sums_a = kernel_terms(source_pad, grad_hidden.reshape(width_a, depth_a, side, side))
    input_grad = back_a.astype(jnp.bfloat16).reshape(1, chan_in, depth_a, side * side)
    samples = lax.axis_size("dp")
    planes_a = depth_a * lax.axis_size("space")
    scale_a = 1.0 / math.sqrt(samples * planes_a * side * side)
    scale_b = 1.0 / math.sqrt(samples * (planes_a // 2) * half * half)
    total_a, total_b = all_reduce(sums_a, sums_b, scale_a, scale_b)
    return (input_grad, total_a, total_b)


def solution(mesh):
    in_specs = (
        P("dp", None, "space", None),
        P("dp", None, "space", None),
        P("dp", None, "space", None),
        P("dp", None, "space", None),
        P(),
        P(),
    )
    out_specs = (P("dp", None, "space", None), P(), P())
    return jax.shard_map(
        per_device, mesh=mesh, in_specs=in_specs, out_specs=out_specs, check_vma=False
    )
```

```python
import math

import jax
import jax.numpy as jnp
from jax import lax
from jax.sharding import PartitionSpec as P
from jax.experimental import pallas as pl
from jax.experimental.pallas import tpu as pltpu

negative_slope = 0.3


def padded_2(cells, sides, width):
    for axis, dim in sides:
        count = lax.axis_size(axis)
        ends = count - 1
        head = lax.slice_in_dim(cells, 0, width, axis=dim)
        tail = lax.slice_in_dim(cells, cells.shape[dim] - width, cells.shape[dim], axis=dim)
        cells = jnp.concatenate(
            [
                lax.ppermute(tail, axis, [(i, (i + 1) % count) for i in range(ends)]),
                cells,
                lax.ppermute(head, axis, [((i + 1) % count, i) for i in range(ends)]),
            ],
            axis=dim,
        )
    return cells


def slopes(values):
    return jnp.where(values > 0, jnp.ones_like(values), negative_slope * jnp.ones_like(values))


def window(padded, tap_z, tap_y, tap_x, depth, side):
    planes = padded[:, tap_z : tap_z + depth, :]
    margin = side + 1
    wider = jnp.pad(planes, ((0, 0), (0, 0), (margin, margin)))
    offset = (tap_y - 1) * side + (tap_x - 1)
    piece = wider[:, :, margin + offset : margin + offset + side * side]
    column = jnp.arange(side * side, dtype=jnp.int32) % side + (tap_x - 1)
    inside = (column >= 0) & (column < side)
    piece = jnp.where(inside, piece, jnp.zeros_like(piece))
    return piece.reshape(padded.shape[0], depth * side * side)


def outer_product(left, right):
    return lax.dot_general(
        left, right, (((1,), (1,)), ((), ())), preferred_element_type=jnp.float32
    )


def _all_reduce_kernel(x_ref, o_a, o_b, full, recv_a, acc_a, recv_1, acc_1, recv_2, acc_2, recv_3, sends, recvs):
    rows = x_ref.shape[0]
    half = rows // 2
    part = half // 3
    quarter, piece = part // 4, part // 16
    mesh_id = pl.DeviceIdType.MESH
    dp = lax.axis_index("dp")
    sp = lax.axis_index("space")
    core = dp % 2
    spot = {"x": dp // 2, "y": sp // 4, "z": sp % 4}
    partner = (spot["x"] * 2 + (1 - core), sp)

    def peer(axis, k):
        moved = dict(spot)
        moved[axis] = (spot[axis] + k) % 4
        return (moved["x"] * 2 + core, moved["y"] * 4 + moved["z"])

    orders = (("x", "y", "z"), ("y", "z", "x"), ("z", "x", "y"))
    peers = [partner] + [peer(axis, k) for axis in "xyz" for k in (1, 2, 3)]
    barrier = pltpu.get_barrier_semaphore()
    for other in peers:
        pl.semaphore_signal(barrier, inc=1, device_id=other, device_id_type=mesh_id)
    pl.semaphore_wait(barrier, len(peers))

    def rows_at(start, size):
        return pl.ds(pl.multiple_of(start, 16), size)

    used = [0]

    def exchange(triples):
        copies = []
        for src, dst, other in triples:
            copy = pltpu.make_async_remote_copy(
                src_ref=src,
                dst_ref=dst,
                send_sem=sends.at[used[0]],
                recv_sem=recvs.at[used[0]],
                device_id=other,
                device_id_type=mesh_id,
            )
            used[0] += 1
            copy.start()
            copies.append(copy)
        for copy in copies:
            copy.wait()

    exchange([(x_ref.at[rows_at((1 - core) * half, half)], recv_a, partner)])
    acc_a[...] = x_ref[rows_at(core * half, half), :] + recv_a[...]
    triples = []
    for p, order in enumerate(orders):
        for k in (1, 2, 3):
            block = p * part + ((spot[order[0]] + k) % 4) * quarter
            triples.append((acc_a.at[rows_at(block, quarter)], recv_1.at[p, k - 1], peer(order[0], k)))
    exchange(triples)
    for p, order in enumerate(orders):
        mine = p * part + spot[order[0]] * quarter
        acc_1[p] = acc_a[rows_at(mine, quarter), :] + recv_1[p, 0] + recv_1[p, 1] + recv_1[p, 2]
    triples = []
    for p, order in enumerate(orders):
        for k in (1, 2, 3):
            block = ((spot[order[1]] + k) % 4) * piece
            triples.append((acc_1.at[p, rows_at(block, piece)], recv_2.at[p, k - 1], peer(order[1], k)))
    exchange(triples)
    for p, order in enumerate(orders):
        mine = spot[order[1]] * piece
        recv_3[p, 0] = acc_1[p, rows_at(mine, piece), :] + recv_2[p, 0] + recv_2[p, 1] + recv_2[p, 2]
    exchange([(recv_3.at[p, 0], recv_3.at[p, k], peer(order[2], k)) for p, order in enumerate(orders) for k in (1, 2, 3)])
    spans = []
    for p, order in enumerate(orders):
        last = spot[order[2]]
        total = recv_3[p, last % 4]
        for j in (1, 2, 3):
            total = total + recv_3[p, (last - j + 4) % 4]
        outer = core * half + p * part + spot[order[0]] * quarter
        own = outer + spot[order[1]] * piece
        full[rows_at(own, piece), :] = total.astype(full.dtype)
        spans.append((outer, own, order))
    exchange([(full.at[rows_at(own, piece)], full.at[rows_at(own, piece)], peer(order[1], k)) for outer, own, order in spans for k in (1, 2, 3)])
    exchange([(full.at[rows_at(outer, quarter)], full.at[rows_at(outer, quarter)], peer(order[0], k)) for outer, own, order in spans for k in (1, 2, 3)])
    block = full.at[rows_at(core * half, half)]
    exchange([(block, block, partner)])
    rows_a, rows_b = o_a.shape[0], o_b.shape[0]
    o_a[...] = full[0:rows_a, :].astype(jnp.float32)
    o_b[:, 0:128] = full[rows_a : rows_a + rows_b, :].astype(jnp.float32)
    o_b[:, 128:256] = full[rows_a + rows_b : rows_a + 2 * rows_b, :].astype(jnp.float32)


def all_reduce(sums_a, sums_b, scale_a, scale_b):
    rows_a = sums_a.shape[0] * sums_a.shape[1]
    rows_b = sums_b.shape[0] * sums_b.shape[1]
    wide = sums_b.reshape(rows_b, 256) * scale_b
    flat = jnp.concatenate([sums_a.reshape(rows_a, 128) * scale_a, wide[:, :128], wide[:, 128:]])
    count = flat.shape[0]
    unit = 6 * 16 * 16
    rows = -(-count // unit) * unit
    flat = jnp.pad(flat, ((0, rows - count), (0, 0)))
    half = rows // 2
    part = half // 3
    quarter, piece = part // 4, part // 16
    f32 = jnp.float32
    out_a, out_b = pl.pallas_call(
        _all_reduce_kernel,
        out_shape=(jax.ShapeDtypeStruct((rows_a, 128), f32), jax.ShapeDtypeStruct((rows_b, 256), f32)),
        in_specs=[pl.BlockSpec(memory_space=pltpu.VMEM)],
        out_specs=(pl.BlockSpec(memory_space=pltpu.VMEM), pl.BlockSpec(memory_space=pltpu.VMEM)),
        scratch_shapes=[
            pltpu.VMEM((rows, 128), jnp.bfloat16),
            pltpu.VMEM((half, 128), f32),
            pltpu.VMEM((half, 128), f32),
            pltpu.VMEM((3, 3, quarter, 128), f32),
            pltpu.VMEM((3, quarter, 128), f32),
            pltpu.VMEM((3, 3, piece, 128), f32),
            pltpu.VMEM((3, piece, 128), f32),
            pltpu.VMEM((3, 4, piece, 128), f32),
            pltpu.SemaphoreType.DMA((47,)),
            pltpu.SemaphoreType.DMA((47,)),
        ],
        compiler_params=pltpu.CompilerParams(collective_id=0, has_side_effects=True),
    )(flat)
    return out_a.reshape(sums_a.shape), out_b.reshape(sums_b.shape)


def conv_cells(field, kernel):
    shaped = kernel.reshape(3, 3, 3, kernel.shape[1], kernel.shape[2])
    result = lax.conv_general_dilated(
        field[None],
        shaped,
        (1, 1, 1),
        ((0, 0), (1, 1), (1, 1)),
        dimension_numbers=("NCDHW", "DHWIO", "NCDHW"),
        preferred_element_type=jnp.float32,
    )
    return result[0]


def back_cells(padded, kernel):
    flipped = kernel[::-1].transpose(0, 2, 1)
    return conv_cells(padded, flipped)


def kernel_terms(padded, upstream):
    taps, chan_in, chan_out = 27, padded.shape[0], upstream.shape[0]
    start = jnp.zeros((taps, chan_in, chan_out), jnp.float32)
    field = padded.astype(jnp.float32)
    unused, pull = jax.vjp(lambda w: conv_cells(field, w), start)
    return pull(upstream.astype(jnp.float32))[0]


def _terms_a_body(src_ref, up_ref, terms_ref):
    cells = up_ref.shape[1]
    width = src_ref.shape[1]
    plane = width // 4
    side = 32
    spot = lax.broadcasted_iota(jnp.int32, (1, cells), 1)
    column = spot % side
    row = (spot // side) % side
    upstream = up_ref[...]
    field = src_ref[...].astype(jnp.float32)
    for b in range(3):
        for c in range(3):
            shift = (b - 1) * side + (c - 1)
            moved = pltpu.roll(field, (width - shift) % width, 1)
            inside = (column + c - 1 >= 0) & (column + c - 1 < side) & (row + b - 1 >= 0) & (row + b - 1 < side)
            for a in range(3):
                window = moved[:, a * plane : a * plane + cells]
                window = jnp.where(inside, window, 0.0).astype(jnp.bfloat16)
                terms_ref[9 * a + 3 * b + c] = lax.dot_general(
                    window, upstream, (((1,), (1,)), ((), ())), preferred_element_type=jnp.float32
                )


def kernel_terms_flat(source_pad, grad_hidden):
    chan_in, chan_out = source_pad.shape[0], grad_hidden.shape[0]
    return pl.pallas_call(
        _terms_a_body,
        out_shape=jax.ShapeDtypeStruct((27, chan_in, chan_out), jnp.float32),
        in_specs=[pl.BlockSpec(memory_space=pltpu.VMEM)] * 2,
        out_specs=pl.BlockSpec(memory_space=pltpu.VMEM),
    )(source_pad.reshape(chan_in, -1), grad_hidden.reshape(chan_out, -1))


def per_device(layer_input, hidden_pre, output_pre, output_grad, weight_a, weight_b):
    side = math.isqrt(layer_input.shape[3])
    half = side // 2
    depth_a = layer_input.shape[2]
    depth_b = depth_a // 2
    source = layer_input[0]
    hidden = hidden_pre[0]
    outer = output_pre[0]
    upstream = output_grad[0]
    chan_in = source.shape[0]
    width_a = hidden.shape[0]
    width_b = outer.shape[0]
    grad_outer = (upstream.astype(jnp.float32) * slopes(outer.astype(jnp.float32))).astype(
        jnp.bfloat16
    )
    hidden_f = hidden.astype(jnp.float32)
    active = jnp.where(hidden_f > 0, hidden_f, negative_slope * hidden_f)
    pooled = (
        active.reshape(width_a, depth_b, 2, half, 2, half, 2)
        .mean(axis=(2, 4, 6))
        .astype(jnp.bfloat16)
    )
    pooled = pooled.reshape(width_a, depth_b, half * half)
    outer_pad = padded_2(grad_outer, (("space", 1),), 1).reshape(width_b, depth_b + 2, half, half)
    pooled_pad = padded_2(pooled, (("space", 1),), 1).reshape(width_a, depth_b + 2, half, half)
    back_b = back_cells(outer_pad, weight_b)
    sums_b = kernel_terms(pooled_pad, grad_outer.reshape(width_b, depth_b, half, half))
    upward = jnp.repeat(jnp.repeat(jnp.repeat(back_b, 2, 1), 2, 2), 2, 3) * 0.125
    upward = upward.reshape(width_a, depth_a * side * side)
    grad_hidden = (upward * slopes(hidden_f.reshape(width_a, depth_a * side * side))).astype(
        jnp.bfloat16
    )
    grad_hidden = grad_hidden.reshape(width_a, depth_a, side * side)
    hidden_pad = padded_2(grad_hidden, (("space", 1),), 1).reshape(width_a, depth_a + 2, side, side)
    source_pad = padded_2(source, (("space", 1),), 1)
    back_a = back_cells(hidden_pad, weight_a)
    sums_a = kernel_terms_flat(source_pad, grad_hidden)
    input_grad = back_a.astype(jnp.bfloat16).reshape(1, chan_in, depth_a, side * side)
    samples = lax.axis_size("dp")
    planes_a = depth_a * lax.axis_size("space")
    scale_a = 1.0 / math.sqrt(samples * planes_a * side * side)
    scale_b = 1.0 / math.sqrt(samples * (planes_a // 2) * half * half)
    total_a, total_b = all_reduce(sums_a, sums_b, scale_a, scale_b)
    return (input_grad, total_a, total_b)


def solution(mesh):
    in_specs = (
        P("dp", None, "space", None),
        P("dp", None, "space", None),
        P("dp", None, "space", None),
        P("dp", None, "space", None),
        P(),
        P(),
    )
    out_specs = (P("dp", None, "space", None), P(), P())
    return jax.shard_map(
        per_device, mesh=mesh, in_specs=in_specs, out_specs=out_specs, check_vma=False
    )
```

```python
import math

import jax
import jax.numpy as jnp
from jax import lax
from jax.sharding import PartitionSpec as P
from jax.experimental import pallas as pl
from jax.experimental.pallas import tpu as pltpu

negative_slope = 0.3


def padded_2(cells, sides, width):
    for axis, dim in sides:
        count = lax.axis_size(axis)
        ends = count - 1
        head = lax.slice_in_dim(cells, 0, width, axis=dim)
        tail = lax.slice_in_dim(cells, cells.shape[dim] - width, cells.shape[dim], axis=dim)
        cells = jnp.concatenate(
            [
                lax.ppermute(tail, axis, [(i, (i + 1) % count) for i in range(ends)]),
                cells,
                lax.ppermute(head, axis, [((i + 1) % count, i) for i in range(ends)]),
            ],
            axis=dim,
        )
    return cells


def slopes(values):
    return jnp.where(values > 0, jnp.ones_like(values), negative_slope * jnp.ones_like(values))


def window(padded, tap_z, tap_y, tap_x, depth, side):
    planes = padded[:, tap_z : tap_z + depth, :]
    margin = side + 1
    wider = jnp.pad(planes, ((0, 0), (0, 0), (margin, margin)))
    offset = (tap_y - 1) * side + (tap_x - 1)
    piece = wider[:, :, margin + offset : margin + offset + side * side]
    column = jnp.arange(side * side, dtype=jnp.int32) % side + (tap_x - 1)
    inside = (column >= 0) & (column < side)
    piece = jnp.where(inside, piece, jnp.zeros_like(piece))
    return piece.reshape(padded.shape[0], depth * side * side)


def outer_product(left, right):
    return lax.dot_general(
        left, right, (((1,), (1,)), ((), ())), preferred_element_type=jnp.float32
    )


def _all_reduce_kernel(x_ref, o_a, o_b, full, recv_a, acc_a, recv_1, acc_1, recv_2, acc_2, recv_3, sends, recvs):
    rows = x_ref.shape[0]
    half = rows // 2
    part = half // 3
    quarter, piece = part // 4, part // 16
    mesh_id = pl.DeviceIdType.MESH
    dp = lax.axis_index("dp")
    sp = lax.axis_index("space")
    core = dp % 2
    spot = {"x": dp // 2, "y": sp // 4, "z": sp % 4}
    partner = (spot["x"] * 2 + (1 - core), sp)

    def peer(axis, k):
        moved = dict(spot)
        moved[axis] = (spot[axis] + k) % 4
        return (moved["x"] * 2 + core, moved["y"] * 4 + moved["z"])

    orders = (("x", "y", "z"), ("y", "z", "x"), ("z", "x", "y"))
    peers = [partner] + [peer(axis, k) for axis in "xyz" for k in (1, 2, 3)]
    barrier = pltpu.get_barrier_semaphore()
    for other in peers:
        pl.semaphore_signal(barrier, inc=1, device_id=other, device_id_type=mesh_id)
    pl.semaphore_wait(barrier, len(peers))

    def rows_at(start, size):
        return pl.ds(pl.multiple_of(start, 16), size)

    used = [0]

    def exchange(triples):
        copies = []
        for src, dst, other in triples:
            copy = pltpu.make_async_remote_copy(
                src_ref=src,
                dst_ref=dst,
                send_sem=sends.at[used[0]],
                recv_sem=recvs.at[used[0]],
                device_id=other,
                device_id_type=mesh_id,
            )
            used[0] += 1
            copy.start()
            copies.append(copy)
        for copy in copies:
            copy.wait()

    exchange([(x_ref.at[rows_at((1 - core) * half, half)], recv_a, partner)])
    acc_a[...] = x_ref[rows_at(core * half, half), :] + recv_a[...]
    triples = []
    for p, order in enumerate(orders):
        for k in (1, 2, 3):
            block = p * part + ((spot[order[0]] + k) % 4) * quarter
            triples.append((acc_a.at[rows_at(block, quarter)], recv_1.at[p, k - 1], peer(order[0], k)))
    exchange(triples)
    for p, order in enumerate(orders):
        mine = p * part + spot[order[0]] * quarter
        acc_1[p] = acc_a[rows_at(mine, quarter), :] + recv_1[p, 0] + recv_1[p, 1] + recv_1[p, 2]
    triples = []
    for p, order in enumerate(orders):
        for k in (1, 2, 3):
            block = ((spot[order[1]] + k) % 4) * piece
            triples.append((acc_1.at[p, rows_at(block, piece)], recv_2.at[p, k - 1], peer(order[1], k)))
    exchange(triples)
    for p, order in enumerate(orders):
        mine = spot[order[1]] * piece
        recv_3[p, 0] = acc_1[p, rows_at(mine, piece), :] + recv_2[p, 0] + recv_2[p, 1] + recv_2[p, 2]
    exchange([(recv_3.at[p, 0], recv_3.at[p, k], peer(order[2], k)) for p, order in enumerate(orders) for k in (1, 2, 3)])
    spans = []
    for p, order in enumerate(orders):
        last = spot[order[2]]
        total = recv_3[p, last % 4]
        for j in (1, 2, 3):
            total = total + recv_3[p, (last - j + 4) % 4]
        outer = core * half + p * part + spot[order[0]] * quarter
        own = outer + spot[order[1]] * piece
        full[rows_at(own, piece), :] = total.astype(full.dtype)
        spans.append((outer, own, order))
    exchange([(full.at[rows_at(own, piece)], full.at[rows_at(own, piece)], peer(order[1], k)) for outer, own, order in spans for k in (1, 2, 3)])
    exchange([(full.at[rows_at(outer, quarter)], full.at[rows_at(outer, quarter)], peer(order[0], k)) for outer, own, order in spans for k in (1, 2, 3)])
    block = full.at[rows_at(core * half, half)]
    exchange([(block, block, partner)])
    rows_a, rows_b = o_a.shape[0], o_b.shape[0]
    o_a[...] = full[0:rows_a, :].astype(jnp.float32)
    o_b[:, 0:128] = full[rows_a : rows_a + rows_b, :].astype(jnp.float32)
    o_b[:, 128:256] = full[rows_a + rows_b : rows_a + 2 * rows_b, :].astype(jnp.float32)


def all_reduce(sums_a, sums_b, scale_a, scale_b):
    rows_a = sums_a.shape[0] * sums_a.shape[1]
    rows_b = sums_b.shape[0] * sums_b.shape[1]
    wide = sums_b.reshape(rows_b, 256) * scale_b
    flat = jnp.concatenate([sums_a.reshape(rows_a, 128) * scale_a, wide[:, :128], wide[:, 128:]])
    count = flat.shape[0]
    unit = 6 * 16 * 16
    rows = -(-count // unit) * unit
    flat = jnp.pad(flat, ((0, rows - count), (0, 0)))
    half = rows // 2
    part = half // 3
    quarter, piece = part // 4, part // 16
    f32 = jnp.float32
    out_a, out_b = pl.pallas_call(
        _all_reduce_kernel,
        out_shape=(jax.ShapeDtypeStruct((rows_a, 128), f32), jax.ShapeDtypeStruct((rows_b, 256), f32)),
        in_specs=[pl.BlockSpec(memory_space=pltpu.VMEM)],
        out_specs=(pl.BlockSpec(memory_space=pltpu.VMEM), pl.BlockSpec(memory_space=pltpu.VMEM)),
        scratch_shapes=[
            pltpu.VMEM((rows, 128), jnp.bfloat16),
            pltpu.VMEM((half, 128), f32),
            pltpu.VMEM((half, 128), f32),
            pltpu.VMEM((3, 3, quarter, 128), f32),
            pltpu.VMEM((3, quarter, 128), f32),
            pltpu.VMEM((3, 3, piece, 128), f32),
            pltpu.VMEM((3, piece, 128), f32),
            pltpu.VMEM((3, 4, piece, 128), f32),
            pltpu.SemaphoreType.DMA((47,)),
            pltpu.SemaphoreType.DMA((47,)),
        ],
        compiler_params=pltpu.CompilerParams(collective_id=0, has_side_effects=True),
    )(flat)
    return out_a.reshape(sums_a.shape), out_b.reshape(sums_b.shape)


def conv_cells(field, kernel):
    shaped = kernel.reshape(3, 3, 3, kernel.shape[1], kernel.shape[2])
    result = lax.conv_general_dilated(
        field[None],
        shaped,
        (1, 1, 1),
        ((0, 0), (1, 1), (1, 1)),
        dimension_numbers=("NCDHW", "DHWIO", "NCDHW"),
        preferred_element_type=jnp.float32,
    )
    return result[0]


def back_cells(padded, kernel):
    flipped = kernel[::-1].transpose(0, 2, 1)
    return conv_cells(padded, flipped)


def kernel_terms(padded, upstream):
    taps, chan_in, chan_out = 27, padded.shape[0], upstream.shape[0]
    start = jnp.zeros((taps, chan_in, chan_out), jnp.float32)
    field = padded.astype(jnp.float32)
    unused, pull = jax.vjp(lambda w: conv_cells(field, w), start)
    return pull(upstream.astype(jnp.float32))[0]


def _terms_a_body(src_ref, up_ref, terms_ref):
    cells = up_ref.shape[1]
    width = src_ref.shape[1]
    plane = width // 4
    side = 32
    spot = lax.broadcasted_iota(jnp.int32, (1, cells), 1)
    column = spot % side
    row = (spot // side) % side
    upstream = up_ref[...]
    field = src_ref[...].astype(jnp.float32)
    for b in range(3):
        for c in range(3):
            shift = (b - 1) * side + (c - 1)
            moved = pltpu.roll(field, (width - shift) % width, 1)
            inside = (column + c - 1 >= 0) & (column + c - 1 < side) & (row + b - 1 >= 0) & (row + b - 1 < side)
            for a in range(3):
                window = moved[:, a * plane : a * plane + cells]
                window = jnp.where(inside, window, 0.0).astype(jnp.bfloat16)
                terms_ref[9 * a + 3 * b + c] = lax.dot_general(
                    window, upstream, (((1,), (1,)), ((), ())), preferred_element_type=jnp.float32
                )


def kernel_terms_flat(source_pad, grad_hidden):
    chan_in, chan_out = source_pad.shape[0], grad_hidden.shape[0]
    return pl.pallas_call(
        _terms_a_body,
        out_shape=jax.ShapeDtypeStruct((27, chan_in, chan_out), jnp.float32),
        in_specs=[pl.BlockSpec(memory_space=pltpu.VMEM)] * 2,
        out_specs=pl.BlockSpec(memory_space=pltpu.VMEM),
    )(source_pad.reshape(chan_in, -1), grad_hidden.reshape(chan_out, -1))


def _back_a_body(pad_ref, w_ref, back_ref):
    cells = back_ref.shape[1]
    plane = pad_ref.shape[1] // 4
    side = 32
    spot = lax.broadcasted_iota(jnp.int32, (1, cells), 1)
    column = spot % side
    row = (spot // side) % side
    back = jnp.zeros((back_ref.shape[0], cells), jnp.float32)
    for b in range(3):
        for c in range(3):
            shift = (b - 1) * side + (c - 1)
            total = jnp.zeros_like(back)
            for a in range(3):
                total = total + jnp.dot(
                    w_ref[9 * a + 3 * b + c],
                    pad_ref[:, (2 - a) * plane : (2 - a) * plane + cells],
                    preferred_element_type=jnp.float32,
                )
            back_in = (column - c + 1 >= 0) & (column - c + 1 < side) & (row - b + 1 >= 0) & (row - b + 1 < side)
            back = back + jnp.where(back_in, pltpu.roll(total, shift % cells, 1), 0.0)
    back_ref[...] = back.astype(back_ref.dtype)


def back_flat(hidden_pad, weight_a, cells):
    chan_in, chan_out = weight_a.shape[1], hidden_pad.shape[0]
    return pl.pallas_call(
        _back_a_body,
        out_shape=jax.ShapeDtypeStruct((chan_in, cells), jnp.bfloat16),
        in_specs=[pl.BlockSpec(memory_space=pltpu.VMEM)] * 2,
        out_specs=pl.BlockSpec(memory_space=pltpu.VMEM),
    )(hidden_pad.reshape(chan_out, -1), weight_a)


def per_device(layer_input, hidden_pre, output_pre, output_grad, weight_a, weight_b):
    side = math.isqrt(layer_input.shape[3])
    half = side // 2
    depth_a = layer_input.shape[2]
    depth_b = depth_a // 2
    source = layer_input[0]
    hidden = hidden_pre[0]
    outer = output_pre[0]
    upstream = output_grad[0]
    chan_in = source.shape[0]
    width_a = hidden.shape[0]
    width_b = outer.shape[0]
    grad_outer = (upstream.astype(jnp.float32) * slopes(outer.astype(jnp.float32))).astype(
        jnp.bfloat16
    )
    hidden_f = hidden.astype(jnp.float32)
    active = jnp.where(hidden_f > 0, hidden_f, negative_slope * hidden_f)
    pooled = (
        active.reshape(width_a, depth_b, 2, half, 2, half, 2)
        .mean(axis=(2, 4, 6))
        .astype(jnp.bfloat16)
    )
    pooled = pooled.reshape(width_a, depth_b, half * half)
    outer_pad = padded_2(grad_outer, (("space", 1),), 1).reshape(width_b, depth_b + 2, half, half)
    pooled_pad = padded_2(pooled, (("space", 1),), 1).reshape(width_a, depth_b + 2, half, half)
    back_b = back_cells(outer_pad, weight_b)
    sums_b = kernel_terms(pooled_pad, grad_outer.reshape(width_b, depth_b, half, half))
    upward = jnp.repeat(jnp.repeat(jnp.repeat(back_b, 2, 1), 2, 2), 2, 3) * 0.125
    upward = upward.reshape(width_a, depth_a * side * side)
    grad_hidden = (upward * slopes(hidden_f.reshape(width_a, depth_a * side * side))).astype(
        jnp.bfloat16
    )
    grad_hidden = grad_hidden.reshape(width_a, depth_a, side * side)
    hidden_pad = padded_2(grad_hidden, (("space", 1),), 1)
    back_a = back_flat(hidden_pad, weight_a, depth_a * side * side)
    source_pad = padded_2(source, (("space", 1),), 1)
    sums_a = kernel_terms_flat(source_pad, grad_hidden)
    input_grad = back_a.astype(jnp.bfloat16).reshape(1, chan_in, depth_a, side * side)
    samples = lax.axis_size("dp")
    planes_a = depth_a * lax.axis_size("space")
    scale_a = 1.0 / math.sqrt(samples * planes_a * side * side)
    scale_b = 1.0 / math.sqrt(samples * (planes_a // 2) * half * half)
    total_a, total_b = all_reduce(sums_a, sums_b, scale_a, scale_b)
    return (input_grad, total_a, total_b)


def solution(mesh):
    in_specs = (
        P("dp", None, "space", None),
        P("dp", None, "space", None),
        P("dp", None, "space", None),
        P("dp", None, "space", None),
        P(),
        P(),
    )
    out_specs = (P("dp", None, "space", None), P(), P())
    return jax.shard_map(
        per_device, mesh=mesh, in_specs=in_specs, out_specs=out_specs, check_vma=False
    )
```

```python
import math

import jax
import jax.numpy as jnp
from jax import lax
from jax.sharding import PartitionSpec as P
from jax.experimental import pallas as pl
from jax.experimental.pallas import tpu as pltpu

negative_slope = 0.3


def padded_2(cells, sides, width):
    for axis, dim in sides:
        count = lax.axis_size(axis)
        ends = count - 1
        head = lax.slice_in_dim(cells, 0, width, axis=dim)
        tail = lax.slice_in_dim(cells, cells.shape[dim] - width, cells.shape[dim], axis=dim)
        cells = jnp.concatenate(
            [
                lax.ppermute(tail, axis, [(i, (i + 1) % count) for i in range(ends)]),
                cells,
                lax.ppermute(head, axis, [((i + 1) % count, i) for i in range(ends)]),
            ],
            axis=dim,
        )
    return cells


def slopes(values):
    return jnp.where(values > 0, jnp.ones_like(values), negative_slope * jnp.ones_like(values))


def window(padded, tap_z, tap_y, tap_x, depth, side):
    planes = padded[:, tap_z : tap_z + depth, :]
    margin = side + 1
    wider = jnp.pad(planes, ((0, 0), (0, 0), (margin, margin)))
    offset = (tap_y - 1) * side + (tap_x - 1)
    piece = wider[:, :, margin + offset : margin + offset + side * side]
    column = jnp.arange(side * side, dtype=jnp.int32) % side + (tap_x - 1)
    inside = (column >= 0) & (column < side)
    piece = jnp.where(inside, piece, jnp.zeros_like(piece))
    return piece.reshape(padded.shape[0], depth * side * side)


def outer_product(left, right):
    return lax.dot_general(
        left, right, (((1,), (1,)), ((), ())), preferred_element_type=jnp.float32
    )


def _all_reduce_kernel(x_ref, o_a, o_b, full, recv_a, acc_a, recv_1, acc_1, recv_2, acc_2, recv_3, sends, recvs):
    rows = x_ref.shape[0]
    half = rows // 2
    part = half // 3
    quarter, piece = part // 4, part // 16
    mesh_id = pl.DeviceIdType.MESH
    dp = lax.axis_index("dp")
    sp = lax.axis_index("space")
    core = dp % 2
    spot = {"x": dp // 2, "y": sp // 4, "z": sp % 4}
    partner = (spot["x"] * 2 + (1 - core), sp)

    def peer(axis, k):
        moved = dict(spot)
        moved[axis] = (spot[axis] + k) % 4
        return (moved["x"] * 2 + core, moved["y"] * 4 + moved["z"])

    orders = (("x", "y", "z"), ("y", "z", "x"), ("z", "x", "y"))
    peers = [partner] + [peer(axis, k) for axis in "xyz" for k in (1, 2, 3)]
    barrier = pltpu.get_barrier_semaphore()
    for other in peers:
        pl.semaphore_signal(barrier, inc=1, device_id=other, device_id_type=mesh_id)
    pl.semaphore_wait(barrier, len(peers))

    def rows_at(start, size):
        return pl.ds(pl.multiple_of(start, 16), size)

    used = [0]

    def exchange(triples):
        copies = []
        for src, dst, other in triples:
            copy = pltpu.make_async_remote_copy(
                src_ref=src,
                dst_ref=dst,
                send_sem=sends.at[used[0]],
                recv_sem=recvs.at[used[0]],
                device_id=other,
                device_id_type=mesh_id,
            )
            used[0] += 1
            copy.start()
            copies.append(copy)
        for copy in copies:
            copy.wait()

    exchange([(x_ref.at[rows_at((1 - core) * half, half)], recv_a, partner)])
    acc_a[...] = x_ref[rows_at(core * half, half), :] + recv_a[...]
    triples = []
    for p, order in enumerate(orders):
        for k in (1, 2, 3):
            block = p * part + ((spot[order[0]] + k) % 4) * quarter
            triples.append((acc_a.at[rows_at(block, quarter)], recv_1.at[p, k - 1], peer(order[0], k)))
    exchange(triples)
    for p, order in enumerate(orders):
        mine = p * part + spot[order[0]] * quarter
        acc_1[p] = acc_a[rows_at(mine, quarter), :] + recv_1[p, 0] + recv_1[p, 1] + recv_1[p, 2]
    triples = []
    for p, order in enumerate(orders):
        for k in (1, 2, 3):
            block = ((spot[order[1]] + k) % 4) * piece
            triples.append((acc_1.at[p, rows_at(block, piece)], recv_2.at[p, k - 1], peer(order[1], k)))
    exchange(triples)
    for p, order in enumerate(orders):
        mine = spot[order[1]] * piece
        recv_3[p, 0] = acc_1[p, rows_at(mine, piece), :] + recv_2[p, 0] + recv_2[p, 1] + recv_2[p, 2]
    exchange([(recv_3.at[p, 0], recv_3.at[p, k], peer(order[2], k)) for p, order in enumerate(orders) for k in (1, 2, 3)])
    spans = []
    for p, order in enumerate(orders):
        last = spot[order[2]]
        total = recv_3[p, last % 4]
        for j in (1, 2, 3):
            total = total + recv_3[p, (last - j + 4) % 4]
        outer = core * half + p * part + spot[order[0]] * quarter
        own = outer + spot[order[1]] * piece
        full[rows_at(own, piece), :] = total.astype(full.dtype)
        spans.append((outer, own, order))
    exchange([(full.at[rows_at(own, piece)], full.at[rows_at(own, piece)], peer(order[1], k)) for outer, own, order in spans for k in (1, 2, 3)])
    exchange([(full.at[rows_at(outer, quarter)], full.at[rows_at(outer, quarter)], peer(order[0], k)) for outer, own, order in spans for k in (1, 2, 3)])
    block = full.at[rows_at(core * half, half)]
    exchange([(block, block, partner)])
    rows_a, rows_b = o_a.shape[0], o_b.shape[0]
    o_a[...] = full[0:rows_a, :].astype(jnp.float32)
    o_b[:, 0:128] = full[rows_a : rows_a + rows_b, :].astype(jnp.float32)
    o_b[:, 128:256] = full[rows_a + rows_b : rows_a + 2 * rows_b, :].astype(jnp.float32)


def all_reduce(sums_a, sums_b, scale_a, scale_b):
    rows_a = sums_a.shape[0] * sums_a.shape[1]
    rows_b = sums_b.shape[0] * sums_b.shape[1]
    wide = sums_b.reshape(rows_b, 256) * scale_b
    flat = jnp.concatenate([sums_a.reshape(rows_a, 128) * scale_a, wide[:, :128], wide[:, 128:]])
    count = flat.shape[0]
    unit = 6 * 16 * 16
    rows = -(-count // unit) * unit
    flat = jnp.pad(flat, ((0, rows - count), (0, 0)))
    half = rows // 2
    part = half // 3
    quarter, piece = part // 4, part // 16
    f32 = jnp.float32
    out_a, out_b = pl.pallas_call(
        _all_reduce_kernel,
        out_shape=(jax.ShapeDtypeStruct((rows_a, 128), f32), jax.ShapeDtypeStruct((rows_b, 256), f32)),
        in_specs=[pl.BlockSpec(memory_space=pltpu.VMEM)],
        out_specs=(pl.BlockSpec(memory_space=pltpu.VMEM), pl.BlockSpec(memory_space=pltpu.VMEM)),
        scratch_shapes=[
            pltpu.VMEM((rows, 128), jnp.bfloat16),
            pltpu.VMEM((half, 128), f32),
            pltpu.VMEM((half, 128), f32),
            pltpu.VMEM((3, 3, quarter, 128), f32),
            pltpu.VMEM((3, quarter, 128), f32),
            pltpu.VMEM((3, 3, piece, 128), f32),
            pltpu.VMEM((3, piece, 128), f32),
            pltpu.VMEM((3, 4, piece, 128), f32),
            pltpu.SemaphoreType.DMA((47,)),
            pltpu.SemaphoreType.DMA((47,)),
        ],
        compiler_params=pltpu.CompilerParams(collective_id=0, has_side_effects=True),
    )(flat)
    return out_a.reshape(sums_a.shape), out_b.reshape(sums_b.shape)


def conv_cells(field, kernel):
    shaped = kernel.reshape(3, 3, 3, kernel.shape[1], kernel.shape[2])
    result = lax.conv_general_dilated(
        field[None],
        shaped,
        (1, 1, 1),
        ((0, 0), (1, 1), (1, 1)),
        dimension_numbers=("NCDHW", "DHWIO", "NCDHW"),
        preferred_element_type=jnp.float32,
    )
    return result[0]


def back_cells(padded, kernel):
    flipped = kernel[::-1].transpose(0, 2, 1)
    return conv_cells(padded, flipped)


def kernel_terms(padded, upstream):
    taps, chan_in, chan_out = 27, padded.shape[0], upstream.shape[0]
    start = jnp.zeros((taps, chan_in, chan_out), jnp.float32)
    field = padded.astype(jnp.float32)
    unused, pull = jax.vjp(lambda w: conv_cells(field, w), start)
    return pull(upstream.astype(jnp.float32))[0]


def _terms_a_body(low_ref, mid_ref, high_ref, up_ref, terms_ref):
    cells = up_ref.shape[1]
    width = 2 * cells
    plane = width // 4
    side = 32
    spot = lax.broadcasted_iota(jnp.int32, (1, cells), 1)
    column = spot % side
    row = (spot // side) % side
    upstream = up_ref[...]
    field = jnp.concatenate([low_ref[...], mid_ref[...], high_ref[...]], axis=1).astype(jnp.float32)
    for b in range(3):
        for c in range(3):
            shift = (b - 1) * side + (c - 1)
            moved = pltpu.roll(field, (width - shift) % width, 1)
            inside = (column + c - 1 >= 0) & (column + c - 1 < side) & (row + b - 1 >= 0) & (row + b - 1 < side)
            for a in range(3):
                window = moved[:, a * plane : a * plane + cells]
                window = jnp.where(inside, window, 0.0).astype(jnp.bfloat16)
                terms_ref[9 * a + 3 * b + c] = lax.dot_general(
                    window, upstream, (((1,), (1,)), ((), ())), preferred_element_type=jnp.float32
                )


def kernel_terms_flat(source, grad_hidden):
    chan_in, chan_out = source.shape[0], grad_hidden.shape[0]
    low, high = halo_planes(source)
    return pl.pallas_call(
        _terms_a_body,
        out_shape=jax.ShapeDtypeStruct((27, chan_in, chan_out), jnp.float32),
        in_specs=[pl.BlockSpec(memory_space=pltpu.VMEM)] * 4,
        out_specs=pl.BlockSpec(memory_space=pltpu.VMEM),
    )(low, source.reshape(chan_in, -1), high, grad_hidden.reshape(chan_out, -1))


def halo_planes(cells):
    count = lax.axis_size("space")
    head = cells[:, 0]
    tail = cells[:, -1]
    low = lax.ppermute(tail, "space", [(i, i + 1) for i in range(count - 1)])
    high = lax.ppermute(head, "space", [(i + 1, i) for i in range(count - 1)])
    return low, high


def _back_a_body(low_ref, mid_ref, high_ref, w_ref, back_ref):
    cells = back_ref.shape[1]
    plane = cells // 2
    padded = jnp.concatenate([low_ref[...], mid_ref[...], high_ref[...]], axis=1)
    side = 32
    spot = lax.broadcasted_iota(jnp.int32, (1, cells), 1)
    column = spot % side
    row = (spot // side) % side
    back = jnp.zeros((back_ref.shape[0], cells), jnp.float32)
    for b in range(3):
        for c in range(3):
            shift = (b - 1) * side + (c - 1)
            total = jnp.zeros_like(back)
            for a in range(3):
                total = total + jnp.dot(
                    w_ref[9 * a + 3 * b + c],
                    padded[:, (2 - a) * plane : (2 - a) * plane + cells],
                    preferred_element_type=jnp.float32,
                )
            back_in = (column - c + 1 >= 0) & (column - c + 1 < side) & (row - b + 1 >= 0) & (row - b + 1 < side)
            back = back + jnp.where(back_in, pltpu.roll(total, shift % cells, 1), 0.0)
    back_ref[...] = back.astype(back_ref.dtype)


def back_flat(grad_hidden, weight_a):
    chan_in, chan_out = weight_a.shape[1], grad_hidden.shape[0]
    cells = grad_hidden.shape[1] * grad_hidden.shape[2]
    low, high = halo_planes(grad_hidden)
    return pl.pallas_call(
        _back_a_body,
        out_shape=jax.ShapeDtypeStruct((chan_in, cells), jnp.bfloat16),
        in_specs=[pl.BlockSpec(memory_space=pltpu.VMEM)] * 4,
        out_specs=pl.BlockSpec(memory_space=pltpu.VMEM),
    )(low, grad_hidden.reshape(chan_out, -1), high, weight_a)


def per_device(layer_input, hidden_pre, output_pre, output_grad, weight_a, weight_b):
    side = math.isqrt(layer_input.shape[3])
    half = side // 2
    depth_a = layer_input.shape[2]
    depth_b = depth_a // 2
    source = layer_input[0]
    hidden = hidden_pre[0]
    outer = output_pre[0]
    upstream = output_grad[0]
    chan_in = source.shape[0]
    width_a = hidden.shape[0]
    width_b = outer.shape[0]
    grad_outer = (upstream.astype(jnp.float32) * slopes(outer.astype(jnp.float32))).astype(
        jnp.bfloat16
    )
    hidden_f = hidden.astype(jnp.float32)
    active = jnp.where(hidden_f > 0, hidden_f, negative_slope * hidden_f)
    pooled = (
        active.reshape(width_a, depth_b, 2, half, 2, half, 2)
        .mean(axis=(2, 4, 6))
        .astype(jnp.bfloat16)
    )
    pooled = pooled.reshape(width_a, depth_b, half * half)
    outer_pad = padded_2(grad_outer, (("space", 1),), 1).reshape(width_b, depth_b + 2, half, half)
    pooled_pad = padded_2(pooled, (("space", 1),), 1).reshape(width_a, depth_b + 2, half, half)
    back_b = back_cells(outer_pad, weight_b)
    sums_b = kernel_terms(pooled_pad, grad_outer.reshape(width_b, depth_b, half, half))
    upward = jnp.repeat(jnp.repeat(jnp.repeat(back_b, 2, 1), 2, 2), 2, 3) * 0.125
    upward = upward.reshape(width_a, depth_a * side * side)
    grad_hidden = (upward * slopes(hidden_f.reshape(width_a, depth_a * side * side))).astype(
        jnp.bfloat16
    )
    grad_hidden = grad_hidden.reshape(width_a, depth_a, side * side)
    back_a = back_flat(grad_hidden, weight_a)
    sums_a = kernel_terms_flat(source, grad_hidden)
    input_grad = back_a.astype(jnp.bfloat16).reshape(1, chan_in, depth_a, side * side)
    samples = lax.axis_size("dp")
    planes_a = depth_a * lax.axis_size("space")
    scale_a = 1.0 / math.sqrt(samples * planes_a * side * side)
    scale_b = 1.0 / math.sqrt(samples * (planes_a // 2) * half * half)
    total_a, total_b = all_reduce(sums_a, sums_b, scale_a, scale_b)
    return (input_grad, total_a, total_b)


def solution(mesh):
    in_specs = (
        P("dp", None, "space", None),
        P("dp", None, "space", None),
        P("dp", None, "space", None),
        P("dp", None, "space", None),
        P(),
        P(),
    )
    out_specs = (P("dp", None, "space", None), P(), P())
    return jax.shard_map(
        per_device, mesh=mesh, in_specs=in_specs, out_specs=out_specs, check_vma=False
    )
```

```python
import math

import jax
import jax.numpy as jnp
from jax import lax
from jax.sharding import PartitionSpec as P
from jax.experimental import pallas as pl
from jax.experimental.pallas import tpu as pltpu

negative_slope = 0.3


def padded_2(cells, sides, width):
    for axis, dim in sides:
        count = lax.axis_size(axis)
        ends = count - 1
        head = lax.slice_in_dim(cells, 0, width, axis=dim)
        tail = lax.slice_in_dim(cells, cells.shape[dim] - width, cells.shape[dim], axis=dim)
        cells = jnp.concatenate(
            [
                lax.ppermute(tail, axis, [(i, (i + 1) % count) for i in range(ends)]),
                cells,
                lax.ppermute(head, axis, [((i + 1) % count, i) for i in range(ends)]),
            ],
            axis=dim,
        )
    return cells


def slopes(values):
    return jnp.where(values > 0, jnp.ones_like(values), negative_slope * jnp.ones_like(values))


def window(padded, tap_z, tap_y, tap_x, depth, side):
    planes = padded[:, tap_z : tap_z + depth, :]
    margin = side + 1
    wider = jnp.pad(planes, ((0, 0), (0, 0), (margin, margin)))
    offset = (tap_y - 1) * side + (tap_x - 1)
    piece = wider[:, :, margin + offset : margin + offset + side * side]
    column = jnp.arange(side * side, dtype=jnp.int32) % side + (tap_x - 1)
    inside = (column >= 0) & (column < side)
    piece = jnp.where(inside, piece, jnp.zeros_like(piece))
    return piece.reshape(padded.shape[0], depth * side * side)


def outer_product(left, right):
    return lax.dot_general(
        left, right, (((1,), (1,)), ((), ())), preferred_element_type=jnp.float32
    )


def _all_reduce_kernel(x_ref, o_a, o_b, full, recv_a, acc_a, recv_1, acc_1, recv_2, acc_2, recv_3, sends, recvs):
    rows = x_ref.shape[0]
    half = rows // 2
    part = half // 3
    quarter, piece = part // 4, part // 16
    mesh_id = pl.DeviceIdType.MESH
    dp = lax.axis_index("dp")
    sp = lax.axis_index("space")
    core = dp % 2
    spot = {"x": dp // 2, "y": sp // 4, "z": sp % 4}
    partner = (spot["x"] * 2 + (1 - core), sp)

    def peer(axis, k):
        moved = dict(spot)
        moved[axis] = (spot[axis] + k) % 4
        return (moved["x"] * 2 + core, moved["y"] * 4 + moved["z"])

    orders = (("x", "y", "z"), ("y", "z", "x"), ("z", "x", "y"))
    peers = [partner] + [peer(axis, k) for axis in "xyz" for k in (1, 2, 3)]
    barrier = pltpu.get_barrier_semaphore()
    for other in peers:
        pl.semaphore_signal(barrier, inc=1, device_id=other, device_id_type=mesh_id)
    pl.semaphore_wait(barrier, len(peers))

    def rows_at(start, size):
        return pl.ds(pl.multiple_of(start, 16), size)

    used = [0]

    def exchange(triples):
        copies = []
        for src, dst, other in triples:
            copy = pltpu.make_async_remote_copy(
                src_ref=src,
                dst_ref=dst,
                send_sem=sends.at[used[0]],
                recv_sem=recvs.at[used[0]],
                device_id=other,
                device_id_type=mesh_id,
            )
            used[0] += 1
            copy.start()
            copies.append(copy)
        for copy in copies:
            copy.wait()

    exchange([(x_ref.at[rows_at((1 - core) * half, half)], recv_a, partner)])
    acc_a[...] = x_ref[rows_at(core * half, half), :] + recv_a[...]
    triples = []
    for p, order in enumerate(orders):
        for k in (1, 2, 3):
            block = p * part + ((spot[order[0]] + k) % 4) * quarter
            triples.append((acc_a.at[rows_at(block, quarter)], recv_1.at[p, k - 1], peer(order[0], k)))
    exchange(triples)
    for p, order in enumerate(orders):
        mine = p * part + spot[order[0]] * quarter
        acc_1[p] = acc_a[rows_at(mine, quarter), :] + recv_1[p, 0] + recv_1[p, 1] + recv_1[p, 2]
    triples = []
    for p, order in enumerate(orders):
        for k in (1, 2, 3):
            block = ((spot[order[1]] + k) % 4) * piece
            triples.append((acc_1.at[p, rows_at(block, piece)], recv_2.at[p, k - 1], peer(order[1], k)))
    exchange(triples)
    for p, order in enumerate(orders):
        mine = spot[order[1]] * piece
        recv_3[p, 0] = acc_1[p, rows_at(mine, piece), :] + recv_2[p, 0] + recv_2[p, 1] + recv_2[p, 2]
    exchange([(recv_3.at[p, 0], recv_3.at[p, k], peer(order[2], k)) for p, order in enumerate(orders) for k in (1, 2, 3)])
    spans = []
    for p, order in enumerate(orders):
        last = spot[order[2]]
        total = recv_3[p, last % 4]
        for j in (1, 2, 3):
            total = total + recv_3[p, (last - j + 4) % 4]
        outer = core * half + p * part + spot[order[0]] * quarter
        own = outer + spot[order[1]] * piece
        full[rows_at(own, piece), :] = total.astype(full.dtype)
        spans.append((outer, own, order))
    exchange([(full.at[rows_at(own, piece)], full.at[rows_at(own, piece)], peer(order[1], k)) for outer, own, order in spans for k in (1, 2, 3)])
    exchange([(full.at[rows_at(outer, quarter)], full.at[rows_at(outer, quarter)], peer(order[0], k)) for outer, own, order in spans for k in (1, 2, 3)])
    block = full.at[rows_at(core * half, half)]
    exchange([(block, block, partner)])
    rows_a, rows_b = o_a.shape[0], o_b.shape[0]
    o_a[...] = full[0:rows_a, :].astype(jnp.float32)
    o_b[:, 0:128] = full[rows_a : rows_a + rows_b, :].astype(jnp.float32)
    o_b[:, 128:256] = full[rows_a + rows_b : rows_a + 2 * rows_b, :].astype(jnp.float32)


def all_reduce(sums_a, sums_b, scale_a, scale_b):
    rows_a = sums_a.shape[0] * sums_a.shape[1]
    rows_b = sums_b.shape[0] * sums_b.shape[1]
    wide = sums_b.reshape(rows_b, 256) * scale_b
    flat = jnp.concatenate([sums_a.reshape(rows_a, 128) * scale_a, wide[:, :128], wide[:, 128:]])
    count = flat.shape[0]
    unit = 6 * 16 * 16
    rows = -(-count // unit) * unit
    flat = jnp.pad(flat, ((0, rows - count), (0, 0)))
    half = rows // 2
    part = half // 3
    quarter, piece = part // 4, part // 16
    f32 = jnp.float32
    out_a, out_b = pl.pallas_call(
        _all_reduce_kernel,
        out_shape=(jax.ShapeDtypeStruct((rows_a, 128), f32), jax.ShapeDtypeStruct((rows_b, 256), f32)),
        in_specs=[pl.BlockSpec(memory_space=pltpu.VMEM)],
        out_specs=(pl.BlockSpec(memory_space=pltpu.VMEM), pl.BlockSpec(memory_space=pltpu.VMEM)),
        scratch_shapes=[
            pltpu.VMEM((rows, 128), jnp.bfloat16),
            pltpu.VMEM((half, 128), f32),
            pltpu.VMEM((half, 128), f32),
            pltpu.VMEM((3, 3, quarter, 128), f32),
            pltpu.VMEM((3, quarter, 128), f32),
            pltpu.VMEM((3, 3, piece, 128), f32),
            pltpu.VMEM((3, piece, 128), f32),
            pltpu.VMEM((3, 4, piece, 128), f32),
            pltpu.SemaphoreType.DMA((47,)),
            pltpu.SemaphoreType.DMA((47,)),
        ],
        compiler_params=pltpu.CompilerParams(collective_id=0, has_side_effects=True),
    )(flat)
    return out_a.reshape(sums_a.shape), out_b.reshape(sums_b.shape)


def conv_cells(field, kernel):
    shaped = kernel.reshape(3, 3, 3, kernel.shape[1], kernel.shape[2])
    result = lax.conv_general_dilated(
        field[None],
        shaped,
        (1, 1, 1),
        ((0, 0), (1, 1), (1, 1)),
        dimension_numbers=("NCDHW", "DHWIO", "NCDHW"),
        preferred_element_type=jnp.float32,
    )
    return result[0]


def back_cells(padded, kernel):
    flipped = kernel[::-1].transpose(0, 2, 1)
    return conv_cells(padded, flipped)


def kernel_terms(padded, upstream):
    taps, chan_in, chan_out = 27, padded.shape[0], upstream.shape[0]
    start = jnp.zeros((taps, chan_in, chan_out), jnp.float32)
    field = padded.astype(jnp.float32)
    unused, pull = jax.vjp(lambda w: conv_cells(field, w), start)
    return pull(upstream.astype(jnp.float32))[0]


def _terms_a_body(src_ref, up_ref, terms_ref):
    cells = up_ref.shape[1]
    width = src_ref.shape[1]
    plane = width // 4
    side = 32
    spot = lax.broadcasted_iota(jnp.int32, (1, cells), 1)
    column = spot % side
    row = (spot // side) % side
    upstream = up_ref[...]
    field = src_ref[...].astype(jnp.float32)
    for b in range(3):
        for c in range(3):
            shift = (b - 1) * side + (c - 1)
            moved = pltpu.roll(field, (width - shift) % width, 1)
            inside = (column + c - 1 >= 0) & (column + c - 1 < side) & (row + b - 1 >= 0) & (row + b - 1 < side)
            for a in range(3):
                window = moved[:, a * plane : a * plane + cells]
                window = jnp.where(inside, window, 0.0).astype(jnp.bfloat16)
                terms_ref[9 * a + 3 * b + c] = lax.dot_general(
                    window, upstream, (((1,), (1,)), ((), ())), preferred_element_type=jnp.float32
                )


def kernel_terms_flat(source_pad, grad_hidden):
    chan_in, chan_out = source_pad.shape[0], grad_hidden.shape[0]
    return pl.pallas_call(
        _terms_a_body,
        out_shape=jax.ShapeDtypeStruct((27, chan_in, chan_out), jnp.float32),
        in_specs=[pl.BlockSpec(memory_space=pltpu.VMEM)] * 2,
        out_specs=pl.BlockSpec(memory_space=pltpu.VMEM),
    )(source_pad.reshape(chan_in, -1), grad_hidden.reshape(chan_out, -1))


def _back_a_body(pad_ref, w_ref, back_ref):
    cells = back_ref.shape[1]
    plane = pad_ref.shape[1] // 4
    side = 32
    spot = lax.broadcasted_iota(jnp.int32, (1, cells), 1)
    column = spot % side
    row = (spot // side) % side
    back = jnp.zeros((back_ref.shape[0], cells), jnp.float32)
    for b in range(3):
        for c in range(3):
            shift = (b - 1) * side + (c - 1)
            total = jnp.zeros_like(back)
            for a in range(3):
                total = total + jnp.dot(
                    w_ref[9 * a + 3 * b + c],
                    pad_ref[:, (2 - a) * plane : (2 - a) * plane + cells],
                    preferred_element_type=jnp.float32,
                )
            back_in = (column - c + 1 >= 0) & (column - c + 1 < side) & (row - b + 1 >= 0) & (row - b + 1 < side)
            back = back + jnp.where(back_in, pltpu.roll(total, shift % cells, 1), 0.0)
    back_ref[...] = back.astype(back_ref.dtype)


def back_flat(hidden_pad, weight_a, cells):
    chan_in, chan_out = weight_a.shape[1], hidden_pad.shape[0]
    return pl.pallas_call(
        _back_a_body,
        out_shape=jax.ShapeDtypeStruct((chan_in, cells), jnp.bfloat16),
        in_specs=[pl.BlockSpec(memory_space=pltpu.VMEM)] * 2,
        out_specs=pl.BlockSpec(memory_space=pltpu.VMEM),
    )(hidden_pad.reshape(chan_out, -1), weight_a)


def per_device(layer_input, hidden_pre, output_pre, output_grad, weight_a, weight_b):
    side = math.isqrt(layer_input.shape[3])
    half = side // 2
    depth_a = layer_input.shape[2]
    depth_b = depth_a // 2
    source = layer_input[0]
    hidden = hidden_pre[0]
    outer = output_pre[0]
    upstream = output_grad[0]
    chan_in = source.shape[0]
    width_a = hidden.shape[0]
    width_b = outer.shape[0]
    grad_outer = (upstream.astype(jnp.float32) * slopes(outer.astype(jnp.float32))).astype(
        jnp.bfloat16
    )
    hidden_f = hidden.astype(jnp.float32)
    active = jnp.where(hidden_f > 0, hidden_f, negative_slope * hidden_f)
    pooled = (
        active.reshape(width_a, depth_b, 2, half, 2, half, 2)
        .mean(axis=(2, 4, 6))
        .astype(jnp.bfloat16)
    )
    pooled = pooled.reshape(width_a, depth_b, half * half)
    outer_pad = padded_2(grad_outer, (("space", 1),), 1).reshape(width_b, depth_b + 2, half, half)
    pooled_pad = padded_2(pooled, (("space", 1),), 1).reshape(width_a, depth_b + 2, half, half)
    back_b = back_cells(outer_pad, weight_b)
    sums_b = kernel_terms(pooled_pad, grad_outer.reshape(width_b, depth_b, half, half))
    upward = jnp.repeat(jnp.repeat(jnp.repeat(back_b, 2, 1), 2, 2), 2, 3) * 0.125
    upward = upward.reshape(width_a, depth_a * side * side)
    grad_hidden = (upward * slopes(hidden_f.reshape(width_a, depth_a * side * side))).astype(
        jnp.bfloat16
    )
    grad_hidden = grad_hidden.reshape(width_a, depth_a, side * side)
    hidden_pad = padded_2(grad_hidden, (("space", 1),), 1)
    back_a = back_flat(hidden_pad, weight_a, depth_a * side * side)
    source_pad = padded_2(source, (("space", 1),), 1)
    sums_a = kernel_terms_flat(source_pad, grad_hidden)
    input_grad = back_a.astype(jnp.bfloat16).reshape(1, chan_in, depth_a, side * side)
    samples = lax.axis_size("dp")
    planes_a = depth_a * lax.axis_size("space")
    scale_a = 1.0 / math.sqrt(samples * planes_a * side * side)
    scale_b = 1.0 / math.sqrt(samples * (planes_a // 2) * half * half)
    sums_a, sums_b, input_grad = lax.optimization_barrier((sums_a, sums_b, input_grad))
    total_a, total_b = all_reduce(sums_a, sums_b, scale_a, scale_b)
    return (input_grad, total_a, total_b)


def solution(mesh):
    in_specs = (
        P("dp", None, "space", None),
        P("dp", None, "space", None),
        P("dp", None, "space", None),
        P("dp", None, "space", None),
        P(),
        P(),
    )
    out_specs = (P("dp", None, "space", None), P(), P())
    return jax.shard_map(
        per_device, mesh=mesh, in_specs=in_specs, out_specs=out_specs, check_vma=False
    )
```

```python
import math

import jax
import jax.numpy as jnp
from jax import lax
from jax.sharding import PartitionSpec as P
from jax.experimental import pallas as pl
from jax.experimental.pallas import tpu as pltpu

negative_slope = 0.3


def padded_2(cells, sides, width):
    for axis, dim in sides:
        count = lax.axis_size(axis)
        ends = count - 1
        head = lax.slice_in_dim(cells, 0, width, axis=dim)
        tail = lax.slice_in_dim(cells, cells.shape[dim] - width, cells.shape[dim], axis=dim)
        cells = jnp.concatenate(
            [
                lax.ppermute(tail, axis, [(i, (i + 1) % count) for i in range(ends)]),
                cells,
                lax.ppermute(head, axis, [((i + 1) % count, i) for i in range(ends)]),
            ],
            axis=dim,
        )
    return cells


def slopes(values):
    return jnp.where(values > 0, jnp.ones_like(values), negative_slope * jnp.ones_like(values))


def window(padded, tap_z, tap_y, tap_x, depth, side):
    planes = padded[:, tap_z : tap_z + depth, :]
    margin = side + 1
    wider = jnp.pad(planes, ((0, 0), (0, 0), (margin, margin)))
    offset = (tap_y - 1) * side + (tap_x - 1)
    piece = wider[:, :, margin + offset : margin + offset + side * side]
    column = jnp.arange(side * side, dtype=jnp.int32) % side + (tap_x - 1)
    inside = (column >= 0) & (column < side)
    piece = jnp.where(inside, piece, jnp.zeros_like(piece))
    return piece.reshape(padded.shape[0], depth * side * side)


def outer_product(left, right):
    return lax.dot_general(
        left, right, (((1,), (1,)), ((), ())), preferred_element_type=jnp.float32
    )


def _all_reduce_kernel(x_ref, o_a, o_b, full, recv_a, acc_a, recv_1, acc_1, recv_2, acc_2, recv_3, sends, recvs):
    rows = x_ref.shape[0]
    half = rows // 2
    part = half // 3
    quarter, piece = part // 4, part // 16
    mesh_id = pl.DeviceIdType.MESH
    dp = lax.axis_index("dp")
    sp = lax.axis_index("space")
    core = dp % 2
    spot = {"x": dp // 2, "y": sp // 4, "z": sp % 4}
    partner = (spot["x"] * 2 + (1 - core), sp)

    def peer(axis, k):
        moved = dict(spot)
        moved[axis] = (spot[axis] + k) % 4
        return (moved["x"] * 2 + core, moved["y"] * 4 + moved["z"])

    orders = (("x", "y", "z"), ("y", "z", "x"), ("z", "x", "y"))
    peers = [partner] + [peer(axis, k) for axis in "xyz" for k in (1, 2, 3)]
    barrier = pltpu.get_barrier_semaphore()
    for other in peers:
        pl.semaphore_signal(barrier, inc=1, device_id=other, device_id_type=mesh_id)
    pl.semaphore_wait(barrier, len(peers))

    def rows_at(start, size):
        return pl.ds(pl.multiple_of(start, 16), size)

    used = [0]

    def exchange(triples):
        copies = []
        for src, dst, other in triples:
            copy = pltpu.make_async_remote_copy(
                src_ref=src,
                dst_ref=dst,
                send_sem=sends.at[used[0]],
                recv_sem=recvs.at[used[0]],
                device_id=other,
                device_id_type=mesh_id,
            )
            used[0] += 1
            copy.start()
            copies.append(copy)
        for copy in copies:
            copy.wait()

    exchange([(x_ref.at[rows_at((1 - core) * half, half)], recv_a, partner)])
    acc_a[...] = x_ref[rows_at(core * half, half), :] + recv_a[...]
    triples = []
    for p, order in enumerate(orders):
        for k in (1, 2, 3):
            block = p * part + ((spot[order[0]] + k) % 4) * quarter
            triples.append((acc_a.at[rows_at(block, quarter)], recv_1.at[p, k - 1], peer(order[0], k)))
    exchange(triples)
    for p, order in enumerate(orders):
        mine = p * part + spot[order[0]] * quarter
        acc_1[p] = acc_a[rows_at(mine, quarter), :] + recv_1[p, 0] + recv_1[p, 1] + recv_1[p, 2]
    triples = []
    for p, order in enumerate(orders):
        for k in (1, 2, 3):
            block = ((spot[order[1]] + k) % 4) * piece
            triples.append((acc_1.at[p, rows_at(block, piece)], recv_2.at[p, k - 1], peer(order[1], k)))
    exchange(triples)
    for p, order in enumerate(orders):
        mine = spot[order[1]] * piece
        recv_3[p, 0] = acc_1[p, rows_at(mine, piece), :] + recv_2[p, 0] + recv_2[p, 1] + recv_2[p, 2]
    exchange([(recv_3.at[p, 0], recv_3.at[p, k], peer(order[2], k)) for p, order in enumerate(orders) for k in (1, 2, 3)])
    spans = []
    for p, order in enumerate(orders):
        last = spot[order[2]]
        total = recv_3[p, last % 4]
        for j in (1, 2, 3):
            total = total + recv_3[p, (last - j + 4) % 4]
        outer = core * half + p * part + spot[order[0]] * quarter
        own = outer + spot[order[1]] * piece
        full[rows_at(own, piece), :] = total.astype(full.dtype)
        spans.append((outer, own, order))
    exchange([(full.at[rows_at(own, piece)], full.at[rows_at(own, piece)], peer(order[1], k)) for outer, own, order in spans for k in (1, 2, 3)])
    exchange([(full.at[rows_at(outer, quarter)], full.at[rows_at(outer, quarter)], peer(order[0], k)) for outer, own, order in spans for k in (1, 2, 3)])
    block = full.at[rows_at(core * half, half)]
    exchange([(block, block, partner)])
    rows_a, rows_b = o_a.shape[0], o_b.shape[0]
    o_a[...] = full[0:rows_a, :].astype(jnp.float32)
    o_b[:, 0:128] = full[rows_a : rows_a + rows_b, :].astype(jnp.float32)
    o_b[:, 128:256] = full[rows_a + rows_b : rows_a + 2 * rows_b, :].astype(jnp.float32)


def all_reduce(sums_a, sums_b, scale_a, scale_b):
    rows_a = sums_a.shape[0] * sums_a.shape[1]
    rows_b = sums_b.shape[0] * sums_b.shape[1]
    wide = sums_b.reshape(rows_b, 256) * scale_b
    flat = jnp.concatenate([sums_a.reshape(rows_a, 128) * scale_a, wide[:, :128], wide[:, 128:]])
    count = flat.shape[0]
    unit = 6 * 16 * 16
    rows = -(-count // unit) * unit
    flat = jnp.pad(flat, ((0, rows - count), (0, 0)))
    half = rows // 2
    part = half // 3
    quarter, piece = part // 4, part // 16
    f32 = jnp.float32
    out_a, out_b = pl.pallas_call(
        _all_reduce_kernel,
        out_shape=(jax.ShapeDtypeStruct((rows_a, 128), f32), jax.ShapeDtypeStruct((rows_b, 256), f32)),
        in_specs=[pl.BlockSpec(memory_space=pltpu.VMEM)],
        out_specs=(pl.BlockSpec(memory_space=pltpu.VMEM), pl.BlockSpec(memory_space=pltpu.VMEM)),
        scratch_shapes=[
            pltpu.VMEM((rows, 128), jnp.bfloat16),
            pltpu.VMEM((half, 128), f32),
            pltpu.VMEM((half, 128), f32),
            pltpu.VMEM((3, 3, quarter, 128), f32),
            pltpu.VMEM((3, quarter, 128), f32),
            pltpu.VMEM((3, 3, piece, 128), f32),
            pltpu.VMEM((3, piece, 128), f32),
            pltpu.VMEM((3, 4, piece, 128), f32),
            pltpu.SemaphoreType.DMA((47,)),
            pltpu.SemaphoreType.DMA((47,)),
        ],
        compiler_params=pltpu.CompilerParams(collective_id=0, has_side_effects=True),
    )(flat)
    return out_a.reshape(sums_a.shape), out_b.reshape(sums_b.shape)


def conv_cells(field, kernel):
    shaped = kernel.reshape(3, 3, 3, kernel.shape[1], kernel.shape[2])
    result = lax.conv_general_dilated(
        field[None],
        shaped,
        (1, 1, 1),
        ((0, 0), (1, 1), (1, 1)),
        dimension_numbers=("NCDHW", "DHWIO", "NCDHW"),
        preferred_element_type=jnp.float32,
    )
    return result[0]


def back_cells(padded, kernel):
    flipped = kernel[::-1].transpose(0, 2, 1)
    return conv_cells(padded, flipped)


def kernel_terms(padded, upstream):
    taps, chan_in, chan_out = 27, padded.shape[0], upstream.shape[0]
    start = jnp.zeros((taps, chan_in, chan_out), jnp.float32)
    field = padded.astype(jnp.float32)
    unused, pull = jax.vjp(lambda w: conv_cells(field, w), start)
    return pull(upstream.astype(jnp.float32))[0]


def _terms_a_body(src_ref, up_ref, terms_ref):
    cells = up_ref.shape[1]
    width = src_ref.shape[1]
    plane = width // 4
    side = 32
    spot = lax.broadcasted_iota(jnp.int32, (1, cells), 1)
    column = spot % side
    row = (spot // side) % side
    upstream = up_ref[...]
    field = src_ref[...].astype(jnp.float32)
    for b in range(3):
        for c in range(3):
            shift = (b - 1) * side + (c - 1)
            moved = pltpu.roll(field, (width - shift) % width, 1)
            inside = (column + c - 1 >= 0) & (column + c - 1 < side) & (row + b - 1 >= 0) & (row + b - 1 < side)
            for a in range(3):
                window = moved[:, a * plane : a * plane + cells]
                window = jnp.where(inside, window, 0.0).astype(jnp.bfloat16)
                terms_ref[9 * a + 3 * b + c] = lax.dot_general(
                    window, upstream, (((1,), (1,)), ((), ())), preferred_element_type=jnp.float32
                )


def kernel_terms_flat(source_pad, grad_hidden):
    chan_in, chan_out = source_pad.shape[0], grad_hidden.shape[0]
    return pl.pallas_call(
        _terms_a_body,
        out_shape=jax.ShapeDtypeStruct((27, chan_in, chan_out), jnp.float32),
        in_specs=[pl.BlockSpec(memory_space=pltpu.VMEM)] * 2,
        out_specs=pl.BlockSpec(memory_space=pltpu.VMEM),
    )(source_pad.reshape(chan_in, -1), grad_hidden.reshape(chan_out, -1))


def _back_a_body(pad_ref, w_ref, back_ref):
    cells = back_ref.shape[1] * back_ref.shape[2]
    plane = pad_ref.shape[1] // 4
    side = 32
    spot = lax.broadcasted_iota(jnp.int32, (1, cells), 1)
    column = spot % side
    row = (spot // side) % side
    back = jnp.zeros((back_ref.shape[0], cells), jnp.float32)
    for b in range(3):
        for c in range(3):
            shift = (b - 1) * side + (c - 1)
            total = jnp.zeros_like(back)
            for a in range(3):
                total = total + jnp.dot(
                    w_ref[9 * a + 3 * b + c],
                    pad_ref[:, (2 - a) * plane : (2 - a) * plane + cells],
                    preferred_element_type=jnp.float32,
                )
            back_in = (column - c + 1 >= 0) & (column - c + 1 < side) & (row - b + 1 >= 0) & (row - b + 1 < side)
            back = back + jnp.where(back_in, pltpu.roll(total, shift % cells, 1), 0.0)
    plane = back_ref.shape[2]
    for z in range(back_ref.shape[1]):
        back_ref[:, z, :] = back[:, z * plane : (z + 1) * plane].astype(back_ref.dtype)


def back_flat(hidden_pad, weight_a, cells):
    chan_in, chan_out = weight_a.shape[1], hidden_pad.shape[0]
    return pl.pallas_call(
        _back_a_body,
        out_shape=jax.ShapeDtypeStruct((chan_in, cells // 1024, 1024), jnp.bfloat16),
        in_specs=[pl.BlockSpec(memory_space=pltpu.VMEM)] * 2,
        out_specs=pl.BlockSpec(memory_space=pltpu.VMEM),
    )(hidden_pad.reshape(chan_out, -1), weight_a)


def per_device(layer_input, hidden_pre, output_pre, output_grad, weight_a, weight_b):
    side = math.isqrt(layer_input.shape[3])
    half = side // 2
    depth_a = layer_input.shape[2]
    depth_b = depth_a // 2
    source = layer_input[0]
    hidden = hidden_pre[0]
    outer = output_pre[0]
    upstream = output_grad[0]
    chan_in = source.shape[0]
    width_a = hidden.shape[0]
    width_b = outer.shape[0]
    grad_outer = (upstream.astype(jnp.float32) * slopes(outer.astype(jnp.float32))).astype(
        jnp.bfloat16
    )
    hidden_f = hidden.astype(jnp.float32)
    active = jnp.where(hidden_f > 0, hidden_f, negative_slope * hidden_f)
    pooled = (
        active.reshape(width_a, depth_b, 2, half, 2, half, 2)
        .mean(axis=(2, 4, 6))
        .astype(jnp.bfloat16)
    )
    pooled = pooled.reshape(width_a, depth_b, half * half)
    outer_pad = padded_2(grad_outer, (("space", 1),), 1).reshape(width_b, depth_b + 2, half, half)
    pooled_pad = padded_2(pooled, (("space", 1),), 1).reshape(width_a, depth_b + 2, half, half)
    back_b = back_cells(outer_pad, weight_b)
    sums_b = kernel_terms(pooled_pad, grad_outer.reshape(width_b, depth_b, half, half))
    upward = jnp.repeat(jnp.repeat(jnp.repeat(back_b, 2, 1), 2, 2), 2, 3) * 0.125
    upward = upward.reshape(width_a, depth_a * side * side)
    grad_hidden = (upward * slopes(hidden_f.reshape(width_a, depth_a * side * side))).astype(
        jnp.bfloat16
    )
    grad_hidden = grad_hidden.reshape(width_a, depth_a, side * side)
    hidden_pad = padded_2(grad_hidden, (("space", 1),), 1)
    back_a = back_flat(hidden_pad, weight_a, depth_a * side * side)
    source_pad = padded_2(source, (("space", 1),), 1)
    sums_a = kernel_terms_flat(source_pad, grad_hidden)
    input_grad = back_a.astype(jnp.bfloat16).reshape(1, chan_in, depth_a, side * side)
    samples = lax.axis_size("dp")
    planes_a = depth_a * lax.axis_size("space")
    scale_a = 1.0 / math.sqrt(samples * planes_a * side * side)
    scale_b = 1.0 / math.sqrt(samples * (planes_a // 2) * half * half)
    total_a, total_b = all_reduce(sums_a, sums_b, scale_a, scale_b)
    return (input_grad, total_a, total_b)


def solution(mesh):
    in_specs = (
        P("dp", None, "space", None),
        P("dp", None, "space", None),
        P("dp", None, "space", None),
        P("dp", None, "space", None),
        P(),
        P(),
    )
    out_specs = (P("dp", None, "space", None), P(), P())
    return jax.shard_map(
        per_device, mesh=mesh, in_specs=in_specs, out_specs=out_specs, check_vma=False
    )
```

```python
import math

import jax
import jax.numpy as jnp
from jax import lax
from jax.sharding import PartitionSpec as P
from jax.experimental import pallas as pl
from jax.experimental.pallas import tpu as pltpu

negative_slope = 0.3


def padded_2(cells, sides, width):
    for axis, dim in sides:
        count = lax.axis_size(axis)
        ends = count - 1
        head = lax.slice_in_dim(cells, 0, width, axis=dim)
        tail = lax.slice_in_dim(cells, cells.shape[dim] - width, cells.shape[dim], axis=dim)
        cells = jnp.concatenate(
            [
                lax.ppermute(tail, axis, [(i, (i + 1) % count) for i in range(ends)]),
                cells,
                lax.ppermute(head, axis, [((i + 1) % count, i) for i in range(ends)]),
            ],
            axis=dim,
        )
    return cells


def slopes(values):
    return jnp.where(values > 0, jnp.ones_like(values), negative_slope * jnp.ones_like(values))


def window(padded, tap_z, tap_y, tap_x, depth, side):
    planes = padded[:, tap_z : tap_z + depth, :]
    margin = side + 1
    wider = jnp.pad(planes, ((0, 0), (0, 0), (margin, margin)))
    offset = (tap_y - 1) * side + (tap_x - 1)
    piece = wider[:, :, margin + offset : margin + offset + side * side]
    column = jnp.arange(side * side, dtype=jnp.int32) % side + (tap_x - 1)
    inside = (column >= 0) & (column < side)
    piece = jnp.where(inside, piece, jnp.zeros_like(piece))
    return piece.reshape(padded.shape[0], depth * side * side)


def outer_product(left, right):
    return lax.dot_general(
        left, right, (((1,), (1,)), ((), ())), preferred_element_type=jnp.float32
    )


def _all_reduce_kernel(x_ref, o_a, o_b, full, recv_a, acc_a, recv_1, acc_1, recv_2, acc_2, recv_3, sends, recvs):
    rows = x_ref.shape[0]
    half = rows // 2
    part = half // 3
    quarter, piece = part // 4, part // 16
    mesh_id = pl.DeviceIdType.MESH
    dp = lax.axis_index("dp")
    sp = lax.axis_index("space")
    core = dp % 2
    spot = {"x": dp // 2, "y": sp // 4, "z": sp % 4}
    partner = (spot["x"] * 2 + (1 - core), sp)

    def peer(axis, k):
        moved = dict(spot)
        moved[axis] = (spot[axis] + k) % 4
        return (moved["x"] * 2 + core, moved["y"] * 4 + moved["z"])

    orders = (("x", "y", "z"), ("y", "z", "x"), ("z", "x", "y"))
    peers = [partner] + [peer(axis, k) for axis in "xyz" for k in (1, 2, 3)]
    barrier = pltpu.get_barrier_semaphore()
    for other in peers:
        pl.semaphore_signal(barrier, inc=1, device_id=other, device_id_type=mesh_id)
    pl.semaphore_wait(barrier, len(peers))

    def rows_at(start, size):
        return pl.ds(pl.multiple_of(start, 16), size)

    used = [0]

    def exchange(triples):
        copies = []
        for src, dst, other in triples:
            copy = pltpu.make_async_remote_copy(
                src_ref=src,
                dst_ref=dst,
                send_sem=sends.at[used[0]],
                recv_sem=recvs.at[used[0]],
                device_id=other,
                device_id_type=mesh_id,
            )
            used[0] += 1
            copy.start()
            copies.append(copy)
        for copy in copies:
            copy.wait()

    exchange([(x_ref.at[rows_at((1 - core) * half, half)], recv_a, partner)])
    acc_a[...] = x_ref[rows_at(core * half, half), :] + recv_a[...]
    triples = []
    for p, order in enumerate(orders):
        for k in (1, 2, 3):
            block = p * part + ((spot[order[0]] + k) % 4) * quarter
            triples.append((acc_a.at[rows_at(block, quarter)], recv_1.at[p, k - 1], peer(order[0], k)))
    exchange(triples)
    for p, order in enumerate(orders):
        mine = p * part + spot[order[0]] * quarter
        acc_1[p] = acc_a[rows_at(mine, quarter), :] + recv_1[p, 0] + recv_1[p, 1] + recv_1[p, 2]
    triples = []
    for p, order in enumerate(orders):
        for k in (1, 2, 3):
            block = ((spot[order[1]] + k) % 4) * piece
            triples.append((acc_1.at[p, rows_at(block, piece)], recv_2.at[p, k - 1], peer(order[1], k)))
    exchange(triples)
    for p, order in enumerate(orders):
        mine = spot[order[1]] * piece
        recv_3[p, 0] = acc_1[p, rows_at(mine, piece), :] + recv_2[p, 0] + recv_2[p, 1] + recv_2[p, 2]
    exchange([(recv_3.at[p, 0], recv_3.at[p, k], peer(order[2], k)) for p, order in enumerate(orders) for k in (1, 2, 3)])
    spans = []
    for p, order in enumerate(orders):
        last = spot[order[2]]
        total = recv_3[p, last % 4]
        for j in (1, 2, 3):
            total = total + recv_3[p, (last - j + 4) % 4]
        outer = core * half + p * part + spot[order[0]] * quarter
        own = outer + spot[order[1]] * piece
        full[rows_at(own, piece), :] = total.astype(full.dtype)
        spans.append((outer, own, order))
    exchange([(full.at[rows_at(own, piece)], full.at[rows_at(own, piece)], peer(order[1], k)) for outer, own, order in spans for k in (1, 2, 3)])
    exchange([(full.at[rows_at(outer, quarter)], full.at[rows_at(outer, quarter)], peer(order[0], k)) for outer, own, order in spans for k in (1, 2, 3)])
    block = full.at[rows_at(core * half, half)]
    exchange([(block, block, partner)])
    rows_a, rows_b = o_a.shape[0], o_b.shape[0]
    o_a[...] = full[0:rows_a, :].astype(jnp.float32)
    o_b[:, 0:128] = full[rows_a : rows_a + rows_b, :].astype(jnp.float32)
    o_b[:, 128:256] = full[rows_a + rows_b : rows_a + 2 * rows_b, :].astype(jnp.float32)


def all_reduce(sums_a, sums_b, scale_a, scale_b):
    rows_a = sums_a.shape[0] * sums_a.shape[1]
    rows_b = sums_b.shape[0] * sums_b.shape[1]
    wide = sums_b.reshape(rows_b, 256) * scale_b
    flat = jnp.concatenate([sums_a.reshape(rows_a, 128) * scale_a, wide[:, :128], wide[:, 128:]])
    count = flat.shape[0]
    unit = 6 * 16 * 16
    rows = -(-count // unit) * unit
    flat = jnp.pad(flat, ((0, rows - count), (0, 0)))
    half = rows // 2
    part = half // 3
    quarter, piece = part // 4, part // 16
    f32 = jnp.float32
    out_a, out_b = pl.pallas_call(
        _all_reduce_kernel,
        out_shape=(jax.ShapeDtypeStruct((rows_a, 128), f32), jax.ShapeDtypeStruct((rows_b, 256), f32)),
        in_specs=[pl.BlockSpec(memory_space=pltpu.VMEM)],
        out_specs=(pl.BlockSpec(memory_space=pltpu.VMEM), pl.BlockSpec(memory_space=pltpu.VMEM)),
        scratch_shapes=[
            pltpu.VMEM((rows, 128), jnp.bfloat16),
            pltpu.VMEM((half, 128), f32),
            pltpu.VMEM((half, 128), f32),
            pltpu.VMEM((3, 3, quarter, 128), f32),
            pltpu.VMEM((3, quarter, 128), f32),
            pltpu.VMEM((3, 3, piece, 128), f32),
            pltpu.VMEM((3, piece, 128), f32),
            pltpu.VMEM((3, 4, piece, 128), f32),
            pltpu.SemaphoreType.DMA((47,)),
            pltpu.SemaphoreType.DMA((47,)),
        ],
        compiler_params=pltpu.CompilerParams(collective_id=0, has_side_effects=True),
    )(flat)
    return out_a.reshape(sums_a.shape), out_b.reshape(sums_b.shape)


def conv_cells(field, kernel):
    shaped = kernel.reshape(3, 3, 3, kernel.shape[1], kernel.shape[2])
    result = lax.conv_general_dilated(
        field[None],
        shaped,
        (1, 1, 1),
        ((0, 0), (1, 1), (1, 1)),
        dimension_numbers=("NCDHW", "DHWIO", "NCDHW"),
        preferred_element_type=jnp.float32,
    )
    return result[0]


def back_cells(padded, kernel):
    flipped = kernel[::-1].transpose(0, 2, 1)
    return conv_cells(padded, flipped)


def kernel_terms(padded, upstream):
    taps, chan_in, chan_out = 27, padded.shape[0], upstream.shape[0]
    start = jnp.zeros((taps, chan_in, chan_out), jnp.float32)
    field = padded.astype(jnp.float32)
    unused, pull = jax.vjp(lambda w: conv_cells(field, w), start)
    return pull(upstream.astype(jnp.float32))[0]


def _terms_a_body(src_ref, up_ref, terms_ref):
    cells = up_ref.shape[1]
    width = src_ref.shape[1]
    plane = width // 4
    side = 32
    spot = lax.broadcasted_iota(jnp.int32, (1, cells), 1)
    column = spot % side
    row = (spot // side) % side
    upstream = up_ref[...]
    field = src_ref[...].astype(jnp.float32)
    for b in range(3):
        for c in range(3):
            shift = (b - 1) * side + (c - 1)
            moved = pltpu.roll(field, (width - shift) % width, 1)
            inside = (column + c - 1 >= 0) & (column + c - 1 < side) & (row + b - 1 >= 0) & (row + b - 1 < side)
            for a in range(3):
                window = moved[:, a * plane : a * plane + cells]
                window = jnp.where(inside, window, 0.0).astype(jnp.bfloat16)
                terms_ref[9 * a + 3 * b + c] = lax.dot_general(
                    window, upstream, (((1,), (1,)), ((), ())), preferred_element_type=jnp.float32
                )


def kernel_terms_flat(source_pad, grad_hidden):
    chan_in, chan_out = source_pad.shape[0], grad_hidden.shape[0]
    return pl.pallas_call(
        _terms_a_body,
        out_shape=jax.ShapeDtypeStruct((27, chan_in, chan_out), jnp.float32),
        in_specs=[pl.BlockSpec(memory_space=pltpu.VMEM)] * 2,
        out_specs=pl.BlockSpec(memory_space=pltpu.VMEM),
    )(source_pad.reshape(chan_in, -1), grad_hidden.reshape(chan_out, -1))


def _back_a_body(low_ref, mid_ref, high_ref, w_ref, back_ref):
    cells = back_ref.shape[1] * back_ref.shape[2]
    plane = back_ref.shape[2]
    padded = jnp.concatenate([low_ref[...], mid_ref[...], high_ref[...]], axis=1)
    side = 32
    spot = lax.broadcasted_iota(jnp.int32, (1, cells), 1)
    column = spot % side
    row = (spot // side) % side
    back = jnp.zeros((back_ref.shape[0], cells), jnp.float32)
    for b in range(3):
        for c in range(3):
            shift = (b - 1) * side + (c - 1)
            total = jnp.zeros_like(back)
            for a in range(3):
                total = total + jnp.dot(
                    w_ref[9 * a + 3 * b + c],
                    padded[:, (2 - a) * plane : (2 - a) * plane + cells],
                    preferred_element_type=jnp.float32,
                )
            back_in = (column - c + 1 >= 0) & (column - c + 1 < side) & (row - b + 1 >= 0) & (row - b + 1 < side)
            back = back + jnp.where(back_in, pltpu.roll(total, shift % cells, 1), 0.0)
    plane = back_ref.shape[2]
    for z in range(back_ref.shape[1]):
        back_ref[:, z, :] = back[:, z * plane : (z + 1) * plane].astype(back_ref.dtype)


def back_flat(grad_hidden, weight_a):
    chan_in, chan_out = weight_a.shape[1], grad_hidden.shape[0]
    count = lax.axis_size("space")
    low = lax.ppermute(grad_hidden[:, -1], "space", [(i, i + 1) for i in range(count - 1)])
    high = lax.ppermute(grad_hidden[:, 0], "space", [(i + 1, i) for i in range(count - 1)])
    return pl.pallas_call(
        _back_a_body,
        out_shape=jax.ShapeDtypeStruct((chan_in,) + grad_hidden.shape[1:], jnp.bfloat16),
        in_specs=[pl.BlockSpec(memory_space=pltpu.VMEM)] * 4,
        out_specs=pl.BlockSpec(memory_space=pltpu.VMEM),
    )(low, grad_hidden.reshape(chan_out, -1), high, weight_a)


def per_device(layer_input, hidden_pre, output_pre, output_grad, weight_a, weight_b):
    side = math.isqrt(layer_input.shape[3])
    half = side // 2
    depth_a = layer_input.shape[2]
    depth_b = depth_a // 2
    source = layer_input[0]
    hidden = hidden_pre[0]
    outer = output_pre[0]
    upstream = output_grad[0]
    chan_in = source.shape[0]
    width_a = hidden.shape[0]
    width_b = outer.shape[0]
    grad_outer = (upstream.astype(jnp.float32) * slopes(outer.astype(jnp.float32))).astype(
        jnp.bfloat16
    )
    hidden_f = hidden.astype(jnp.float32)
    active = jnp.where(hidden_f > 0, hidden_f, negative_slope * hidden_f)
    pooled = (
        active.reshape(width_a, depth_b, 2, half, 2, half, 2)
        .mean(axis=(2, 4, 6))
        .astype(jnp.bfloat16)
    )
    pooled = pooled.reshape(width_a, depth_b, half * half)
    outer_pad = padded_2(grad_outer, (("space", 1),), 1).reshape(width_b, depth_b + 2, half, half)
    pooled_pad = padded_2(pooled, (("space", 1),), 1).reshape(width_a, depth_b + 2, half, half)
    back_b = back_cells(outer_pad, weight_b)
    sums_b = kernel_terms(pooled_pad, grad_outer.reshape(width_b, depth_b, half, half))
    upward = jnp.repeat(jnp.repeat(jnp.repeat(back_b, 2, 1), 2, 2), 2, 3) * 0.125
    upward = upward.reshape(width_a, depth_a * side * side)
    grad_hidden = (upward * slopes(hidden_f.reshape(width_a, depth_a * side * side))).astype(
        jnp.bfloat16
    )
    grad_hidden = grad_hidden.reshape(width_a, depth_a, side * side)
    back_a = back_flat(grad_hidden, weight_a)
    source_pad = padded_2(source, (("space", 1),), 1)
    sums_a = kernel_terms_flat(source_pad, grad_hidden)
    input_grad = back_a.astype(jnp.bfloat16).reshape(1, chan_in, depth_a, side * side)
    samples = lax.axis_size("dp")
    planes_a = depth_a * lax.axis_size("space")
    scale_a = 1.0 / math.sqrt(samples * planes_a * side * side)
    scale_b = 1.0 / math.sqrt(samples * (planes_a // 2) * half * half)
    total_a, total_b = all_reduce(sums_a, sums_b, scale_a, scale_b)
    return (input_grad, total_a, total_b)


def solution(mesh):
    in_specs = (
        P("dp", None, "space", None),
        P("dp", None, "space", None),
        P("dp", None, "space", None),
        P("dp", None, "space", None),
        P(),
        P(),
    )
    out_specs = (P("dp", None, "space", None), P(), P())
    return jax.shard_map(
        per_device, mesh=mesh, in_specs=in_specs, out_specs=out_specs, check_vma=False
    )
```

```python
import math

import jax
import jax.numpy as jnp
from jax import lax
from jax.sharding import PartitionSpec as P
from jax.experimental import pallas as pl
from jax.experimental.pallas import tpu as pltpu

negative_slope = 0.3


def padded_2(cells, sides, width):
    for axis, dim in sides:
        count = lax.axis_size(axis)
        ends = count - 1
        head = lax.slice_in_dim(cells, 0, width, axis=dim)
        tail = lax.slice_in_dim(cells, cells.shape[dim] - width, cells.shape[dim], axis=dim)
        cells = jnp.concatenate(
            [
                lax.ppermute(tail, axis, [(i, (i + 1) % count) for i in range(ends)]),
                cells,
                lax.ppermute(head, axis, [((i + 1) % count, i) for i in range(ends)]),
            ],
            axis=dim,
        )
    return cells


def slopes(values):
    return jnp.where(values > 0, jnp.ones_like(values), negative_slope * jnp.ones_like(values))


def window(padded, tap_z, tap_y, tap_x, depth, side):
    planes = padded[:, tap_z : tap_z + depth, :]
    margin = side + 1
    wider = jnp.pad(planes, ((0, 0), (0, 0), (margin, margin)))
    offset = (tap_y - 1) * side + (tap_x - 1)
    piece = wider[:, :, margin + offset : margin + offset + side * side]
    column = jnp.arange(side * side, dtype=jnp.int32) % side + (tap_x - 1)
    inside = (column >= 0) & (column < side)
    piece = jnp.where(inside, piece, jnp.zeros_like(piece))
    return piece.reshape(padded.shape[0], depth * side * side)


def outer_product(left, right):
    return lax.dot_general(
        left, right, (((1,), (1,)), ((), ())), preferred_element_type=jnp.float32
    )


def _all_reduce_kernel(x_ref, o_a, o_b, full, recv_a, acc_a, recv_1, acc_1, recv_2, acc_2, recv_3, sends, recvs):
    rows = x_ref.shape[0]
    half = rows // 2
    part = half // 3
    quarter, piece = part // 4, part // 16
    mesh_id = pl.DeviceIdType.MESH
    dp = lax.axis_index("dp")
    sp = lax.axis_index("space")
    core = dp % 2
    spot = {"x": dp // 2, "y": sp // 4, "z": sp % 4}
    partner = (spot["x"] * 2 + (1 - core), sp)

    def peer(axis, k):
        moved = dict(spot)
        moved[axis] = (spot[axis] + k) % 4
        return (moved["x"] * 2 + core, moved["y"] * 4 + moved["z"])

    orders = (("x", "y", "z"), ("y", "z", "x"), ("z", "x", "y"))
    peers = [partner] + [peer(axis, k) for axis in "xyz" for k in (1, 2, 3)]
    barrier = pltpu.get_barrier_semaphore()
    for other in peers:
        pl.semaphore_signal(barrier, inc=1, device_id=other, device_id_type=mesh_id)
    pl.semaphore_wait(barrier, len(peers))

    def rows_at(start, size):
        return pl.ds(pl.multiple_of(start, 16), size)

    used = [0]

    def exchange(triples):
        copies = []
        for src, dst, other in triples:
            copy = pltpu.make_async_remote_copy(
                src_ref=src,
                dst_ref=dst,
                send_sem=sends.at[used[0]],
                recv_sem=recvs.at[used[0]],
                device_id=other,
                device_id_type=mesh_id,
            )
            used[0] += 1
            copy.start()
            copies.append(copy)
        for copy in copies:
            copy.wait()

    exchange([(x_ref.at[rows_at((1 - core) * half, half)], recv_a, partner)])
    acc_a[...] = x_ref[rows_at(core * half, half), :] + recv_a[...]
    triples = []
    for p, order in enumerate(orders):
        for k in (1, 2, 3):
            block = p * part + ((spot[order[0]] + k) % 4) * quarter
            triples.append((acc_a.at[rows_at(block, quarter)], recv_1.at[p, k - 1], peer(order[0], k)))
    exchange(triples)
    for p, order in enumerate(orders):
        mine = p * part + spot[order[0]] * quarter
        acc_1[p] = acc_a[rows_at(mine, quarter), :] + recv_1[p, 0] + recv_1[p, 1] + recv_1[p, 2]
    triples = []
    for p, order in enumerate(orders):
        for k in (1, 2, 3):
            block = ((spot[order[1]] + k) % 4) * piece
            triples.append((acc_1.at[p, rows_at(block, piece)], recv_2.at[p, k - 1], peer(order[1], k)))
    exchange(triples)
    for p, order in enumerate(orders):
        mine = spot[order[1]] * piece
        recv_3[p, 0] = acc_1[p, rows_at(mine, piece), :] + recv_2[p, 0] + recv_2[p, 1] + recv_2[p, 2]
    exchange([(recv_3.at[p, 0], recv_3.at[p, k], peer(order[2], k)) for p, order in enumerate(orders) for k in (1, 2, 3)])
    spans = []
    for p, order in enumerate(orders):
        last = spot[order[2]]
        total = recv_3[p, last % 4]
        for j in (1, 2, 3):
            total = total + recv_3[p, (last - j + 4) % 4]
        outer = core * half + p * part + spot[order[0]] * quarter
        own = outer + spot[order[1]] * piece
        full[rows_at(own, piece), :] = total.astype(full.dtype)
        spans.append((outer, own, order))
    exchange([(full.at[rows_at(own, piece)], full.at[rows_at(own, piece)], peer(order[1], k)) for outer, own, order in spans for k in (1, 2, 3)])
    exchange([(full.at[rows_at(outer, quarter)], full.at[rows_at(outer, quarter)], peer(order[0], k)) for outer, own, order in spans for k in (1, 2, 3)])
    block = full.at[rows_at(core * half, half)]
    exchange([(block, block, partner)])
    rows_a, rows_b = o_a.shape[0], o_b.shape[0]
    o_a[...] = full[0:rows_a, :].astype(jnp.float32)
    o_b[:, 0:128] = full[rows_a : rows_a + rows_b, :].astype(jnp.float32)
    o_b[:, 128:256] = full[rows_a + rows_b : rows_a + 2 * rows_b, :].astype(jnp.float32)


def all_reduce(sums_a, sums_b, scale_a, scale_b):
    rows_a = sums_a.shape[0] * sums_a.shape[1]
    rows_b = sums_b.shape[0] * sums_b.shape[1]
    wide = sums_b.reshape(rows_b, 256) * scale_b
    flat = jnp.concatenate([sums_a.reshape(rows_a, 128) * scale_a, wide[:, :128], wide[:, 128:]])
    count = flat.shape[0]
    unit = 6 * 16 * 16
    rows = -(-count // unit) * unit
    flat = jnp.pad(flat, ((0, rows - count), (0, 0)))
    half = rows // 2
    part = half // 3
    quarter, piece = part // 4, part // 16
    f32 = jnp.float32
    out_a, out_b = pl.pallas_call(
        _all_reduce_kernel,
        out_shape=(jax.ShapeDtypeStruct((rows_a, 128), f32), jax.ShapeDtypeStruct((rows_b, 256), f32)),
        in_specs=[pl.BlockSpec(memory_space=pltpu.VMEM)],
        out_specs=(pl.BlockSpec(memory_space=pltpu.VMEM), pl.BlockSpec(memory_space=pltpu.VMEM)),
        scratch_shapes=[
            pltpu.VMEM((rows, 128), jnp.bfloat16),
            pltpu.VMEM((half, 128), f32),
            pltpu.VMEM((half, 128), f32),
            pltpu.VMEM((3, 3, quarter, 128), f32),
            pltpu.VMEM((3, quarter, 128), f32),
            pltpu.VMEM((3, 3, piece, 128), f32),
            pltpu.VMEM((3, piece, 128), f32),
            pltpu.VMEM((3, 4, piece, 128), f32),
            pltpu.SemaphoreType.DMA((47,)),
            pltpu.SemaphoreType.DMA((47,)),
        ],
        compiler_params=pltpu.CompilerParams(collective_id=0, has_side_effects=True),
    )(flat)
    return out_a.reshape(sums_a.shape), out_b.reshape(sums_b.shape)


def conv_cells(field, kernel):
    shaped = kernel.reshape(3, 3, 3, kernel.shape[1], kernel.shape[2])
    result = lax.conv_general_dilated(
        field[None],
        shaped,
        (1, 1, 1),
        ((0, 0), (1, 1), (1, 1)),
        dimension_numbers=("NCDHW", "DHWIO", "NCDHW"),
        preferred_element_type=jnp.float32,
    )
    return result[0]


def back_cells(padded, kernel):
    shaped = kernel.reshape(3, 3, 3, kernel.shape[1], kernel.shape[2])
    result = lax.conv_general_dilated(
        padded[None, :, ::-1, ::-1, ::-1],
        shaped,
        (1, 1, 1),
        ((0, 0), (1, 1), (1, 1)),
        dimension_numbers=("NCDHW", "DHWOI", "NCDHW"),
        preferred_element_type=jnp.float32,
    )
    return result[0, :, ::-1, ::-1, ::-1]


def kernel_terms(padded, upstream):
    taps, chan_in, chan_out = 27, padded.shape[0], upstream.shape[0]
    start = jnp.zeros((taps, chan_in, chan_out), jnp.float32)
    field = padded.astype(jnp.float32)
    unused, pull = jax.vjp(lambda w: conv_cells(field, w), start)
    return pull(upstream.astype(jnp.float32))[0]


def _terms_a_body(src_ref, up_ref, terms_ref):
    cells = up_ref.shape[1]
    width = src_ref.shape[1]
    plane = width // 4
    side = 32
    spot = lax.broadcasted_iota(jnp.int32, (1, cells), 1)
    column = spot % side
    row = (spot // side) % side
    upstream = up_ref[...]
    field = src_ref[...].astype(jnp.float32)
    for b in range(3):
        for c in range(3):
            shift = (b - 1) * side + (c - 1)
            moved = pltpu.roll(field, (width - shift) % width, 1)
            inside = (column + c - 1 >= 0) & (column + c - 1 < side) & (row + b - 1 >= 0) & (row + b - 1 < side)
            for a in range(3):
                window = moved[:, a * plane : a * plane + cells]
                window = jnp.where(inside, window, 0.0).astype(jnp.bfloat16)
                terms_ref[9 * a + 3 * b + c] = lax.dot_general(
                    window, upstream, (((1,), (1,)), ((), ())), preferred_element_type=jnp.float32
                )


def kernel_terms_flat(source_pad, grad_hidden):
    chan_in, chan_out = source_pad.shape[0], grad_hidden.shape[0]
    return pl.pallas_call(
        _terms_a_body,
        out_shape=jax.ShapeDtypeStruct((27, chan_in, chan_out), jnp.float32),
        in_specs=[pl.BlockSpec(memory_space=pltpu.VMEM)] * 2,
        out_specs=pl.BlockSpec(memory_space=pltpu.VMEM),
    )(source_pad.reshape(chan_in, -1), grad_hidden.reshape(chan_out, -1))


def _back_a_body(pad_ref, w_ref, back_ref):
    cells = back_ref.shape[1] * back_ref.shape[2]
    plane = pad_ref.shape[1] // 4
    side = 32
    spot = lax.broadcasted_iota(jnp.int32, (1, cells), 1)
    column = spot % side
    row = (spot // side) % side
    back = jnp.zeros((back_ref.shape[0], cells), jnp.float32)
    for b in range(3):
        for c in range(3):
            shift = (b - 1) * side + (c - 1)
            total = jnp.zeros_like(back)
            for a in range(3):
                total = total + jnp.dot(
                    w_ref[9 * a + 3 * b + c],
                    pad_ref[:, (2 - a) * plane : (2 - a) * plane + cells],
                    preferred_element_type=jnp.float32,
                )
            back_in = (column - c + 1 >= 0) & (column - c + 1 < side) & (row - b + 1 >= 0) & (row - b + 1 < side)
            back = back + jnp.where(back_in, pltpu.roll(total, shift % cells, 1), 0.0)
    plane = back_ref.shape[2]
    for z in range(back_ref.shape[1]):
        back_ref[:, z, :] = back[:, z * plane : (z + 1) * plane].astype(back_ref.dtype)


def back_flat(hidden_pad, weight_a, cells):
    chan_in, chan_out = weight_a.shape[1], hidden_pad.shape[0]
    return pl.pallas_call(
        _back_a_body,
        out_shape=jax.ShapeDtypeStruct((chan_in, cells // 1024, 1024), jnp.bfloat16),
        in_specs=[pl.BlockSpec(memory_space=pltpu.VMEM)] * 2,
        out_specs=pl.BlockSpec(memory_space=pltpu.VMEM),
    )(hidden_pad.reshape(chan_out, -1), weight_a)


def per_device(layer_input, hidden_pre, output_pre, output_grad, weight_a, weight_b):
    side = math.isqrt(layer_input.shape[3])
    half = side // 2
    depth_a = layer_input.shape[2]
    depth_b = depth_a // 2
    source = layer_input[0]
    hidden = hidden_pre[0]
    outer = output_pre[0]
    upstream = output_grad[0]
    chan_in = source.shape[0]
    width_a = hidden.shape[0]
    width_b = outer.shape[0]
    grad_outer = (upstream.astype(jnp.float32) * slopes(outer.astype(jnp.float32))).astype(
        jnp.bfloat16
    )
    hidden_f = hidden.astype(jnp.float32)
    active = jnp.where(hidden_f > 0, hidden_f, negative_slope * hidden_f)
    pooled = (
        active.reshape(width_a, depth_b, 2, half, 2, half, 2)
        .mean(axis=(2, 4, 6))
        .astype(jnp.bfloat16)
    )
    pooled = pooled.reshape(width_a, depth_b, half * half)
    outer_pad = padded_2(grad_outer, (("space", 1),), 1).reshape(width_b, depth_b + 2, half, half)
    pooled_pad = padded_2(pooled, (("space", 1),), 1).reshape(width_a, depth_b + 2, half, half)
    back_b = back_cells(outer_pad, weight_b)
    sums_b = kernel_terms(pooled_pad, grad_outer.reshape(width_b, depth_b, half, half))
    upward = jnp.repeat(jnp.repeat(jnp.repeat(back_b, 2, 1), 2, 2), 2, 3) * 0.125
    upward = upward.reshape(width_a, depth_a * side * side)
    grad_hidden = (upward * slopes(hidden_f.reshape(width_a, depth_a * side * side))).astype(
        jnp.bfloat16
    )
    grad_hidden = grad_hidden.reshape(width_a, depth_a, side * side)
    hidden_pad = padded_2(grad_hidden, (("space", 1),), 1)
    back_a = back_flat(hidden_pad, weight_a, depth_a * side * side)
    source_pad = padded_2(source, (("space", 1),), 1)
    sums_a = kernel_terms_flat(source_pad, grad_hidden)
    input_grad = back_a.astype(jnp.bfloat16).reshape(1, chan_in, depth_a, side * side)
    samples = lax.axis_size("dp")
    planes_a = depth_a * lax.axis_size("space")
    scale_a = 1.0 / math.sqrt(samples * planes_a * side * side)
    scale_b = 1.0 / math.sqrt(samples * (planes_a // 2) * half * half)
    total_a, total_b = all_reduce(sums_a, sums_b, scale_a, scale_b)
    return (input_grad, total_a, total_b)


def solution(mesh):
    in_specs = (
        P("dp", None, "space", None),
        P("dp", None, "space", None),
        P("dp", None, "space", None),
        P("dp", None, "space", None),
        P(),
        P(),
    )
    out_specs = (P("dp", None, "space", None), P(), P())
    return jax.shard_map(
        per_device, mesh=mesh, in_specs=in_specs, out_specs=out_specs, check_vma=False
    )
```

```python
import math

import jax
import jax.numpy as jnp
from jax import lax
from jax.sharding import PartitionSpec as P
from jax.experimental import pallas as pl
from jax.experimental.pallas import tpu as pltpu

negative_slope = 0.3


def padded_2(cells, sides, width):
    for axis, dim in sides:
        count = lax.axis_size(axis)
        ends = count - 1
        head = lax.slice_in_dim(cells, 0, width, axis=dim)
        tail = lax.slice_in_dim(cells, cells.shape[dim] - width, cells.shape[dim], axis=dim)
        cells = jnp.concatenate(
            [
                lax.ppermute(tail, axis, [(i, (i + 1) % count) for i in range(ends)]),
                cells,
                lax.ppermute(head, axis, [((i + 1) % count, i) for i in range(ends)]),
            ],
            axis=dim,
        )
    return cells


def slopes(values):
    return jnp.where(values > 0, jnp.ones_like(values), negative_slope * jnp.ones_like(values))


def window(padded, tap_z, tap_y, tap_x, depth, side):
    planes = padded[:, tap_z : tap_z + depth, :]
    margin = side + 1
    wider = jnp.pad(planes, ((0, 0), (0, 0), (margin, margin)))
    offset = (tap_y - 1) * side + (tap_x - 1)
    piece = wider[:, :, margin + offset : margin + offset + side * side]
    column = jnp.arange(side * side, dtype=jnp.int32) % side + (tap_x - 1)
    inside = (column >= 0) & (column < side)
    piece = jnp.where(inside, piece, jnp.zeros_like(piece))
    return piece.reshape(padded.shape[0], depth * side * side)


def outer_product(left, right):
    return lax.dot_general(
        left, right, (((1,), (1,)), ((), ())), preferred_element_type=jnp.float32
    )


def _all_reduce_kernel(x_ref, o_a, o_b, full, recv_a, acc_a, recv_1, acc_1, recv_2, acc_2, recv_3, sends, recvs):
    rows = x_ref.shape[0]
    half = rows // 2
    part = half // 3
    quarter, piece = part // 4, part // 16
    mesh_id = pl.DeviceIdType.MESH
    dp = lax.axis_index("dp")
    sp = lax.axis_index("space")
    core = dp % 2
    spot = {"x": dp // 2, "y": sp // 4, "z": sp % 4}
    partner = (spot["x"] * 2 + (1 - core), sp)

    def peer(axis, k):
        moved = dict(spot)
        moved[axis] = (spot[axis] + k) % 4
        return (moved["x"] * 2 + core, moved["y"] * 4 + moved["z"])

    orders = (("x", "y", "z"), ("y", "z", "x"), ("z", "x", "y"))
    peers = [partner] + [peer(axis, k) for axis in "xyz" for k in (1, 2, 3)]
    barrier = pltpu.get_barrier_semaphore()
    for other in peers:
        pl.semaphore_signal(barrier, inc=1, device_id=other, device_id_type=mesh_id)
    pl.semaphore_wait(barrier, len(peers))

    def rows_at(start, size):
        return pl.ds(pl.multiple_of(start, 16), size)

    used = [0]

    def exchange(triples):
        copies = []
        for src, dst, other in triples:
            copy = pltpu.make_async_remote_copy(
                src_ref=src,
                dst_ref=dst,
                send_sem=sends.at[used[0]],
                recv_sem=recvs.at[used[0]],
                device_id=other,
                device_id_type=mesh_id,
            )
            used[0] += 1
            copy.start()
            copies.append(copy)
        for copy in copies:
            copy.wait()

    exchange([(x_ref.at[rows_at((1 - core) * half, half)], recv_a, partner)])
    acc_a[...] = x_ref[rows_at(core * half, half), :] + recv_a[...]
    triples = []
    for p, order in enumerate(orders):
        for k in (1, 2, 3):
            block = p * part + ((spot[order[0]] + k) % 4) * quarter
            triples.append((acc_a.at[rows_at(block, quarter)], recv_1.at[p, k - 1], peer(order[0], k)))
    exchange(triples)
    for p, order in enumerate(orders):
        mine = p * part + spot[order[0]] * quarter
        acc_1[p] = acc_a[rows_at(mine, quarter), :] + recv_1[p, 0] + recv_1[p, 1] + recv_1[p, 2]
    triples = []
    for p, order in enumerate(orders):
        for k in (1, 2, 3):
            block = ((spot[order[1]] + k) % 4) * piece
            triples.append((acc_1.at[p, rows_at(block, piece)], recv_2.at[p, k - 1], peer(order[1], k)))
    exchange(triples)
    for p, order in enumerate(orders):
        mine = spot[order[1]] * piece
        recv_3[p, 0] = acc_1[p, rows_at(mine, piece), :] + recv_2[p, 0] + recv_2[p, 1] + recv_2[p, 2]
    exchange([(recv_3.at[p, 0], recv_3.at[p, k], peer(order[2], k)) for p, order in enumerate(orders) for k in (1, 2, 3)])
    spans = []
    for p, order in enumerate(orders):
        last = spot[order[2]]
        total = recv_3[p, last % 4]
        for j in (1, 2, 3):
            total = total + recv_3[p, (last - j + 4) % 4]
        outer = core * half + p * part + spot[order[0]] * quarter
        own = outer + spot[order[1]] * piece
        full[rows_at(own, piece), :] = total.astype(full.dtype)
        spans.append((outer, own, order))
    exchange([(full.at[rows_at(own, piece)], full.at[rows_at(own, piece)], peer(order[1], k)) for outer, own, order in spans for k in (1, 2, 3)])
    exchange([(full.at[rows_at(outer, quarter)], full.at[rows_at(outer, quarter)], peer(order[0], k)) for outer, own, order in spans for k in (1, 2, 3)])
    block = full.at[rows_at(core * half, half)]
    exchange([(block, block, partner)])
    rows_a, rows_b = o_a.shape[0], o_b.shape[0]
    o_a[...] = full[0:rows_a, :].astype(jnp.float32)
    o_b[:, 0:128] = full[rows_a : rows_a + rows_b, :].astype(jnp.float32)
    o_b[:, 128:256] = full[rows_a + rows_b : rows_a + 2 * rows_b, :].astype(jnp.float32)


def all_reduce(sums_a, sums_b, scale_a, scale_b):
    rows_a = sums_a.shape[0] * sums_a.shape[1]
    rows_b = sums_b.shape[0] * sums_b.shape[1]
    wide = sums_b.reshape(rows_b, 256) * scale_b
    flat = jnp.concatenate([sums_a.reshape(rows_a, 128) * scale_a, wide[:, :128], wide[:, 128:]])
    count = flat.shape[0]
    unit = 6 * 16 * 16
    rows = -(-count // unit) * unit
    flat = jnp.pad(flat, ((0, rows - count), (0, 0)))
    half = rows // 2
    part = half // 3
    quarter, piece = part // 4, part // 16
    f32 = jnp.float32
    out_a, out_b = pl.pallas_call(
        _all_reduce_kernel,
        out_shape=(jax.ShapeDtypeStruct((rows_a, 128), f32), jax.ShapeDtypeStruct((rows_b, 256), f32)),
        in_specs=[pl.BlockSpec(memory_space=pltpu.VMEM)],
        out_specs=(pl.BlockSpec(memory_space=pltpu.VMEM), pl.BlockSpec(memory_space=pltpu.VMEM)),
        scratch_shapes=[
            pltpu.VMEM((rows, 128), jnp.bfloat16),
            pltpu.VMEM((half, 128), f32),
            pltpu.VMEM((half, 128), f32),
            pltpu.VMEM((3, 3, quarter, 128), f32),
            pltpu.VMEM((3, quarter, 128), f32),
            pltpu.VMEM((3, 3, piece, 128), f32),
            pltpu.VMEM((3, piece, 128), f32),
            pltpu.VMEM((3, 4, piece, 128), f32),
            pltpu.SemaphoreType.DMA((47,)),
            pltpu.SemaphoreType.DMA((47,)),
        ],
        compiler_params=pltpu.CompilerParams(collective_id=0, has_side_effects=True),
    )(flat)
    return out_a.reshape(sums_a.shape), out_b.reshape(sums_b.shape)


def conv_cells(field, kernel):
    shaped = kernel.reshape(3, 3, 3, kernel.shape[1], kernel.shape[2])
    result = lax.conv_general_dilated(
        field[None],
        shaped,
        (1, 1, 1),
        ((0, 0), (1, 1), (1, 1)),
        dimension_numbers=("NCDHW", "DHWIO", "NCDHW"),
        preferred_element_type=jnp.float32,
    )
    return result[0]


def back_cells(padded, kernel):
    flipped = kernel[::-1].transpose(0, 2, 1)
    return conv_cells(padded, flipped)


def kernel_terms(padded, upstream):
    taps, chan_in, chan_out = 27, padded.shape[0], upstream.shape[0]
    start = jnp.zeros((taps, chan_in, chan_out), jnp.float32)
    field = padded.astype(jnp.float32)
    unused, pull = jax.vjp(lambda w: conv_cells(field, w), start)
    return pull(upstream.astype(jnp.float32))[0]


def _terms_a_body(src_ref, up_ref, terms_ref):
    cells = up_ref.shape[1]
    width = src_ref.shape[1]
    plane = width // 4
    side = 32
    spot = lax.broadcasted_iota(jnp.int32, (1, cells), 1)
    column = spot % side
    row = (spot // side) % side
    upstream = up_ref[...]
    field = src_ref[...]
    for b in range(3):
        for c in range(3):
            shift = (b - 1) * side + (c - 1)
            moved = pltpu.roll(field, (width - shift) % width, 1)
            inside = (column + c - 1 >= 0) & (column + c - 1 < side) & (row + b - 1 >= 0) & (row + b - 1 < side)
            for a in range(3):
                window = moved[:, a * plane : a * plane + cells]
                window = jnp.where(inside, window, jnp.zeros_like(window))
                terms_ref[9 * a + 3 * b + c] = lax.dot_general(
                    window, upstream, (((1,), (1,)), ((), ())), preferred_element_type=jnp.float32
                )


def kernel_terms_flat(source_pad, grad_hidden):
    chan_in, chan_out = source_pad.shape[0], grad_hidden.shape[0]
    return pl.pallas_call(
        _terms_a_body,
        out_shape=jax.ShapeDtypeStruct((27, chan_in, chan_out), jnp.float32),
        in_specs=[pl.BlockSpec(memory_space=pltpu.VMEM)] * 2,
        out_specs=pl.BlockSpec(memory_space=pltpu.VMEM),
    )(source_pad.reshape(chan_in, -1), grad_hidden.reshape(chan_out, -1))


def _back_a_body(pad_ref, w_ref, back_ref):
    cells = back_ref.shape[1] * back_ref.shape[2]
    plane = pad_ref.shape[1] // 4
    side = 32
    spot = lax.broadcasted_iota(jnp.int32, (1, cells), 1)
    column = spot % side
    row = (spot // side) % side
    back = jnp.zeros((back_ref.shape[0], cells), jnp.float32)
    for b in range(3):
        for c in range(3):
            shift = (b - 1) * side + (c - 1)
            total = jnp.zeros_like(back)
            for a in range(3):
                total = total + jnp.dot(
                    w_ref[9 * a + 3 * b + c],
                    pad_ref[:, (2 - a) * plane : (2 - a) * plane + cells],
                    preferred_element_type=jnp.float32,
                )
            back_in = (column - c + 1 >= 0) & (column - c + 1 < side) & (row - b + 1 >= 0) & (row - b + 1 < side)
            back = back + jnp.where(back_in, pltpu.roll(total, shift % cells, 1), 0.0)
    plane = back_ref.shape[2]
    for z in range(back_ref.shape[1]):
        back_ref[:, z, :] = back[:, z * plane : (z + 1) * plane].astype(back_ref.dtype)


def back_flat(hidden_pad, weight_a, cells):
    chan_in, chan_out = weight_a.shape[1], hidden_pad.shape[0]
    return pl.pallas_call(
        _back_a_body,
        out_shape=jax.ShapeDtypeStruct((chan_in, cells // 1024, 1024), jnp.bfloat16),
        in_specs=[pl.BlockSpec(memory_space=pltpu.VMEM)] * 2,
        out_specs=pl.BlockSpec(memory_space=pltpu.VMEM),
    )(hidden_pad.reshape(chan_out, -1), weight_a)


def per_device(layer_input, hidden_pre, output_pre, output_grad, weight_a, weight_b):
    side = math.isqrt(layer_input.shape[3])
    half = side // 2
    depth_a = layer_input.shape[2]
    depth_b = depth_a // 2
    source = layer_input[0]
    hidden = hidden_pre[0]
    outer = output_pre[0]
    upstream = output_grad[0]
    chan_in = source.shape[0]
    width_a = hidden.shape[0]
    width_b = outer.shape[0]
    grad_outer = (upstream.astype(jnp.float32) * slopes(outer.astype(jnp.float32))).astype(
        jnp.bfloat16
    )
    hidden_f = hidden.astype(jnp.float32)
    active = jnp.where(hidden_f > 0, hidden_f, negative_slope * hidden_f)
    pooled = (
        active.reshape(width_a, depth_b, 2, half, 2, half, 2)
        .mean(axis=(2, 4, 6))
        .astype(jnp.bfloat16)
    )
    pooled = pooled.reshape(width_a, depth_b, half * half)
    outer_pad = padded_2(grad_outer, (("space", 1),), 1).reshape(width_b, depth_b + 2, half, half)
    pooled_pad = padded_2(pooled, (("space", 1),), 1).reshape(width_a, depth_b + 2, half, half)
    back_b = back_cells(outer_pad, weight_b)
    sums_b = kernel_terms(pooled_pad, grad_outer.reshape(width_b, depth_b, half, half))
    upward = jnp.repeat(jnp.repeat(jnp.repeat(back_b, 2, 1), 2, 2), 2, 3) * 0.125
    upward = upward.reshape(width_a, depth_a * side * side)
    grad_hidden = (upward * slopes(hidden_f.reshape(width_a, depth_a * side * side))).astype(
        jnp.bfloat16
    )
    grad_hidden = grad_hidden.reshape(width_a, depth_a, side * side)
    hidden_pad = padded_2(grad_hidden, (("space", 1),), 1)
    back_a = back_flat(hidden_pad, weight_a, depth_a * side * side)
    source_pad = padded_2(source, (("space", 1),), 1)
    sums_a = kernel_terms_flat(source_pad, grad_hidden)
    input_grad = back_a.astype(jnp.bfloat16).reshape(1, chan_in, depth_a, side * side)
    samples = lax.axis_size("dp")
    planes_a = depth_a * lax.axis_size("space")
    scale_a = 1.0 / math.sqrt(samples * planes_a * side * side)
    scale_b = 1.0 / math.sqrt(samples * (planes_a // 2) * half * half)
    total_a, total_b = all_reduce(sums_a, sums_b, scale_a, scale_b)
    return (input_grad, total_a, total_b)


def solution(mesh):
    in_specs = (
        P("dp", None, "space", None),
        P("dp", None, "space", None),
        P("dp", None, "space", None),
        P("dp", None, "space", None),
        P(),
        P(),
    )
    out_specs = (P("dp", None, "space", None), P(), P())
    return jax.shard_map(
        per_device, mesh=mesh, in_specs=in_specs, out_specs=out_specs, check_vma=False
    )
```
